512 devices in a mesh: gx: 32 (over x, y), gy: 16 (over z, core).
Axes of the slice: x: 4, y: 8, z: 8, core: 2. Of those that a mesh axis runs over, the one named last changes fastest.
Arguments:
- modes: float32 [4, 128, 8192], P(None, 'gx', 'gy'), may hold values from -6 to 6
- directions: float32 [4, 128, 8192], P(None, 'gx', 'gy'), may hold values from -6 to 6
- locked: float32 [60, 128, 8192], P(None, 'gx', 'gy'), may hold values from -9 to 9
- perm_class: int32 [128, 8192], P('gx', 'gy'), may hold values from 0 to 15
- perm_table: float32 [16], replicated, may hold values from 0.01 to 1
- locked_count: int32 [1], replicated, may hold values from 30 to 60
Outputs:
- new_modes: float32 [4, 128, 8192], P(None, 'gx', 'gy')
- new_directions: float32 [4, 128, 8192], P(None, 'gx', 'gy')
- ritz_values: float32 [4], replicated
- locked_correlation: float32 [60, 4], replicated
The draws below stay inside these ranges and needn't reach their ends.
All inputs are finite; a program needn't handle non-finite values.
Results may differ from the reference program's by a relative error of at most 0.0003.
Values sent between devices are 32-bit elements; how exact they have to be, the bound alone decides.
No kernel may reach another device: no remote copies, remote signals or barrier semaphores. Data moves between devices by JAX's collectives and lax.ppermute only.
A program may use at most 64 MiB of HBM per device.

```python
import math
import jax
import jax.numpy as jnp
from jax import lax

NZ = 64
ACTIVE = 4
LOCKED = 60
NCLASS = 16
SWEEPS = 3
RITZ = 3
NX = 128
NY = 128


def shared_base(key):
    extent = (ACTIVE, NX, NY * NZ)
    return jnp.clip(jax.random.normal(jax.random.fold_in(key, 11), extent, jnp.float32), -6.0, 6.0)


def draw_modes(key, part):
    return shared_base(key)


def draw_locked(key, part):
    base_field = shared_base(key)
    extent = (LOCKED, NX, NY * NZ)
    noise = jnp.clip(jax.random.normal(jax.random.fold_in(key, 12), extent, jnp.float32), -6.0, 6.0)
    return noise + 0.5 * jnp.tile(base_field, (LOCKED // ACTIVE, 1, 1))


def set_ends(drawn, rng, smallest, largest):
    shape = drawn.shape
    spot = [jax.random.randint(jax.random.fold_in(rng, axis), (), 0, shape[axis]) for axis in range(len(shape))]
    drawn = drawn.at[tuple(spot)].set(smallest)
    longest = shape.index(max(shape))
    spot[longest] = (spot[longest] + 1) % shape[longest]
    return drawn.at[tuple(spot)].set(largest)


def steps_of(key, shape, shards, smallest, high):
    gain, own = 1.0, jax.random.fold_in(key, 6)
    for axis_at, parts in shards:
        heights = jnp.exp(jax.random.uniform(jax.random.fold_in(own, axis_at), (parts,), jnp.float32, smallest / len(shards), high / len(shards)))
        gain = gain * jnp.repeat(heights, shape[axis_at] // parts).reshape([-1 if axis == axis_at else 1 for axis in range(len(shape))])
    return gain


def scatter_about(own_key, shape, spread, reach, cuts=(), kind=jnp.bfloat16):
    result = jax.random.normal(own_key, shape, jnp.float32) * spread
    if len(cuts) > 0:
        result = steps_of(own_key, shape, cuts, -0.22, 0.18) * result
    return jnp.clip(result, min=-reach, max=reach).astype(kind)


def setup_inputs(seed: int = 0) -> dict:
    streams_of = jax.random.split(jax.random.key(seed), 7)
    return {
        "modes": draw_modes(jax.random.fold_in(streams_of[6], 71), 0),
        "directions": scatter_about(streams_of[1], (ACTIVE, NX, NY * NZ), 1.0, 6.0, ((1, 32), (2, 16)), jnp.float32),
        "locked": draw_locked(jax.random.fold_in(streams_of[6], 71), 0),
        "perm_class": set_ends(jax.random.randint(streams_of[3], (NX, NY * NZ), 0, NCLASS), jax.random.fold_in(streams_of[3], 1), 0, NCLASS - 1).astype(jnp.int32),
        "perm_table": jnp.clip(jnp.exp(jax.random.uniform(streams_of[4], (NCLASS,), jnp.float32, math.log(0.01), math.log(1.0))), 0.01, 1.0),
        "locked_count": jax.random.randint(streams_of[5], (1,), LOCKED // 2, LOCKED + 1).astype(jnp.int32),
    }


OMEGA = 0.6
EPSILON = 1e-06
PRECISE = lax.Precision.HIGHEST

def face_value(lower_k, upper_k):
    return jnp.where(lower_k > 0, jnp.where(upper_k > 0, 2.0 * lower_k * upper_k / (lower_k + upper_k), 2.0 * lower_k), 2.0 * upper_k)

def assemble(x_lower, x_upper, y_lower, y_upper, z_lower, z_upper):
    diagonal = x_lower + x_upper + y_lower + y_upper + z_lower + z_upper
    return jnp.stack([diagonal, x_lower, x_upper, y_lower, y_upper, z_lower, z_upper])

def fine_coef(rimmed):
    interior = rimmed[1:-1, 1:-1]
    z_padded = jnp.pad(interior, ((0, 0), (0, 0), (1, 1)))
    x_lower = face_value(rimmed[:-2, 1:-1], interior)
    x_upper = face_value(interior, rimmed[2:, 1:-1])
    y_lower = face_value(rimmed[1:-1, :-2], interior)
    y_upper = face_value(interior, rimmed[1:-1, 2:])
    z_lower = face_value(z_padded[:, :, :-2], interior)
    z_upper = face_value(interior, z_padded[:, :, 2:])
    return assemble(x_lower, x_upper, y_lower, y_upper, z_lower, z_upper)

def pair_sum(blocks, which_dim):
    extent = blocks.shape
    return blocks.reshape(extent[:which_dim] + (extent[which_dim] // 2, 2) + extent[which_dim + 1:]).sum(which_dim + 1)

def coarsen(coeffs):
    x_lower = pair_sum(pair_sum(coeffs[1][0::2], 1), 2)
    x_upper = pair_sum(pair_sum(coeffs[2][1::2], 1), 2)
    y_lower = pair_sum(pair_sum(coeffs[3][:, 0::2], 0), 2)
    y_upper = pair_sum(pair_sum(coeffs[4][:, 1::2], 0), 2)
    z_lower = pair_sum(pair_sum(coeffs[5][:, :, 0::2], 0), 1)
    z_upper = pair_sum(pair_sum(coeffs[6][:, :, 1::2], 0), 1)
    return assemble(x_lower, x_upper, y_lower, y_upper, z_lower, z_upper)

def stencil(rimmed, coeffs):
    center = rimmed[:, 1:-1, 1:-1]
    z_padded = jnp.pad(center, ((0, 0), (0, 0), (0, 0), (1, 1)))
    beside = coeffs[1] * rimmed[:, :-2, 1:-1] + coeffs[2] * rimmed[:, 2:, 1:-1]
    beside = beside + coeffs[3] * rimmed[:, 1:-1, :-2] + coeffs[4] * rimmed[:, 1:-1, 2:]
    beside = beside + coeffs[5] * z_padded[..., :-2] + coeffs[6] * z_padded[..., 2:]
    return coeffs[0] * center - beside

def restrict(field):
    return pair_sum(pair_sum(pair_sum(field, 1), 2), 3)

def prolong(field):
    return jnp.repeat(jnp.repeat(jnp.repeat(field, 2, 1), 2, 2), 2, 3)

def operate(field, coeffs):
    return stencil(jnp.pad(field, ((0, 0), (1, 1), (1, 1), (0, 0))), coeffs)

def line_solve(source, coeffs, shift):
    lower = jnp.transpose(coeffs[3], (0, 2, 1))
    upper = jnp.transpose(coeffs[4], (0, 2, 1))
    others = jnp.transpose(coeffs[1] + coeffs[2] + coeffs[5] + coeffs[6], (0, 2, 1))
    main = lower + upper + shift * others
    below = jnp.concatenate([jnp.zeros_like(lower[..., :1]), -lower[..., 1:]], -1)
    above = jnp.concatenate([-upper[..., :-1], jnp.zeros_like(upper[..., :1])], -1)
    right = jnp.transpose(source, (1, 3, 2, 0))
    solved = lax.linalg.tridiagonal_solve(below, main, above, right)
    return jnp.transpose(solved, (3, 0, 2, 1))

def vcycle(residual, fine_coeffs, middle_coeffs, coarse_coeffs):
    error_fine = OMEGA * residual / fine_coeffs[0]
    source_mid = restrict(residual - operate(error_fine, fine_coeffs))
    error_mid = OMEGA * source_mid / middle_coeffs[0]
    source_low = restrict(source_mid - operate(error_mid, middle_coeffs))
    line_len = source_low.shape[2]
    error_low = line_solve(source_low, coarse_coeffs, 4.0 / float(line_len * line_len))
    for sweep_no in range(SWEEPS - 1):
        error_low = error_low + OMEGA * (source_low - operate(error_low, coarse_coeffs)) / coarse_coeffs[0]
    error_mid = error_mid + prolong(error_low)
    error_mid = error_mid + OMEGA * (source_mid - operate(error_mid, middle_coeffs)) / middle_coeffs[0]
    error_fine = error_fine + prolong(error_mid)
    return error_fine + OMEGA * (residual - operate(error_fine, fine_coeffs)) / fine_coeffs[0]

def rayleigh_ritz(gram_m, gram_a):
    gram_a = 0.5 * (gram_a + gram_a.T)
    chol_m = jnp.linalg.cholesky(gram_m)
    half_solved = lax.linalg.triangular_solve(chol_m, gram_a, left_side=True, lower=True)
    reduced = lax.linalg.triangular_solve(chol_m, half_solved.T, left_side=True, lower=True)
    reduced = 0.5 * (reduced + reduced.T)
    spectral_top = jnp.trace(reduced)
    basis_q = jnp.eye(gram_m.shape[0], ACTIVE, dtype=jnp.float32)
    for ritz_step in range(RITZ):
        raised = spectral_top * basis_q - jnp.dot(reduced, basis_q, precision=PRECISE)
        factor = jnp.linalg.cholesky(jnp.dot(raised.T, raised, precision=PRECISE))
        basis_q = lax.linalg.triangular_solve(factor, raised.T, left_side=True, lower=True).T
    ritz_values = jnp.sum(basis_q * jnp.dot(reduced, basis_q, precision=PRECISE), axis=0)
    coefficients = lax.linalg.triangular_solve(chol_m, basis_q, left_side=True, lower=True, transpose_a=True)
    return (coefficients, ritz_values)

def reference(modes, directions, locked, perm_class, perm_table, locked_count):
    conduct = perm_table[perm_class].reshape(NX, NY, NZ)
    fine_coeffs = fine_coef(jnp.pad(conduct, ((1, 1), (1, 1), (0, 0))))
    middle_coeffs = coarsen(fine_coeffs)
    coarse_coeffs = coarsen(middle_coeffs)
    field_x = modes.reshape(ACTIVE, NX, NY, NZ)
    field_p = directions.reshape(ACTIVE, NX, NY, NZ)
    locked_grid = locked.reshape(LOCKED, NX, NY, NZ)
    cell_count = float(NX * NY * NZ)
    image_x = operate(field_x, fine_coeffs)
    image_p = operate(field_p, fine_coeffs)
    top_sum = jnp.einsum('kxyz,kxyz->k', field_x, image_x, precision=PRECISE)
    norm_sum = jnp.einsum('kxyz,kxyz->k', field_x, field_x, precision=PRECISE)
    rayleigh_q = top_sum / cell_count / (norm_sum / cell_count + EPSILON)
    residual = image_x - rayleigh_q[:, None, None, None] * field_x
    in_use = (jnp.arange(LOCKED, dtype=jnp.int32) < locked_count[0])[:, None]
    coupling = jnp.where(in_use, jnp.einsum('jxyz,kxyz->jk', locked_grid, residual, precision=PRECISE) / cell_count, 0.0)
    residual = residual - jnp.einsum('jk,jxyz->kxyz', coupling, locked_grid, precision=PRECISE)
    precond = vcycle(residual, fine_coeffs, middle_coeffs, coarse_coeffs)
    correlation = jnp.where(in_use, jnp.einsum('jxyz,kxyz->jk', locked_grid, precond, precision=PRECISE) / cell_count, 0.0)
    projected = precond - jnp.einsum('jk,jxyz->kxyz', correlation, locked_grid, precision=PRECISE)
    image_w = operate(projected, fine_coeffs)
    trial = jnp.concatenate([field_x, projected, field_p], 0)
    images = jnp.concatenate([image_x, image_w, image_p], 0)
    gram_m = jnp.einsum('axyz,bxyz->ab', trial, trial, precision=PRECISE) / cell_count
    gram_a = jnp.einsum('axyz,bxyz->ab', trial, images, precision=PRECISE) / cell_count
    coefficients, ritz_values = rayleigh_ritz(gram_m, gram_a)
    new_modes = jnp.einsum('ak,axyz->kxyz', coefficients, trial, precision=PRECISE)
    new_directions = jnp.einsum('ak,axyz->kxyz', coefficients[ACTIVE:], trial[ACTIVE:], precision=PRECISE)
    return (new_modes.reshape(ACTIVE, NX, NY * NZ), new_directions.reshape(ACTIVE, NX, NY * NZ), ritz_values, correlation)
```

```python
import jax
import jax.numpy as jnp
from jax import lax
from jax.sharding import PartitionSpec as P

NZ = 64
ACTIVE = 4
SWEEPS = 3
RITZ = 3


OMEGA = 0.6
EPSILON = 1e-06
PRECISE = lax.Precision.HIGHEST


def extended(block, sides, width):
    for axis, dim in sides:
        count = lax.axis_size(axis)
        forward = [(i, i + 1) for i in range(count - 1)]
        backward = [(target, source) for source, target in forward]
        low = lax.ppermute(
            lax.slice_in_dim(block, block.shape[dim] - width, None, axis=dim), axis, forward
        )
        high = lax.ppermute(lax.slice_in_dim(block, 0, width, axis=dim), axis, backward)
        block = jnp.concatenate([low, block, high], axis=dim)
    return block


def sum_all(parts):
    flat = jnp.concatenate([part.reshape(-1) for part in parts])
    count = flat.shape[0]
    flat = jnp.pad(flat, (0, -count % 128))
    for axis in ("gy", "gx"):
        spread = jnp.broadcast_to(flat, (lax.axis_size(axis),) + flat.shape)
        flat = jnp.sum(lax.all_to_all(spread, axis, 0, 0), axis=0)
    sums, start = [], 0
    for part in parts:
        sums.append(flat[start : start + part.size].reshape(part.shape))
        start += part.size
    return sums


def gather_y(block):
    count = lax.axis_size("gy")
    got = lax.all_to_all(jnp.broadcast_to(block, (count,) + block.shape), "gy", 0, 0)
    got = jnp.moveaxis(got, 0, 2)
    return got.reshape(got.shape[:2] + (got.shape[2] * got.shape[3],) + got.shape[4:])


def face_value(lower_k, upper_k):
    return jnp.where(
        lower_k > 0,
        jnp.where(upper_k > 0, 2.0 * lower_k * upper_k / (lower_k + upper_k), 2.0 * lower_k),
        2.0 * upper_k,
    )


def assemble(x_lower, x_upper, y_lower, y_upper, z_lower, z_upper):
    diagonal = x_lower + x_upper + y_lower + y_upper + z_lower + z_upper
    return jnp.stack([diagonal, x_lower, x_upper, y_lower, y_upper, z_lower, z_upper])


def fine_coef(rimmed):
    interior = rimmed[1:-1, 1:-1]
    z_padded = jnp.pad(interior, ((0, 0), (0, 0), (1, 1)))
    x_lower = face_value(rimmed[:-2, 1:-1], interior)
    x_upper = face_value(interior, rimmed[2:, 1:-1])
    y_lower = face_value(rimmed[1:-1, :-2], interior)
    y_upper = face_value(interior, rimmed[1:-1, 2:])
    z_lower = face_value(z_padded[:, :, :-2], interior)
    z_upper = face_value(interior, z_padded[:, :, 2:])
    return assemble(x_lower, x_upper, y_lower, y_upper, z_lower, z_upper)


def pair_sum(blocks, which_dim):
    extent = blocks.shape
    return blocks.reshape(
        extent[:which_dim] + (extent[which_dim] // 2, 2) + extent[which_dim + 1 :]
    ).sum(which_dim + 1)


def coarsen(coeffs):
    x_lower = pair_sum(pair_sum(coeffs[1][0::2], 1), 2)
    x_upper = pair_sum(pair_sum(coeffs[2][1::2], 1), 2)
    y_lower = pair_sum(pair_sum(coeffs[3][:, 0::2], 0), 2)
    y_upper = pair_sum(pair_sum(coeffs[4][:, 1::2], 0), 2)
    z_lower = pair_sum(pair_sum(coeffs[5][:, :, 0::2], 0), 1)
    z_upper = pair_sum(pair_sum(coeffs[6][:, :, 1::2], 0), 1)
    return assemble(x_lower, x_upper, y_lower, y_upper, z_lower, z_upper)


def stencil(rimmed, coeffs):
    center = rimmed[:, 1:-1, 1:-1]
    z_padded = jnp.pad(center, ((0, 0), (0, 0), (0, 0), (1, 1)))
    beside = coeffs[1] * rimmed[:, :-2, 1:-1] + coeffs[2] * rimmed[:, 2:, 1:-1]
    beside = beside + coeffs[3] * rimmed[:, 1:-1, :-2] + coeffs[4] * rimmed[:, 1:-1, 2:]
    beside = beside + coeffs[5] * z_padded[..., :-2] + coeffs[6] * z_padded[..., 2:]
    return coeffs[0] * center - beside


def restrict(field):
    return pair_sum(pair_sum(pair_sum(field, 1), 2), 3)


def prolong(field):
    return jnp.repeat(jnp.repeat(jnp.repeat(field, 2, 1), 2, 2), 2, 3)


def line_solve(source, coeffs, shift):
    lower = jnp.transpose(coeffs[3], (0, 2, 1))
    upper = jnp.transpose(coeffs[4], (0, 2, 1))
    others = jnp.transpose(coeffs[1] + coeffs[2] + coeffs[5] + coeffs[6], (0, 2, 1))
    main = lower + upper + shift * others
    below = jnp.concatenate([jnp.zeros_like(lower[..., :1]), -lower[..., 1:]], -1)
    above = jnp.concatenate([-upper[..., :-1], jnp.zeros_like(upper[..., :1])], -1)
    right = jnp.transpose(source, (1, 3, 2, 0))
    solved = lax.linalg.tridiagonal_solve(below, main, above, right)
    return jnp.transpose(solved, (3, 0, 2, 1))


def fine_apply(field, coeffs):
    return stencil(extended(field, (("gx", 1), ("gy", 2)), 1), coeffs)


def middle_apply(field, coeffs):
    return stencil(extended(field, (("gx", 1), ("gy", 2)), 1), coeffs)


def coarse_solve(source, coeffs):
    span_coarse = source.shape[2]
    gathered = gather_y(source)
    line_len = gathered.shape[2]
    update = line_solve(gathered, coeffs, 4.0 / float(line_len * line_len))
    for sweep_no in range(SWEEPS - 1):
        rimmed = extended(update, (("gx", 1),), 1)
        rimmed = jnp.pad(rimmed, ((0, 0), (0, 0), (1, 1), (0, 0)))
        update = update + OMEGA * (gathered - stencil(rimmed, coeffs)) / coeffs[0]
    return lax.dynamic_slice_in_dim(update, lax.axis_index("gy") * span_coarse, span_coarse, 2)


def vcycle(residual, fine_coeffs, middle_coeffs, coarse_coeffs):
    error_fine = OMEGA * residual / fine_coeffs[0]
    source_mid = restrict(residual - fine_apply(error_fine, fine_coeffs))
    error_mid = OMEGA * source_mid / middle_coeffs[0]
    source_low = restrict(source_mid - middle_apply(error_mid, middle_coeffs))
    error_low = coarse_solve(source_low, coarse_coeffs)
    error_mid = error_mid + prolong(error_low)
    error_mid = (
        error_mid + OMEGA * (source_mid - middle_apply(error_mid, middle_coeffs)) / middle_coeffs[0]
    )
    error_fine = error_fine + prolong(error_mid)
    return error_fine + OMEGA * (residual - fine_apply(error_fine, fine_coeffs)) / fine_coeffs[0]


def rayleigh_ritz(gram_m, gram_a):
    gram_a = 0.5 * (gram_a + gram_a.T)
    chol_m = jnp.linalg.cholesky(gram_m)
    half_solved = lax.linalg.triangular_solve(chol_m, gram_a, left_side=True, lower=True)
    reduced = lax.linalg.triangular_solve(chol_m, half_solved.T, left_side=True, lower=True)
    reduced = 0.5 * (reduced + reduced.T)
    spectral_top = jnp.trace(reduced)
    basis_q = jnp.eye(gram_m.shape[0], ACTIVE, dtype=jnp.float32)
    for ritz_step in range(RITZ):
        raised = spectral_top * basis_q - jnp.dot(reduced, basis_q, precision=PRECISE)
        factor = jnp.linalg.cholesky(jnp.dot(raised.T, raised, precision=PRECISE))
        basis_q = lax.linalg.triangular_solve(factor, raised.T, left_side=True, lower=True).T
    ritz_values = jnp.sum(basis_q * jnp.dot(reduced, basis_q, precision=PRECISE), axis=0)
    coefficients = lax.linalg.triangular_solve(
        chol_m, basis_q, left_side=True, lower=True, transpose_a=True
    )
    return (coefficients, ritz_values)


def on_device(modes, directions, locked, perm_class, perm_table, locked_count):
    active, rows_dev, plane_dev = modes.shape
    z_cells = NZ
    span_dev = plane_dev // z_cells
    classes = jnp.arange(perm_table.shape[0], dtype=jnp.int32)
    conduct = jnp.sum(
        jnp.where(perm_class[None] == classes[:, None, None], perm_table[:, None, None], 0.0),
        axis=0,
    )
    conduct = conduct.reshape(rows_dev, span_dev, z_cells)
    rimmed = extended(conduct, (("gx", 0), ("gy", 1)), 1)
    fine_coeffs = fine_coef(rimmed)
    middle_coeffs = coarsen(fine_coeffs)
    coarse_coeffs = coarsen(middle_coeffs)
    coarse_coeffs = gather_y(coarse_coeffs)
    field_x = modes.reshape(active, rows_dev, span_dev, z_cells)
    field_p = directions.reshape(active, rows_dev, span_dev, z_cells)
    locked_grid = locked.reshape(locked.shape[0], rows_dev, span_dev, z_cells)
    cell_count = float(rows_dev * span_dev * z_cells * lax.axis_size("gx") * lax.axis_size("gy"))
    start_fields = jnp.concatenate([field_x, field_p], 0)
    start_images = stencil(extended(start_fields, (("gx", 1), ("gy", 2)), 1), fine_coeffs)
    image_x = start_images[:active]
    image_p = start_images[active:]
    top_part = jnp.einsum("kxyz,kxyz->k", field_x, image_x, precision=PRECISE)
    norm_part = jnp.einsum("kxyz,kxyz->k", field_x, field_x, precision=PRECISE)
    in_use = (jnp.arange(locked.shape[0], dtype=jnp.int32) < locked_count[0])[:, None]
    image_part = jnp.einsum("jxyz,kxyz->jk", locked_grid, image_x, precision=PRECISE)
    overlap_part = jnp.einsum("jxyz,kxyz->jk", locked_grid, field_x, precision=PRECISE)
    top_sum, norm_sum, image_sum, overlap_sum = sum_all(
        [top_part, norm_part, image_part, overlap_part]
    )
    rayleigh_q = top_sum / cell_count / (norm_sum / cell_count + EPSILON)
    residual = image_x - rayleigh_q[:, None, None, None] * field_x
    coupling = (image_sum - rayleigh_q * overlap_sum) / cell_count
    coupling = jnp.where(in_use, coupling, 0.0)
    residual = residual - jnp.einsum("jk,jxyz->kxyz", coupling, locked_grid, precision=PRECISE)
    precond = vcycle(residual, fine_coeffs, middle_coeffs, coarse_coeffs)
    correlation_part = jnp.einsum("jxyz,kxyz->jk", locked_grid, precond, precision=PRECISE)
    correlation = jnp.where(in_use, sum_all([correlation_part])[0] / cell_count, 0.0)
    projected = precond - jnp.einsum("jk,jxyz->kxyz", correlation, locked_grid, precision=PRECISE)
    image_w = fine_apply(projected, fine_coeffs)
    trial = jnp.concatenate([field_x, projected, field_p], 0)
    images = jnp.concatenate([image_x, image_w, image_p], 0)
    mass_part = jnp.einsum("axyz,bxyz->ab", trial, trial, precision=PRECISE)
    stiff_part = jnp.einsum("axyz,bxyz->ab", trial, images, precision=PRECISE)
    mass_sum, stiff_sum = sum_all([mass_part, stiff_part])
    coefficients, ritz_values = rayleigh_ritz(mass_sum / cell_count, stiff_sum / cell_count)
    new_modes = jnp.einsum("ak,axyz->kxyz", coefficients, trial, precision=PRECISE)
    new_directions = jnp.einsum(
        "ak,axyz->kxyz", coefficients[active:], trial[active:], precision=PRECISE
    )
    return (
        new_modes.reshape(active, rows_dev, plane_dev),
        new_directions.reshape(active, rows_dev, plane_dev),
        ritz_values,
        correlation,
    )


def solution(mesh):
    placed = (
        P(None, "gx", "gy"),
        P(None, "gx", "gy"),
        P(None, "gx", "gy"),
        P("gx", "gy"),
        P(),
        P(),
    )
    return jax.shard_map(
        on_device,
        mesh=mesh,
        in_specs=placed,
        out_specs=(P(None, "gx", "gy"), P(None, "gx", "gy"), P(), P()),
        check_vma=False,
    )
```

```python
import functools

import jax
import jax.numpy as jnp
from jax import lax
from jax.experimental import pallas as pl
from jax.experimental.pallas import tpu as pltpu
from jax.sharding import PartitionSpec as P

NZ = 64
ACTIVE = 4
LOCKED = 60
BASIS = 68
ROWS = 72
SWEEPS = 3
RITZ = 3
OMEGA = 0.6
EPSILON = 1e-06
PRECISE = lax.Precision.HIGHEST
WIDE = 1280
OWN = 384
INTERPRET = False


def kernel_call(body, out, *args, scratch=(), scalars=0):
    specs = [pl.BlockSpec(memory_space=pltpu.SMEM)] * scalars
    specs += [pl.BlockSpec(memory_space=pltpu.VMEM)] * (len(args) - scalars)
    shapes = [jax.ShapeDtypeStruct(shape, jnp.float32) for shape in out]
    outs = pl.pallas_call(
        body,
        out_shape=shapes,
        in_specs=specs,
        out_specs=[pl.BlockSpec(memory_space=pltpu.VMEM)] * len(out),
        scratch_shapes=[pltpu.VMEM(shape, jnp.float32) for shape in scratch],
        interpret=INTERPRET,
    )(*args)
    return outs


def roll(value, shift, axis=1):
    return pltpu.roll(value, shift % value.shape[axis], axis)


def lanes_of(value):
    return lax.broadcasted_iota(jnp.int32, value.shape, 1)


def pair_z(value):
    even = lanes_of(value) % 2 == 0
    return value + jnp.where(even, roll(value, -1), roll(value, 1))


def pair_y(value):
    first = lanes_of(value) % 128 < 64
    return value + jnp.where(first, roll(value, -64), roll(value, 64))


def quad_z(value):
    first = lanes_of(value) % 4 < 2
    return value + jnp.where(first, roll(value, -2), roll(value, 2))


def quad_y(value):
    odd = (lanes_of(value) // 128) % 2 == 1
    return value + jnp.where(odd, roll(value, -128), roll(value, 128))


def dot_nt(left, right):
    return lax.dot_general(
        left, right, (((1,), (1,)), ((), ())), precision=PRECISE, preferred_element_type=jnp.float32
    )


def dot_nn(left, right):
    return lax.dot_general(
        left, right, (((1,), (0,)), ((), ())), precision=PRECISE, preferred_element_type=jnp.float32
    )


def relax_weight(diagonal):
    inside = diagonal > 0
    return jnp.where(inside, OMEGA / jnp.where(inside, diagonal, 1.0), 0.0)


def joined(here, there):
    both = (here > 0) & (there > 0)
    return jnp.where(both, 2.0 * here * there / jnp.where(both, here + there, 1.0), 0.0)


def face(coupling, here, there):
    return coupling + jnp.where(there > 0, 0.0, 2.0 * here)


def coef_kernel(
    shift, cond_left, cond_mid, cond_right, basis, left, right, low, high,
    fine_out, middle_out, image_out, now_out, gram_out, coarse_out, cond, vmat, umat,
):
    cond[0:4, :] = cond_left[...]
    cond[4:8, :] = cond_mid[...]
    cond[8:12, :] = cond_right[...]
    cond[12:16, :] = jnp.zeros((4, WIDE), jnp.float32)
    here = cond[...]
    z_at = lanes_of(here) % 64
    x_next, x_prev = roll(here, -1, 0), roll(here, 1, 0)
    y_next, y_prev = roll(here, -64), roll(here, 64)
    z_next = jnp.where(z_at < 63, roll(here, -1), 0.0)
    z_prev = jnp.where(z_at > 0, roll(here, 1), 0.0)
    tx, ty, tz = joined(here, x_next), joined(here, y_next), joined(here, z_next)
    y_faces = face(ty, here, y_next) + face(roll(ty, 64), here, y_prev)
    diagonal = face(tx, here, x_next) + face(roll(tx, 1, 0), here, x_prev) + y_faces
    diagonal = diagonal + face(tz, here, z_next) + face(roll(tz, 1), here, z_prev)
    for at, value in enumerate((diagonal, tx, ty, tz, relax_weight(diagonal))):
        fine_out[at] = value

    def pairs(value):
        return pair_y(pair_z(value))

    def pair_x(value):
        return value + roll(value, -1, 0)

    upper_y = lanes_of(here) % 128 >= 64
    sum_x = pairs(tx)
    odd_y = pair_x(pairs(jnp.where(upper_y, ty, 0.0)))
    odd_z = pair_x(pairs(jnp.where(z_at % 2 == 1, tz, 0.0)))
    even_y = pair_x(pairs(jnp.where(upper_y, 0.0, ty)))
    even_z = pair_x(pairs(jnp.where(z_at % 2 == 1, 0.0, tz)))
    tx1, ty1, tz1 = roll(sum_x, -1, 0), odd_y, odd_z
    diagonal1 = pair_x(pairs(diagonal)) - 2.0 * (sum_x + even_y + even_z)
    y_faces1 = pair_x(pairs(y_faces)) - 2.0 * even_y
    for at, value in enumerate((diagonal1, tx1, ty1, tz1, relax_weight(diagonal1))):
        middle_out[at] = value

    def quads(value):
        return quad_y(quad_z(value))

    def both_rows(value):
        return value + roll(value, -2, 0)

    upper_tile = (lanes_of(here) // 128) % 2 == 0
    sum_x1 = quads(tx1)
    ty2 = both_rows(quads(jnp.where(upper_tile, ty1, 0.0)))
    tz2 = both_rows(quads(jnp.where(z_at % 4 >= 2, tz1, 0.0)))
    inner_y = both_rows(quads(jnp.where(upper_tile, 0.0, ty1)))
    inner_z = both_rows(quads(jnp.where(z_at % 4 >= 2, 0.0, tz1)))
    tx2 = roll(sum_x1, -2, 0)
    diagonal2 = both_rows(quads(diagonal1)) - 2.0 * (sum_x1 + inner_y + inner_z)
    y_faces2 = both_rows(quads(y_faces1)) - 2.0 * inner_y
    line2 = y_faces2 + shift * (diagonal2 - y_faces2)
    coarse_out[...] = jnp.zeros((8, 128), jnp.float32)
    for at, value in enumerate((tx2, ty2, tz2, diagonal2, line2)):
        first, second = value[4:5, 384:512], value[4:5, 640:768]
        coarse_out[at : at + 1, :] = jnp.where(lanes_of(first) < 64, first, second)

    gram = jnp.zeros((80, 128), jnp.float32)
    for at in range(4):
        plane = 4 + at
        row = slice(plane, plane + 1)
        wide = jnp.concatenate([low[at], basis[at], high[at]], axis=1)
        dg, sx, sy, sz = (fine_out[kind, row, 256:1024] for kind in range(4))
        image = dg * wide - sy * roll(wide, -64) - roll(sy * wide, 64)
        image = (image - sz * roll(wide, -1) - roll(sz * wide, 1))[:, 128:640]
        after = right[...] if at == 3 else basis[at + 1]
        before = left[...] if at == 0 else basis[at - 1]
        image = image - fine_out[1, row, OWN : OWN + 512] * after
        image = image - fine_out[1, plane - 1 : plane, OWN : OWN + 512] * before
        image_out[at] = image
        vmat[0:72, :] = basis[at]
        vmat[68:128, :] = image[8:68]
        umat[0:72, :] = basis[at]
        umat[72:80, :] = image[0:8]
        gram = gram + dot_nt(umat[...], vmat[...])
    gram_out[0:80, :] = gram
    gram_out[80:128, :] = jnp.zeros((48, 128), jnp.float32)
    now_out[0:4, :] = gram[0:4]
    now_out[4:8, :] = gram[72:76]


def half_of(value, half, wanted):
    return jnp.where(half == wanted, value, roll(value, 64))


def spot_of(value, place):
    lane = lanes_of(value)
    return (lane // 64 == place // 4) & (lane % 4 == place % 4)


def middle_kernel(lines, at_y, got, out):
    total = got[0, 0:16, :]
    for source in range(1, got.shape[0]):
        total = total + got[source, 0:16, :]
    out[0:16, :] = total
    packed = jnp.zeros((8, 128), jnp.float32)
    for place in range(8):
        line = 2 * at_y[0] - 3 + place
        valid = (line >= 0) & (line < lines)
        kept = jnp.clip(line, 0, lines - 1)
        value = half_of(got[kept // 2, 16:24, :], kept % 2, place // 4)
        packed = packed + jnp.where(spot_of(value, place) & valid, value, 0.0)
    out[16:24, :] = packed


def residual_kernel(cells, count, got, basis, image, res_out, low_out, high_out, sums_out):
    total = got[0, 0:16, :]
    for source in range(1, got.shape[0]):
        total = total + got[source, 0:16, :]
    sums_out[...] = total[8:16]
    overlap, energy = total[0:4], total[4:8]
    lane = lanes_of(overlap)
    own = lane == lax.broadcasted_iota(jnp.int32, overlap.shape, 0)
    norm = jnp.sum(jnp.where(own, overlap, 0.0), axis=1, keepdims=True)
    top = jnp.sum(jnp.where(own, energy, 0.0), axis=1, keepdims=True)
    quotient = top / cells / (norm / cells + EPSILON)
    coupling = (energy - quotient * overlap) / cells
    used = (lane >= 8) & (lane < 8 + count[0])
    weights = jnp.where(used, coupling, 0.0)
    weights = jnp.concatenate([weights, jnp.zeros((4, 128), jnp.float32)], axis=0)
    for at in range(4):
        field = basis[at]
        value = image[at][0:4] - quotient * field[0:4]
        value = value - dot_nn(weights[:, 0:ROWS], field)[0:4]
        res_out[at] = value
        low_out[at] = value[:, 0:384]
        high_out[at] = value[:, 128:512]


def padded(value):
    return jnp.concatenate([value, jnp.zeros(value.shape, jnp.float32)], axis=0)


def apply_at(values, coefs, row, row_step, at, y_step, z_step, keys):
    here = values[at]
    dg, sx, sy, sz = (coefs[kind, row : row + 1, :] for kind in range(4))
    before = coefs[1, row - row_step : row - row_step + 1, :]
    image = dg * here - sx * values[at + 1] - before * values[at - 1]
    image = image - sy * roll(here, -y_step) - roll(sy * here, y_step)
    return image - sz * roll(here, -z_step) - roll(sz * here, z_step)


def fine_image(values, fine, plane):
    return apply_at(values, fine, plane, 1, plane, 64, 1, None)


def middle_image(values, middle, plane):
    return apply_at(values, middle, 2 * plane, 2, plane, 128, 2, None)


def planes_of(left, mid, right, first, last):
    parts = (left, mid, right)
    return {at: padded(parts[at // 4][at % 4]) for at in range(first, last)}


def down_kernel(left, mid, right, fine, middle, r1_out, r2_out, strip_out):
    source = planes_of(left, mid, right, 1, 11)
    error = {at: fine[4, at : at + 1, :] * source[at] for at in range(1, 11)}
    rest = {at: source[at] - fine_image(error, fine, at) for at in range(2, 10)}
    source1, error1 = {}, {}
    for plane in range(1, 5):
        value = pair_y(pair_z(rest[2 * plane] + rest[2 * plane + 1]))
        source1[plane] = value
        r1_out[plane - 1] = value[0:4]
        error1[plane] = middle[4, 2 * plane : 2 * plane + 1, :] * value
    low = sum(source1[plane] - middle_image(error1, middle, plane) for plane in (2, 3))
    low = quad_y(quad_z(low))
    r2_out[0:4, :] = low[0:4, 384:512]
    r2_out[4:8, :] = low[0:4, 640:768]
    for at in range(2):
        tiles = [error1[2 + at][0:4, 128 * t : 128 * t + 128] for t in range(1, 9)]
        lane = lanes_of(tiles[0])
        half, odd = lane // 64, lane % 2
        for group in range(2):
            a, b, c, d = tiles[4 * group : 4 * group + 4]
            value = jnp.where(half == 0, jnp.where(odd == 0, a, b), jnp.where(odd == 0, c, d))
            strip_out[at, 4 * group : 4 * group + 4, :] = value


def line_kernel(lines, at_y, got, coefs, out, solved):
    factors, previous, previous_factor, previous_link = [], None, None, None
    for source in range(lines // 2):
        rows = coefs[source, 16:24, :]
        turned = roll(rows, 64)
        first = lanes_of(rows) < 64
        for part in range(2):
            line = 2 * source + part
            value = jnp.where(first, rows, turned) if part == 0 else jnp.where(first, turned, rows)
            link, main = value[1:2], value[4:5]
            right = got[source, 4 * part : 4 * part + 4, :]
            solved[line, 4:8, :] = right
            if line == 0:
                scale = 1.0 / main
                update = scale * right
            else:
                scale = 1.0 / (main - previous_link * previous_factor)
                update = scale * (right + previous_link * previous)
            previous, previous_factor, previous_link = update, link * scale, link
            solved[line, 0:4, :] = update
            factors.append(previous_factor)
    for line in range(lines - 2, -1, -1):
        previous = solved[line, 0:4, :] + factors[line] * previous
        solved[line, 0:4, :] = previous
    packed = jnp.zeros((8, 128), jnp.float32)
    for place in range(8):
        line = 2 * at_y[0] - 3 + place
        valid = (line >= 0) & (line < lines)
        value = solved[jnp.clip(line, 0, lines - 1)]
        packed = packed + jnp.where(spot_of(value, place) & valid, value, 0.0)
    out[...] = packed


def up_kernel(
    at_x, got, coefs, r1, left, mid, right, fine, middle, basis, image, pre_out, now_out, vmat, wmat
):
    count = got.shape[0]
    error, source, links = {}, {}, {}
    for step in range(-3, 4):
        index = at_x[0] + step
        valid = ((index >= 0) & (index < count)).astype(jnp.float32)
        kept = jnp.clip(index, 0, count - 1)
        rows = got[kept, 0:8, :] * valid
        error[step] = padded(rows[0:4])
        source[step] = padded(rows[4:8])
        links[step] = coefs[kept, 16:24, :] * valid
    lane = lanes_of(error[0])
    spot = lane % 4
    for reach in range(SWEEPS - 2, -1, -1):
        updated = dict(error)
        for step in range(-1 - reach, 2 + reach):
            here = error[step]
            sx, sy, sz, dg = (links[step][kind : kind + 1] for kind in range(4))
            up = jnp.where(spot < 3, roll(here, -1), roll(here, -61))
            flux = sy * here
            down = jnp.where(spot > 0, roll(flux, 1), roll(flux, 61))
            value = dg * here - sx * error[step + 1] - links[step - 1][0:1] * error[step - 1]
            value = value - sy * up - down - sz * roll(here, -4) - roll(sz * here, 4)
            updated[step] = here + relax_weight(dg) * (source[step] - value)
        error = updated
    blank = jnp.zeros((8, 128), jnp.float32)
    coarse = {}
    for step in range(-1, 2):
        tiles = []
        for place in range(2, 6):
            value = jnp.where(spot_of(error[step], place), error[step], 0.0)
            value = quad_z(pair_z(value))
            value = value + roll(value, 64)
            tiles += [value, value]
        coarse[step] = jnp.concatenate([blank] + tiles + [blank], axis=1)

    def strip(step):
        index = at_x[0] + step
        valid = ((index >= 0) & (index < count)).astype(jnp.float32)
        rows = got[jnp.clip(index, 0, count - 1), 8:16, :] * valid
        tiles = []
        for group in range(2):
            part = padded(rows[4 * group : 4 * group + 4])
            for place in range(4):
                at = (lane // 64 == place // 2) & (lane % 2 == place % 2)
                value = pair_z(jnp.where(at, part, 0.0))
                tiles.append(value + roll(value, 64))
        return jnp.concatenate([blank] + tiles + [blank], axis=1)

    error1, source1 = {0: strip(-1) + coarse[-1], 5: strip(1) + coarse[1]}, {}
    for plane in range(1, 5):
        source1[plane] = padded(r1[plane - 1])
        weight = middle[4, 2 * plane : 2 * plane + 1, :]
        error1[plane] = weight * source1[plane] + coarse[plane // 2 - 1]
    final1 = {}
    for plane in range(1, 5):
        weight = middle[4, 2 * plane : 2 * plane + 1, :]
        final1[plane] = error1[plane] + weight * (
            source1[plane] - middle_image(error1, middle, plane)
        )
    source0 = planes_of(left, mid, right, 2, 10)
    error0 = {
        at: fine[4, at : at + 1, :] * source0[at] + final1[at // 2] for at in range(2, 10)
    }
    final0 = {}
    for at in range(3, 9):
        weight = fine[4, at : at + 1, :]
        final0[at] = error0[at] + weight * (source0[at] - fine_image(error0, fine, at))
    overlap = jnp.zeros((8, ROWS), jnp.float32)
    energy = jnp.zeros((8, ROWS), jnp.float32)
    for at in range(4):
        own = slice(OWN, OWN + 512)
        value = final0[4 + at][:, own]
        pre_out[at] = value[0:4]
        vmat[...] = basis[at]
        vmat[68:72, :] = value[0:4]
        wmat[...] = image[at]
        wmat[68:72, :] = fine_image(final0, fine, 4 + at)[0:4, own]
        overlap = overlap + dot_nt(value, vmat[...])
        energy = energy + dot_nt(value, wmat[...])
    now_out[...] = jnp.zeros((8, 128), jnp.float32)
    now_out[0:4, 0:ROWS] = overlap[0:4]
    now_out[4:8, 0:ROWS] = energy[0:4]


def eliminate(matrix, steps):
    row = lax.broadcasted_iota(jnp.int32, matrix.shape, 0)
    lane = lanes_of(matrix)
    for step in range(steps):
        column = jnp.sum(jnp.where(lane == step, matrix, 0.0), axis=1, keepdims=True)
        pivot = jnp.sum(jnp.where(row == step, matrix, 0.0), axis=0, keepdims=True)
        head = jnp.sum(jnp.where(lanes_of(pivot) == step, pivot, 0.0), axis=1, keepdims=True)
        below = jnp.where(row > step, column, 0.0) / head
        scaled = jnp.where(row == step, matrix * lax.rsqrt(head), matrix)
        matrix = scaled - below * pivot
    return matrix


def ritz_kernel(
    cells, count, got, gathered, basis, pre, modes_out, dirs_out, ritz_out, corr_out, field
):
    total = got[0]
    for source in range(1, got.shape[0]):
        total = total + got[source]
    total = total / cells
    gram = gathered[...] / cells
    shape = (16, 128)
    row = lax.broadcasted_iota(jnp.int32, shape, 0)
    lane = lax.broadcasted_iota(jnp.int32, shape, 1)
    zero4 = jnp.zeros((4, 128), jnp.float32)
    lane4 = lanes_of(zero4)
    used = (lane4 >= 8) & (lane4 < 8 + count[0])
    corr = jnp.where(used, total[0:4], 0.0)
    corr_out[...] = jnp.concatenate([corr, zero4], axis=0)
    locked_part = jnp.concatenate([zero4, -corr, zero4, zero4], axis=0)
    ones = ((row < 4) & (lane == row)) | ((row >= 8) & (row < 12) & (lane == row - 4))
    pre_ones = (row >= 4) & (row < 8) & (lane == row + 64)
    on_basis = jnp.where(ones, 1.0, locked_part)
    weights = jnp.where(pre_ones, 1.0, on_basis)
    pre_lane = (lane >= 68) & (lane < 72)

    def from_pre(part):
        rows4 = jnp.concatenate([zero4, part, zero4, zero4], axis=0)
        rows4 = jnp.where(lane < 72, rows4, 0.0)
        return jnp.where(pre_lane, 0.5 * rows4, rows4)

    first = jnp.where(lane < 68, dot_nn(on_basis, gram), 0.0)
    side = from_pre(total[0:4])
    mass = dot_nt(first, on_basis) + dot_nt(side, weights) + dot_nt(weights, side)
    second = jnp.where(lane >= 68, dot_nn(locked_part, gram), 0.0)
    pair = gram[72:80]
    pair = jnp.concatenate([pair[0:4], zero4, pair[4:8], zero4], axis=0)
    pair = jnp.where(lane < 68, jnp.where(lane < 8, 0.5 * pair, pair), 0.0)
    side = from_pre(total[4:8])
    stiff = dot_nt(second, roll(locked_part, 60))
    stiff = stiff + dot_nt(pair, on_basis) + dot_nt(on_basis, pair)
    stiff = stiff + dot_nt(side, weights) + dot_nt(weights, side)
    eye = jnp.where((row < 12) & (lane == row + 64), 1.0, 0.0)
    wide = jnp.zeros((16, 112), jnp.float32)
    mass = jnp.concatenate([mass, wide], axis=1)
    stiff = jnp.concatenate([stiff, wide], axis=1)
    done = eliminate(mass + roll(stiff, 32) + eye, 12)
    inside = (row < 12) & (lane < 12)
    half = jnp.where(inside, roll(done, -32), 0.0)
    inverse = jnp.where(inside, roll(done, -64), 0.0)
    reduced = dot_nt(half, inverse) + dot_nt(inverse, half)
    reduced = 0.5 * jnp.concatenate([reduced, wide], axis=1)
    top = jnp.sum(jnp.where(lane == row, reduced, 0.0), axis=(0, 1), keepdims=True)
    square = jnp.concatenate([reduced, jnp.zeros((112, 128), jnp.float32)], axis=0)
    row8 = lax.broadcasted_iota(jnp.int32, (8, 128), 0)
    lane8 = lax.broadcasted_iota(jnp.int32, (8, 128), 1)
    first4 = row8 < 4
    basis_q = jnp.where(first4 & (lane8 == row8), 1.0, 0.0)
    for step in range(RITZ):
        raised = top * basis_q - dot_nn(basis_q, square)
        products = dot_nt(raised, raised)
        products = jnp.concatenate([products, jnp.zeros((8, 120), jnp.float32)], axis=1)
        joint = products + roll(raised, 32)
        basis_q = jnp.where(first4 & (lane8 < 12), roll(eliminate(joint, 4), -32), 0.0)
    ritz = jnp.sum(basis_q * dot_nn(basis_q, square), axis=1, keepdims=True)
    ritz_out[...] = jnp.broadcast_to(ritz, (8, 128))
    tall = jnp.concatenate([inverse, jnp.zeros((112, 128), jnp.float32)], axis=0)
    coefs = dot_nn(basis_q, tall)
    tail = jnp.where(lane8 >= 4, coefs, 0.0)
    both = jnp.concatenate([coefs[0:4], tail[0:4]], axis=0)
    weights = jnp.concatenate([weights, jnp.zeros((112, 128), jnp.float32)], axis=0)
    mix = dot_nn(both, weights)[:, 0:ROWS]
    for at in range(4):
        field[...] = basis[at]
        field[68:72, :] = pre[at]
        value = dot_nn(mix, field[...])
        for part in range(4):
            modes_out[part, at : at + 1, :] = value[part : part + 1]
            dirs_out[part, at : at + 1, :] = value[4 + part : 5 + part]


def pair_shift(low, high, axis):
    count = lax.axis_size(axis)
    forward = [(at, at + 1) for at in range(count - 1)]
    backward = [(at + 1, at) for at in range(count - 1)]
    return lax.ppermute(high, axis, forward), lax.ppermute(low, axis, backward)


def spread(block, axis):
    count = lax.axis_size(axis)
    return lax.all_to_all(jnp.broadcast_to(block, (count,) + block.shape), axis, 0, 0)


def on_device(modes, directions, locked, perm_class, perm_table, locked_count):
    size_x, size_y = lax.axis_size("gx"), lax.axis_size("gy")
    at_x, at_y = lax.axis_index("gx"), lax.axis_index("gy")
    scalar_x = at_x.astype(jnp.int32).reshape(1)
    scalar_y = at_y.astype(jnp.int32).reshape(1)
    lines = 2 * size_y
    cells = float(4 * 512 * size_x * size_y)
    classes = jnp.arange(perm_table.shape[0], dtype=jnp.int32)
    conduct = jnp.sum(
        jnp.where(perm_class[None] == classes[:, None, None], perm_table[:, None, None], 0.0),
        axis=0,
    )
    basis = jnp.concatenate([modes, directions, locked, jnp.zeros((4, 4, 512), jnp.float32)], 0)
    basis = jnp.transpose(basis, (1, 0, 2))

    def edge(field, cond):
        extra = jnp.pad(cond.reshape(4, 3, 128), ((0, 0), (0, 1), (0, 0)))
        return jnp.concatenate([field[:, :BASIS], extra], axis=1)

    low, high = pair_shift(
        edge(basis[:, :, :128], conduct[:, :384]), edge(basis[:, :, 384:], conduct[:, 128:]), "gy"
    )
    cond_low = low[:, 68:71].reshape(4, 384)
    cond_high = high[:, 68:71].reshape(4, 384)
    conduct = jnp.concatenate([cond_low, conduct, cond_high], axis=1)
    rows = jnp.pad(conduct.reshape(10, 512), ((0, 2), (0, 0)))
    left, right = pair_shift(
        jnp.concatenate([basis[0, :BASIS], rows], 0),
        jnp.concatenate([basis[3, :BASIS], rows], 0),
        "gx",
    )
    cond_left = left[68:78].reshape(4, WIDE)
    cond_right = right[68:78].reshape(4, WIDE)
    fine, middle, image, now, gram, coarse = kernel_call(
        functools.partial(coef_kernel, 4.0 / float(lines * lines)),
        [(5, 16, WIDE), (5, 16, WIDE), (4, ROWS, 512), (8, 128), (128, 128), (8, 128)],
        cond_left, conduct, cond_right, basis, left[:ROWS], right[:ROWS], low, high,
        scratch=[(16, WIDE), (128, 512), (80, 512)],
    )
    shared = (size_y, 8, 128)
    packed = jnp.concatenate(
        [
            jnp.broadcast_to(now, shared),
            gram.reshape(shared),
            jnp.broadcast_to(coarse, shared),
        ],
        axis=1,
    )
    got_y = lax.all_to_all(packed, "gy", 0, 0)
    (chunk,) = kernel_call(
        functools.partial(middle_kernel, lines), [(24, 128)], scalar_y, got_y, scalars=1
    )
    got_x = spread(chunk, "gx")
    residual, res_low, res_high, sums = kernel_call(
        functools.partial(residual_kernel, cells),
        [(4, 4, 512), (4, 4, 384), (4, 4, 384), (8, 128)],
        locked_count, got_x, basis, image,
        scalars=1,
    )
    low, high = pair_shift(res_low, res_high, "gy")
    mid = jnp.concatenate([low, residual, high], axis=2)
    left, right = pair_shift(mid, mid, "gx")
    r1, r2, strips = kernel_call(
        down_kernel, [(4, 4, WIDE), (8, 128), (2, 8, 128)], left, mid, right, fine, middle
    )
    lines_y = spread(r2, "gy")
    (solved,) = kernel_call(
        functools.partial(line_kernel, lines), [(8, 128)], scalar_y, lines_y, got_y,
        scratch=[(lines, 8, 128)], scalars=1,
    )
    after = (jnp.arange(size_x, dtype=jnp.int32) > at_x)[:, None, None]
    packed = jnp.concatenate(
        [
            jnp.broadcast_to(solved, (size_x, 8, 128)),
            jnp.where(after, strips[0][None], strips[1][None]),
        ],
        axis=1,
    )
    around = lax.all_to_all(packed, "gx", 0, 0)
    precond, now = kernel_call(
        up_kernel, [(4, 4, 512), (8, 128)],
        scalar_x, around, got_x, r1, left, mid, right, fine, middle, basis, image,
        scratch=[(ROWS, 512), (ROWS, 512)], scalars=1,
    )
    got_y = spread(jnp.concatenate([now, sums], axis=0), "gy")
    gathered = got_y[:, 8:].reshape(8 * size_y, 128)
    got_x = spread(jnp.sum(got_y[:, :8], axis=0), "gx")
    new_modes, new_directions, ritz, corr = kernel_call(
        functools.partial(ritz_kernel, cells),
        [(4, 4, 512), (4, 4, 512), (8, 128), (8, 128)],
        locked_count, got_x, gathered, basis, precond,
        scratch=[(ROWS, 512)], scalars=1,
    )
    return (new_modes, new_directions, ritz[:4, 0], corr[:4, 8:68].T)


def solution(mesh):
    placed = (
        P(None, "gx", "gy"),
        P(None, "gx", "gy"),
        P(None, "gx", "gy"),
        P("gx", "gy"),
        P(),
        P(),
    )
    return jax.shard_map(
        on_device,
        mesh=mesh,
        in_specs=placed,
        out_specs=(P(None, "gx", "gy"), P(None, "gx", "gy"), P(), P()),
        check_vma=False,
    )
```

```python
import functools

import jax
import jax.numpy as jnp
from jax import lax
from jax.experimental import pallas as pl
from jax.experimental.pallas import tpu as pltpu
from jax.sharding import PartitionSpec as P

NZ = 64
ACTIVE = 4
LOCKED = 60
BASIS = 68
ROWS = 72
SWEEPS = 3
RITZ = 3
OMEGA = 0.6
EPSILON = 1e-06
PRECISE = lax.Precision.HIGHEST
WIDE = 1280
OWN = 384
INTERPRET = False


def kernel_call(body, out, *args, scratch=(), scalars=0, results=False):
    specs = [pl.BlockSpec(memory_space=pltpu.SMEM)] * scalars
    specs += [pl.BlockSpec(memory_space=pltpu.VMEM)] * (len(args) - scalars)
    stored = [pl.BlockSpec(memory_space=pltpu.VMEM if len(shape) > 1 else pltpu.SMEM) for shape in out]
    on_chip = not (results or INTERPRET)
    shapes = [
        pltpu.VMEM(shape, jnp.float32) if on_chip else jax.ShapeDtypeStruct(shape, jnp.float32)
        for shape in out
    ]
    if not INTERPRET:
        args = list(args[:scalars]) + [
            pltpu.with_memory_space_constraint(value, pltpu.VMEM) for value in args[scalars:]
        ]
    outs = pl.pallas_call(
        body,
        out_shape=shapes,
        in_specs=specs,
        out_specs=stored,
        scratch_shapes=[pltpu.VMEM(shape, jnp.float32) for shape in scratch],
        interpret=INTERPRET,
    )(*args)
    return outs


def roll(value, shift, axis=1):
    return pltpu.roll(value, shift % value.shape[axis], axis)


def lanes_of(value):
    return lax.broadcasted_iota(jnp.int32, value.shape, 1)


def pair_z(value):
    even = lanes_of(value) % 2 == 0
    return value + jnp.where(even, roll(value, -1), roll(value, 1))


def pair_y(value):
    first = lanes_of(value) % 128 < 64
    return value + jnp.where(first, roll(value, -64), roll(value, 64))


def quad_z(value):
    first = lanes_of(value) % 4 < 2
    return value + jnp.where(first, roll(value, -2), roll(value, 2))


def quad_y(value):
    odd = (lanes_of(value) // 128) % 2 == 1
    return value + jnp.where(odd, roll(value, -128), roll(value, 128))


def dot_nt(left, right):
    return lax.dot_general(
        left, right, (((1,), (1,)), ((), ())), precision=PRECISE, preferred_element_type=jnp.float32
    )


def dot_nn(left, right):
    return lax.dot_general(
        left, right, (((1,), (0,)), ((), ())), precision=PRECISE, preferred_element_type=jnp.float32
    )


def relax_weight(diagonal):
    inside = diagonal > 0
    return jnp.where(inside, OMEGA / jnp.where(inside, diagonal, 1.0), 0.0)


def joined(here, there):
    both = (here > 0) & (there > 0)
    return jnp.where(both, 2.0 * here * there / jnp.where(both, here + there, 1.0), 0.0)


def face(coupling, here, there):
    return coupling + jnp.where(there > 0, 0.0, 2.0 * here)


def coef_kernel(
    shift, count, cond_left, cond_mid, cond_right, basis, left, right, low, high,
    fine_out, middle_out, image_out, used_out, send_out, cond, vmat, umat,
):
    used = lanes_of(used_out)
    used_out[...] = jnp.where((used >= 8) & (used < 8 + count[0]), 1.0, 0.0)
    cond[0:4, :] = cond_left[...]
    cond[4:8, :] = cond_mid[...]
    cond[8:12, :] = cond_right[...]
    cond[12:16, :] = jnp.zeros((4, WIDE), jnp.float32)
    here = cond[...]
    z_at = lanes_of(here) % 64
    x_next, x_prev = roll(here, -1, 0), roll(here, 1, 0)
    y_next, y_prev = roll(here, -64), roll(here, 64)
    z_next = jnp.where(z_at < 63, roll(here, -1), 0.0)
    z_prev = jnp.where(z_at > 0, roll(here, 1), 0.0)
    tx, ty, tz = joined(here, x_next), joined(here, y_next), joined(here, z_next)
    y_faces = face(ty, here, y_next) + face(roll(ty, 64), here, y_prev)
    diagonal = face(tx, here, x_next) + face(roll(tx, 1, 0), here, x_prev) + y_faces
    diagonal = diagonal + face(tz, here, z_next) + face(roll(tz, 1), here, z_prev)
    for at, value in enumerate((diagonal, tx, ty, tz, relax_weight(diagonal))):
        fine_out[at] = value

    def pairs(value):
        return pair_y(pair_z(value))

    def pair_x(value):
        return value + roll(value, -1, 0)

    upper_y = lanes_of(here) % 128 >= 64
    sum_x = pairs(tx)
    odd_y = pair_x(pairs(jnp.where(upper_y, ty, 0.0)))
    odd_z = pair_x(pairs(jnp.where(z_at % 2 == 1, tz, 0.0)))
    even_y = pair_x(pairs(jnp.where(upper_y, 0.0, ty)))
    even_z = pair_x(pairs(jnp.where(z_at % 2 == 1, 0.0, tz)))
    tx1, ty1, tz1 = roll(sum_x, -1, 0), odd_y, odd_z
    diagonal1 = pair_x(pairs(diagonal)) - 2.0 * (sum_x + even_y + even_z)
    y_faces1 = pair_x(pairs(y_faces)) - 2.0 * even_y
    for at, value in enumerate((diagonal1, tx1, ty1, tz1, relax_weight(diagonal1))):
        middle_out[at] = value

    def quads(value):
        return quad_y(quad_z(value))

    def both_rows(value):
        return value + roll(value, -2, 0)

    upper_tile = (lanes_of(here) // 128) % 2 == 0
    sum_x1 = quads(tx1)
    ty2 = both_rows(quads(jnp.where(upper_tile, ty1, 0.0)))
    tz2 = both_rows(quads(jnp.where(z_at % 4 >= 2, tz1, 0.0)))
    inner_y = both_rows(quads(jnp.where(upper_tile, 0.0, ty1)))
    inner_z = both_rows(quads(jnp.where(z_at % 4 >= 2, 0.0, tz1)))
    tx2 = roll(sum_x1, -2, 0)
    diagonal2 = both_rows(quads(diagonal1)) - 2.0 * (sum_x1 + inner_y + inner_z)
    y_faces2 = both_rows(quads(y_faces1)) - 2.0 * inner_y
    line2 = y_faces2 + shift * (diagonal2 - y_faces2)
    coarse = []
    for value in (tx2, ty2, tz2, diagonal2, line2):
        first, second = value[4:5, 384:512], value[4:5, 640:768]
        coarse.append(jnp.where(lanes_of(first) < 64, first, second))
    coarse = jnp.concatenate(coarse + [jnp.zeros((3, 128), jnp.float32)], axis=0)

    gram = jnp.zeros((80, 128), jnp.float32)
    for at in range(4):
        plane = 4 + at
        row = slice(plane, plane + 1)
        wide = jnp.concatenate([low[at], basis[at], high[at]], axis=1)
        dg, sx, sy, sz = (fine_out[kind, row, 256:1024] for kind in range(4))
        image = dg * wide - sy * roll(wide, -64) - roll(sy * wide, 64)
        image = (image - sz * roll(wide, -1) - roll(sz * wide, 1))[:, 128:640]
        after = right[...] if at == 3 else basis[at + 1]
        before = left[...] if at == 0 else basis[at - 1]
        image = image - fine_out[1, row, OWN : OWN + 512] * after
        image = image - fine_out[1, plane - 1 : plane, OWN : OWN + 512] * before
        image_out[at] = image
        vmat[0:72, :] = basis[at]
        vmat[68:128, :] = image[8:68]
        umat[0:72, :] = basis[at]
        umat[72:80, :] = image[0:8]
        gram = gram + dot_nt(umat[...], vmat[...])
    now = jnp.concatenate([gram[0:4], gram[72:76]], axis=0)
    for target in range(send_out.shape[0]):
        send_out[target, 0:8, :] = now
        if target < 10:
            send_out[target, 8:16, :] = gram[8 * target : 8 * target + 8]
        else:
            send_out[target, 8:16, :] = jnp.zeros((8, 128), jnp.float32)
        send_out[target, 16:24, :] = coarse


def half_of(value, half, wanted):
    return value if half == wanted else roll(value, 64)


def spot_of(value, place):
    lane = lanes_of(value)
    return (lane // 64 == place // 4) & (lane % 4 == place % 4)


def middle_kernel(lines, got, send_out):
    at_y = lax.axis_index("gy")
    total = got[0, 0:16, :]
    for source in range(1, got.shape[0]):
        total = total + got[source, 0:16, :]
    packed = jnp.zeros((8, 128), jnp.float32)
    for place in range(8):
        source = at_y + (place - 3) // 2
        valid = (source >= 0) & (source < lines // 2)
        value = got[jnp.clip(source, 0, lines // 2 - 1), 16:24, :]
        value = half_of(value, (place - 3) % 2, place // 4)
        packed = packed + jnp.where(spot_of(value, place) & valid, value, 0.0)
    for target in range(send_out.shape[0]):
        send_out[target, 0:16, :] = total
        send_out[target, 16:24, :] = packed


def residual_kernel(cells, got, used, basis, image, res_out, low_out, high_out, sums_out):
    total = got[0, 0:16, :]
    for source in range(1, got.shape[0]):
        total = total + got[source, 0:16, :]
    sums_out[...] = total[8:16]
    overlap, energy = total[0:4], total[4:8]
    lane = lanes_of(overlap)
    own = lane == lax.broadcasted_iota(jnp.int32, overlap.shape, 0)
    norm = jnp.sum(jnp.where(own, overlap, 0.0), axis=1, keepdims=True)
    top = jnp.sum(jnp.where(own, energy, 0.0), axis=1, keepdims=True)
    quotient = top / cells / (norm / cells + EPSILON)
    coupling = (energy - quotient * overlap) / cells
    weights = jnp.where(used[0:4, :] > 0, coupling, 0.0)
    weights = jnp.concatenate([weights, jnp.zeros((4, 128), jnp.float32)], axis=0)
    for at in range(4):
        field = basis[at]
        value = image[at][0:4] - quotient * field[0:4]
        value = value - dot_nn(weights[:, 0:ROWS], field)[0:4]
        res_out[at] = value
        low_out[at] = value[:, 0:384]
        high_out[at] = value[:, 128:512]


def padded(value):
    return jnp.concatenate([value, jnp.zeros(value.shape, jnp.float32)], axis=0)


def apply_at(values, coefs, row, row_step, at, y_step, z_step, keys):
    here = values[at]
    dg, sx, sy, sz = (coefs[kind, row : row + 1, :] for kind in range(4))
    before = coefs[1, row - row_step : row - row_step + 1, :]
    image = dg * here - sx * values[at + 1] - before * values[at - 1]
    image = image - sy * roll(here, -y_step) - roll(sy * here, y_step)
    return image - sz * roll(here, -z_step) - roll(sz * here, z_step)


def fine_image(values, fine, plane):
    return apply_at(values, fine, plane, 1, plane, 64, 1, None)


def middle_image(values, middle, plane):
    return apply_at(values, middle, 2 * plane, 2, plane, 128, 2, None)


def planes_of(left, mid, right, first, last):
    parts = (left, mid, right)
    return {at: padded(parts[at // 4][at % 4]) for at in range(first, last)}


def down_kernel(left, mid, right, fine, middle, r1_out, send_out, strip_out):
    source = planes_of(left, mid, right, 1, 11)
    error = {at: fine[4, at : at + 1, :] * source[at] for at in range(1, 11)}
    rest = {at: source[at] - fine_image(error, fine, at) for at in range(2, 10)}
    source1, error1 = {}, {}
    for plane in range(1, 5):
        value = pair_y(pair_z(rest[2 * plane] + rest[2 * plane + 1]))
        source1[plane] = value
        r1_out[plane - 1] = value[0:4]
        error1[plane] = middle[4, 2 * plane : 2 * plane + 1, :] * value
    low = sum(source1[plane] - middle_image(error1, middle, plane) for plane in (2, 3))
    low = quad_y(quad_z(low))
    both = jnp.concatenate([low[0:4, 384:512], low[0:4, 640:768]], axis=0)
    for target in range(send_out.shape[0]):
        send_out[target] = both
    for at in range(2):
        tiles = [error1[2 + at][0:4, 128 * t : 128 * t + 128] for t in range(1, 9)]
        lane = lanes_of(tiles[0])
        half, odd = lane // 64, lane % 2
        for group in range(2):
            a, b, c, d = tiles[4 * group : 4 * group + 4]
            value = jnp.where(half == 0, jnp.where(odd == 0, a, b), jnp.where(odd == 0, c, d))
            strip_out[at, 4 * group : 4 * group + 4, :] = value


def line_kernel(lines, got, coefs, strips, send_out, solved):
    at_x, at_y = lax.axis_index("gx"), lax.axis_index("gy")
    factors, previous, previous_factor, previous_link = [], None, None, None
    for source in range(lines // 2):
        rows = coefs[source, 16:24, :]
        turned = roll(rows, 64)
        first = lanes_of(rows) < 64
        for part in range(2):
            line = 2 * source + part
            value = jnp.where(first, rows, turned) if part == 0 else jnp.where(first, turned, rows)
            link, main = value[1:2], value[4:5]
            right = got[source, 4 * part : 4 * part + 4, :]
            solved[line, 4:8, :] = right
            if line == 0:
                scale = 1.0 / main
                update = scale * right
            else:
                scale = 1.0 / (main - previous_link * previous_factor)
                update = scale * (right + previous_link * previous)
            previous, previous_factor, previous_link = update, link * scale, link
            solved[line, 0:4, :] = update
            factors.append(previous_factor)
    for line in range(lines - 2, -1, -1):
        previous = solved[line, 0:4, :] + factors[line] * previous
        solved[line, 0:4, :] = previous
    packed = jnp.zeros((8, 128), jnp.float32)
    for place in range(8):
        line = 2 * at_y - 3 + place
        valid = (line >= 0) & (line < lines)
        value = solved[jnp.clip(line, 0, lines - 1)]
        packed = packed + jnp.where(spot_of(value, place) & valid, value, 0.0)
    for target in range(send_out.shape[0]):
        send_out[target, 0:8, :] = packed
        send_out[target, 8:16, :] = strips[(at_x >= target).astype(jnp.int32)]


def up_kernel(
    got, coefs, r1, left, mid, right, fine, middle, basis, image, sums, pre_out, send_out, vmat, wmat
):
    at_x = lax.axis_index("gx")
    count = got.shape[0]
    error, source, links = {}, {}, {}
    for step in range(-3, 4):
        index = at_x + step
        valid = ((index >= 0) & (index < count)).astype(jnp.float32)
        kept = jnp.clip(index, 0, count - 1)
        rows = got[kept, 0:8, :] * valid
        error[step] = padded(rows[0:4])
        source[step] = padded(rows[4:8])
        links[step] = coefs[kept, 16:24, :] * valid
    lane = lanes_of(error[0])
    spot = lane % 4
    for reach in range(SWEEPS - 2, -1, -1):
        updated = dict(error)
        for step in range(-1 - reach, 2 + reach):
            here = error[step]
            sx, sy, sz, dg = (links[step][kind : kind + 1] for kind in range(4))
            up = jnp.where(spot < 3, roll(here, -1), roll(here, -61))
            flux = sy * here
            down = jnp.where(spot > 0, roll(flux, 1), roll(flux, 61))
            value = dg * here - sx * error[step + 1] - links[step - 1][0:1] * error[step - 1]
            value = value - sy * up - down - sz * roll(here, -4) - roll(sz * here, 4)
            updated[step] = here + relax_weight(dg) * (source[step] - value)
        error = updated
    blank = jnp.zeros((8, 128), jnp.float32)
    coarse = {}
    for step in range(-1, 2):
        tiles = []
        for place in range(2, 6):
            value = jnp.where(spot_of(error[step], place), error[step], 0.0)
            value = quad_z(pair_z(value))
            value = value + roll(value, 64)
            tiles += [value, value]
        coarse[step] = jnp.concatenate([blank] + tiles + [blank], axis=1)

    def strip(step):
        index = at_x + step
        valid = ((index >= 0) & (index < count)).astype(jnp.float32)
        rows = got[jnp.clip(index, 0, count - 1), 8:16, :] * valid
        tiles = []
        for group in range(2):
            part = padded(rows[4 * group : 4 * group + 4])
            for place in range(4):
                at = (lane // 64 == place // 2) & (lane % 2 == place % 2)
                value = pair_z(jnp.where(at, part, 0.0))
                tiles.append(value + roll(value, 64))
        return jnp.concatenate([blank] + tiles + [blank], axis=1)

    error1, source1 = {0: strip(-1) + coarse[-1], 5: strip(1) + coarse[1]}, {}
    for plane in range(1, 5):
        source1[plane] = padded(r1[plane - 1])
        weight = middle[4, 2 * plane : 2 * plane + 1, :]
        error1[plane] = weight * source1[plane] + coarse[plane // 2 - 1]
    final1 = {}
    for plane in range(1, 5):
        weight = middle[4, 2 * plane : 2 * plane + 1, :]
        final1[plane] = error1[plane] + weight * (
            source1[plane] - middle_image(error1, middle, plane)
        )
    source0 = planes_of(left, mid, right, 2, 10)
    error0 = {
        at: fine[4, at : at + 1, :] * source0[at] + final1[at // 2] for at in range(2, 10)
    }
    final0 = {}
    for at in range(3, 9):
        weight = fine[4, at : at + 1, :]
        final0[at] = error0[at] + weight * (source0[at] - fine_image(error0, fine, at))
    overlap = jnp.zeros((8, ROWS), jnp.float32)
    energy = jnp.zeros((8, ROWS), jnp.float32)
    for at in range(4):
        own = slice(OWN, OWN + 512)
        value = final0[4 + at][:, own]
        pre_out[at] = value[0:4]
        vmat[...] = basis[at]
        vmat[68:72, :] = value[0:4]
        wmat[...] = image[at]
        wmat[68:72, :] = fine_image(final0, fine, 4 + at)[0:4, own]
        overlap = overlap + dot_nt(value, vmat[...])
        energy = energy + dot_nt(value, wmat[...])
    now = jnp.concatenate([overlap[0:4], energy[0:4]], axis=0)
    now = jnp.concatenate([now, jnp.zeros((8, 128 - ROWS), jnp.float32)], axis=1)
    for target in range(send_out.shape[0]):
        send_out[target, 0:8, :] = now
        send_out[target, 8:16, :] = sums[...]


def eliminate(matrix, steps):
    row = lax.broadcasted_iota(jnp.int32, matrix.shape, 0)
    for step in range(steps):
        pivot = matrix[step : step + 1, :] / matrix[step : step + 1, step : step + 1]
        column = matrix[:, step : step + 1]
        matrix = matrix - jnp.where(row > step, column, 0.0) * pivot
    diagonal = jnp.where(lanes_of(matrix) == row, matrix, 0.0)
    diagonal = jnp.sum(diagonal, axis=1, keepdims=True)
    scale = lax.rsqrt(jnp.where(row[:, 0:1] < steps, diagonal, 1.0))
    return matrix * scale


def ritz_kernel(
    cells, got, gathered, used, basis, pre, modes_out, dirs_out, ritz_out, corr_out, field
):
    total = got[0]
    for source in range(1, got.shape[0]):
        total = total + got[source]
    total = total / cells
    gram = gathered[...] / cells
    shape = (16, 128)
    row = lax.broadcasted_iota(jnp.int32, shape, 0)
    lane = lax.broadcasted_iota(jnp.int32, shape, 1)
    zero4 = jnp.zeros((4, 128), jnp.float32)
    corr = jnp.where(used[0:4, :] > 0, total[0:4], 0.0)
    pick = lax.broadcasted_iota(jnp.int32, (64, 128), 0) + 8
    pick = jnp.where(lax.broadcasted_iota(jnp.int32, (64, 128), 1) == pick, 1.0, 0.0)
    corr_out[...] = dot_nt(pick, jnp.concatenate([corr, zero4], axis=0))[0:LOCKED, 0:4]
    locked_part = jnp.concatenate([zero4, -corr, zero4, zero4], axis=0)
    ones = ((row < 4) & (lane == row)) | ((row >= 8) & (row < 12) & (lane == row - 4))
    pre_ones = (row >= 4) & (row < 8) & (lane == row + 64)
    on_basis = jnp.where(ones, 1.0, locked_part)
    weights = jnp.where(pre_ones, 1.0, on_basis)
    pre_lane = (lane >= 68) & (lane < 72)

    def from_pre(part):
        rows4 = jnp.concatenate([zero4, part, zero4, zero4], axis=0)
        rows4 = jnp.where(lane < 72, rows4, 0.0)
        return jnp.where(pre_lane, 0.5 * rows4, rows4)

    first = jnp.where(lane < 68, dot_nn(on_basis, gram), 0.0)
    side = from_pre(total[0:4])
    mass = dot_nt(first, on_basis) + dot_nt(side, weights) + dot_nt(weights, side)
    second = jnp.where(lane >= 68, dot_nn(locked_part, gram), 0.0)
    pair = gram[72:80]
    pair = jnp.concatenate([pair[0:4], zero4, pair[4:8], zero4], axis=0)
    pair = jnp.where(lane < 68, jnp.where(lane < 8, 0.5 * pair, pair), 0.0)
    side = from_pre(total[4:8])
    stiff = dot_nt(second, roll(locked_part, 60))
    stiff = stiff + dot_nt(pair, on_basis) + dot_nt(on_basis, pair)
    stiff = stiff + dot_nt(side, weights) + dot_nt(weights, side)
    eye = jnp.where((row < 12) & (lane == row + 64), 1.0, 0.0)
    wide = jnp.zeros((16, 112), jnp.float32)
    mass = jnp.concatenate([mass, wide], axis=1)
    stiff = jnp.concatenate([stiff, wide], axis=1)
    done = eliminate(mass + roll(stiff, 32) + eye, 12)
    inside = (row < 12) & (lane < 12)
    half = jnp.where(inside, roll(done, -32), 0.0)
    inverse = jnp.where(inside, roll(done, -64), 0.0)
    reduced = dot_nt(half, inverse) + dot_nt(inverse, half)
    reduced = 0.5 * jnp.concatenate([reduced, wide], axis=1)
    top = jnp.sum(jnp.where(lane == row, reduced, 0.0), axis=(0, 1), keepdims=True)
    square = jnp.concatenate([reduced, jnp.zeros((112, 128), jnp.float32)], axis=0)
    row8 = lax.broadcasted_iota(jnp.int32, (8, 128), 0)
    lane8 = lax.broadcasted_iota(jnp.int32, (8, 128), 1)
    first4 = row8 < 4
    basis_q = jnp.where(first4 & (lane8 == row8), 1.0, 0.0)
    for step in range(RITZ):
        raised = top * basis_q - dot_nn(basis_q, square)
        products = dot_nt(raised, raised)
        products = jnp.concatenate([products, jnp.zeros((8, 120), jnp.float32)], axis=1)
        joint = products + roll(raised, 32)
        basis_q = jnp.where(first4 & (lane8 < 12), roll(eliminate(joint, 4), -32), 0.0)
    ritz = jnp.sum(basis_q * dot_nn(basis_q, square), axis=1, keepdims=True)
    for part in range(ACTIVE):
        ritz_out[part] = ritz[part, 0]
    tall = jnp.concatenate([inverse, jnp.zeros((112, 128), jnp.float32)], axis=0)
    coefs = dot_nn(basis_q, tall)
    tail = jnp.where(lane8 >= 4, coefs, 0.0)
    both = jnp.concatenate([coefs[0:4], tail[0:4]], axis=0)
    weights = jnp.concatenate([weights, jnp.zeros((112, 128), jnp.float32)], axis=0)
    mix = dot_nn(both, weights)[:, 0:ROWS]
    for at in range(4):
        field[...] = basis[at]
        field[68:72, :] = pre[at]
        value = dot_nn(mix, field[...])
        for part in range(4):
            modes_out[part, at : at + 1, :] = value[part : part + 1]
            dirs_out[part, at : at + 1, :] = value[4 + part : 5 + part]


def pair_shift(low, high, axis):
    count = lax.axis_size(axis)
    forward = [(at, at + 1) for at in range(count - 1)]
    backward = [(at + 1, at) for at in range(count - 1)]
    return lax.ppermute(high, axis, forward), lax.ppermute(low, axis, backward)


def spread(block, axis):
    count = lax.axis_size(axis)
    return lax.all_to_all(jnp.broadcast_to(block, (count,) + block.shape), axis, 0, 0)


def on_device(modes, directions, locked, perm_class, perm_table, locked_count):
    size_x, size_y = lax.axis_size("gx"), lax.axis_size("gy")
    lines = 2 * size_y
    cells = float(4 * 512 * size_x * size_y)
    classes = jnp.arange(perm_table.shape[0], dtype=jnp.int32)
    conduct = jnp.sum(
        jnp.where(perm_class[None] == classes[:, None, None], perm_table[:, None, None], 0.0),
        axis=0,
    )
    basis = jnp.concatenate([modes, directions, locked, jnp.zeros((4, 4, 512), jnp.float32)], 0)
    basis = jnp.transpose(basis, (1, 0, 2))

    def edge(field, cond):
        extra = jnp.pad(cond.reshape(4, 3, 128), ((0, 0), (0, 1), (0, 0)))
        return jnp.concatenate([field[:, :BASIS], extra], axis=1)

    low, high = pair_shift(
        edge(basis[:, :, :128], conduct[:, :384]), edge(basis[:, :, 384:], conduct[:, 128:]), "gy"
    )
    cond_low = low[:, 68:71].reshape(4, 384)
    cond_high = high[:, 68:71].reshape(4, 384)
    conduct = jnp.concatenate([cond_low, conduct, cond_high], axis=1)
    rows = jnp.pad(conduct.reshape(10, 512), ((0, 2), (0, 0)))
    left, right = pair_shift(
        jnp.concatenate([basis[0, :BASIS], rows], 0),
        jnp.concatenate([basis[3, :BASIS], rows], 0),
        "gx",
    )
    cond_left = left[68:78].reshape(4, WIDE)
    cond_right = right[68:78].reshape(4, WIDE)
    fine, middle, image, used, send = kernel_call(
        functools.partial(coef_kernel, 4.0 / float(lines * lines)),
        [(5, 16, WIDE), (5, 16, WIDE), (4, ROWS, 512), (8, 128), (size_y, 24, 128)],
        locked_count, cond_left, conduct, cond_right, basis, left[:ROWS], right[:ROWS], low, high,
        scratch=[(16, WIDE), (128, 512), (80, 512)], scalars=1,
    )
    got_y = lax.all_to_all(send, "gy", 0, 0)
    (send,) = kernel_call(
        functools.partial(middle_kernel, lines), [(size_x, 24, 128)], got_y
    )
    got_x = lax.all_to_all(send, "gx", 0, 0)
    residual, res_low, res_high, sums = kernel_call(
        functools.partial(residual_kernel, cells),
        [(4, 4, 512), (4, 4, 384), (4, 4, 384), (8, 128)],
        got_x, used, basis, image,
    )
    low, high = pair_shift(res_low, res_high, "gy")
    mid = jnp.concatenate([low, residual, high], axis=2)
    left, right = pair_shift(mid, mid, "gx")
    r1, send, strips = kernel_call(
        down_kernel, [(4, 4, WIDE), (size_y, 8, 128), (2, 8, 128)], left, mid, right, fine, middle
    )
    (send,) = kernel_call(
        functools.partial(line_kernel, lines), [(size_x, 16, 128)],
        lax.all_to_all(send, "gy", 0, 0), got_y, strips,
        scratch=[(lines, 8, 128)],
    )
    precond, send = kernel_call(
        up_kernel, [(4, 4, 512), (size_y, 16, 128)],
        lax.all_to_all(send, "gx", 0, 0), got_x, r1, left, mid, right, fine, middle, basis, image,
        sums,
        scratch=[(ROWS, 512), (ROWS, 512)],
    )
    got_y = lax.all_to_all(send, "gy", 0, 0)
    gathered = got_y[:, 8:].reshape(8 * size_y, 128)
    got_x = spread(jnp.sum(got_y[:, :8], axis=0), "gx")
    return tuple(
        kernel_call(
            functools.partial(ritz_kernel, cells),
            [(4, 4, 512), (4, 4, 512), (4,), (LOCKED, 4)],
            got_x, gathered, used, basis, precond,
            scratch=[(ROWS, 512)], results=True,
        )
    )


def solution(mesh):
    placed = (
        P(None, "gx", "gy"),
        P(None, "gx", "gy"),
        P(None, "gx", "gy"),
        P("gx", "gy"),
        P(),
        P(),
    )
    return jax.shard_map(
        on_device,
        mesh=mesh,
        in_specs=placed,
        out_specs=(P(None, "gx", "gy"), P(None, "gx", "gy"), P(), P()),
        check_vma=False,
    )
```

```python
import functools

import jax
import jax.numpy as jnp
from jax import lax
from jax.experimental import pallas as pl
from jax.experimental.pallas import tpu as pltpu
from jax.sharding import PartitionSpec as P

NZ = 64
ACTIVE = 4
LOCKED = 60
BASIS = 68
ROWS = 72
SWEEPS = 3
RITZ = 3
OMEGA = 0.6
EPSILON = 1e-06
PRECISE = lax.Precision.HIGHEST
WIDE = 1280
OWN = 384
INTERPRET = False


def kernel_call(body, out, *args, scratch=(), scalars=0, far=(), far_out=(), results=False):
    specs, placed = [], []
    for at, value in enumerate(args):
        space = pltpu.SMEM if at < scalars else pl.ANY if at in far else pltpu.VMEM
        specs.append(pl.BlockSpec(memory_space=space))
        if space is pltpu.VMEM and not INTERPRET:
            value = pltpu.with_memory_space_constraint(value, pltpu.VMEM)
        placed.append(value)
    shapes, stored = [], []
    for at, shape in enumerate(out):
        space = pltpu.SMEM if len(shape) == 1 else pl.ANY if at in far_out else pltpu.VMEM
        stored.append(pl.BlockSpec(memory_space=space))
        if space is pltpu.VMEM and not (results or INTERPRET):
            shapes.append(pltpu.VMEM(shape, jnp.float32))
        else:
            shapes.append(jax.ShapeDtypeStruct(shape, jnp.float32))
    copies = len(far) + len(far_out)
    held = [pltpu.VMEM(shape, jnp.float32) for shape in scratch]
    held += [pltpu.SemaphoreType.DMA] * copies
    return pl.pallas_call(
        body,
        out_shape=shapes,
        in_specs=specs,
        out_specs=stored,
        scratch_shapes=held,
        interpret=INTERPRET,
    )(*placed)


def roll(value, shift, axis=1):
    return pltpu.roll(value, shift % value.shape[axis], axis)


def lanes_of(value):
    return lax.broadcasted_iota(jnp.int32, value.shape, 1)


def pair_z(value):
    even = lanes_of(value) % 2 == 0
    return value + jnp.where(even, roll(value, -1), roll(value, 1))


def pair_y(value):
    first = lanes_of(value) % 128 < 64
    return value + jnp.where(first, roll(value, -64), roll(value, 64))


def quad_z(value):
    first = lanes_of(value) % 4 < 2
    return value + jnp.where(first, roll(value, -2), roll(value, 2))


def quad_y(value):
    odd = (lanes_of(value) // 128) % 2 == 1
    return value + jnp.where(odd, roll(value, -128), roll(value, 128))


def dot_nt(left, right):
    return lax.dot_general(
        left, right, (((1,), (1,)), ((), ())), precision=PRECISE, preferred_element_type=jnp.float32
    )


def dot_nn(left, right):
    return lax.dot_general(
        left, right, (((1,), (0,)), ((), ())), precision=PRECISE, preferred_element_type=jnp.float32
    )


def relax_weight(diagonal):
    inside = diagonal > 0
    return jnp.where(inside, OMEGA / jnp.where(inside, diagonal, 1.0), 0.0)


def joined(here, there):
    both = (here > 0) & (there > 0)
    return jnp.where(both, 2.0 * here * there / jnp.where(both, here + there, 1.0), 0.0)


def face(coupling, here, there):
    return coupling + jnp.where(there > 0, 0.0, 2.0 * here)


def coef_kernel(
    shift, count, cond_left, cond_mid, cond_right, basis, left, right, low, high,
    fine_far, middle_far, image_out, used_out, send_out, cond, vmat, umat, fine_out, middle_out,
    fine_done, middle_done,
):
    used = lanes_of(used_out)
    used_out[...] = jnp.where((used >= 8) & (used < 8 + count[0]), 1.0, 0.0)
    cond[0:4, :] = cond_left[...]
    cond[4:8, :] = cond_mid[...]
    cond[8:12, :] = cond_right[...]
    cond[12:16, :] = jnp.zeros((4, WIDE), jnp.float32)
    here = cond[...]
    z_at = lanes_of(here) % 64
    x_next, x_prev = roll(here, -1, 0), roll(here, 1, 0)
    y_next, y_prev = roll(here, -64), roll(here, 64)
    z_next = jnp.where(z_at < 63, roll(here, -1), 0.0)
    z_prev = jnp.where(z_at > 0, roll(here, 1), 0.0)
    tx, ty, tz = joined(here, x_next), joined(here, y_next), joined(here, z_next)
    y_faces = face(ty, here, y_next) + face(roll(ty, 64), here, y_prev)
    diagonal = face(tx, here, x_next) + face(roll(tx, 1, 0), here, x_prev) + y_faces
    diagonal = diagonal + face(tz, here, z_next) + face(roll(tz, 1), here, z_prev)
    for at, value in enumerate((diagonal, tx, ty, tz, relax_weight(diagonal))):
        fine_out[at] = value

    def pairs(value):
        return pair_y(pair_z(value))

    def pair_x(value):
        return value + roll(value, -1, 0)

    upper_y = lanes_of(here) % 128 >= 64
    sum_x = pairs(tx)
    odd_y = pair_x(pairs(jnp.where(upper_y, ty, 0.0)))
    odd_z = pair_x(pairs(jnp.where(z_at % 2 == 1, tz, 0.0)))
    even_y = pair_x(pairs(jnp.where(upper_y, 0.0, ty)))
    even_z = pair_x(pairs(jnp.where(z_at % 2 == 1, 0.0, tz)))
    tx1, ty1, tz1 = roll(sum_x, -1, 0), odd_y, odd_z
    diagonal1 = pair_x(pairs(diagonal)) - 2.0 * (sum_x + even_y + even_z)
    y_faces1 = pair_x(pairs(y_faces)) - 2.0 * even_y
    for at, value in enumerate((diagonal1, tx1, ty1, tz1, relax_weight(diagonal1))):
        middle_out[at] = value
    fine_copy = pltpu.make_async_copy(fine_out, fine_far, fine_done)
    middle_copy = pltpu.make_async_copy(middle_out, middle_far, middle_done)
    fine_copy.start()
    middle_copy.start()

    def quads(value):
        return quad_y(quad_z(value))

    def both_rows(value):
        return value + roll(value, -2, 0)

    upper_tile = (lanes_of(here) // 128) % 2 == 0
    sum_x1 = quads(tx1)
    ty2 = both_rows(quads(jnp.where(upper_tile, ty1, 0.0)))
    tz2 = both_rows(quads(jnp.where(z_at % 4 >= 2, tz1, 0.0)))
    inner_y = both_rows(quads(jnp.where(upper_tile, 0.0, ty1)))
    inner_z = both_rows(quads(jnp.where(z_at % 4 >= 2, 0.0, tz1)))
    tx2 = roll(sum_x1, -2, 0)
    diagonal2 = both_rows(quads(diagonal1)) - 2.0 * (sum_x1 + inner_y + inner_z)
    y_faces2 = both_rows(quads(y_faces1)) - 2.0 * inner_y
    line2 = y_faces2 + shift * (diagonal2 - y_faces2)
    coarse = []
    for value in (tx2, ty2, tz2, diagonal2, line2):
        first, second = value[4:5, 384:512], value[4:5, 640:768]
        coarse.append(jnp.where(lanes_of(first) < 64, first, second))

    gram = jnp.zeros((80, 128), jnp.float32)
    for at in range(4):
        plane = 4 + at
        row = slice(plane, plane + 1)
        below, above = low[at % 2, 0:ROWS, :], high[at % 2, 0:ROWS, :]
        below = roll(below, 64) if at < 2 else below
        above = above if at < 2 else roll(above, 64)
        wide = jnp.concatenate([below, basis[at], above], axis=1)
        dg, sx, sy, sz = (fine_out[kind, row, 256:1024] for kind in range(4))
        image = dg * wide - sy * roll(wide, -64) - roll(sy * wide, 64)
        image = (image - sz * roll(wide, -1) - roll(sz * wide, 1))[:, 128:640]
        after = right[...] if at == 3 else basis[at + 1]
        before = left[...] if at == 0 else basis[at - 1]
        image = image - fine_out[1, row, OWN : OWN + 512] * after
        image = image - fine_out[1, plane - 1 : plane, OWN : OWN + 512] * before
        image_out[at] = image[0:8]
        vmat[0:72, :] = basis[at]
        vmat[68:128, :] = image[8:68]
        umat[0:72, :] = basis[at]
        umat[72:80, :] = image[0:8]
        gram = gram + dot_nt(umat[...], vmat[...])
    now = packed_rows(jnp.concatenate([gram[0:4], gram[72:76]], axis=0), [coarse[0], coarse[2]])
    rest = jnp.concatenate([coarse[1], coarse[4], coarse[3]], axis=0)
    for target in range(send_out.shape[0]):
        send_out[target, 0:8, :] = now
        send_out[target, 8:13, :] = gram[5 * target : 5 * target + 5]
        send_out[target, 13:16, :] = rest
    fine_copy.wait()
    middle_copy.wait()


def packed_rows(rows, extra):
    lane = lanes_of(rows)
    row = lax.broadcasted_iota(jnp.int32, rows.shape, 0)
    for at, value in enumerate(extra):
        for part in range(4):
            moved = roll(value, 96 - 32 * part)
            rows = jnp.where((row == 4 * at + part) & (lane >= 96), moved, rows)
    return rows


def unpacked_row(rows, at):
    lane = lanes_of(rows[0:1])
    value = roll(rows[4 * at : 4 * at + 1], -96)
    for part in range(1, 4):
        moved = roll(rows[4 * at + part : 4 * at + part + 1], 32 * part - 96)
        value = jnp.where(lane // 32 == part, moved, value)
    return value


def half_of(value, half, wanted):
    return value if half == wanted else roll(value, 64)


def spot_of(value, place):
    lane = lanes_of(value)
    return (lane // 64 == place // 4) & (lane % 4 == place % 4)


def middle_kernel(lines, got, send_out):
    at_y = lax.axis_index("gy")
    total = got[0]
    for source in range(1, got.shape[0]):
        total = total + got[source]
    packed = jnp.zeros((4, 128), jnp.float32)
    for place in range(8):
        source = at_y + (place - 3) // 2
        valid = (source >= 0) & (source < lines // 2)
        value = got[jnp.clip(source, 0, lines // 2 - 1)]
        tx, tz = unpacked_row(value, 0), unpacked_row(value, 1)
        value = jnp.concatenate([tx, value[13:14], tz, value[15:16]], axis=0)
        value = half_of(value, (place - 3) % 2, place // 4)
        packed = packed + jnp.where(spot_of(value, place) & valid, value, 0.0)
    now = packed_rows(total[0:8], [packed[0:1]])
    for target in range(send_out.shape[0]):
        send_out[target, 0:8, :] = now
        send_out[target, 8:13, :] = total[8:13]
        send_out[target, 13:16, :] = packed[1:4]


def residual_kernel(cells, got, used, basis, image, res_out, low_out, high_out, sums_out):
    total = got[0]
    for source in range(1, got.shape[0]):
        total = total + got[source]
    sums_out[...] = total[8:16]
    overlap, energy = total[0:4], total[4:8]
    lane = lanes_of(overlap)
    own = lane == lax.broadcasted_iota(jnp.int32, overlap.shape, 0)
    norm = jnp.sum(jnp.where(own, overlap, 0.0), axis=1, keepdims=True)
    top = jnp.sum(jnp.where(own, energy, 0.0), axis=1, keepdims=True)
    quotient = top / cells / (norm / cells + EPSILON)
    coupling = (energy - quotient * overlap) / cells
    weights = jnp.where(used[0:4, :] > 0, coupling, 0.0)
    weights = jnp.concatenate([weights, jnp.zeros((4, 128), jnp.float32)], axis=0)
    for at in range(4):
        field = basis[at]
        value = image[at][0:4] - quotient * field[0:4]
        value = value - dot_nn(weights[:, 0:ROWS], field)[0:4]
        res_out[at] = value
        low_out[at] = value[:, 0:384]
        high_out[at] = value[:, 128:512]


def padded(value):
    return jnp.concatenate([value, jnp.zeros(value.shape, jnp.float32)], axis=0)


def apply_at(values, coefs, row, row_step, at, y_step, z_step, keys):
    here = values[at]
    dg, sx, sy, sz = (coefs[kind, row : row + 1, :] for kind in range(4))
    before = coefs[1, row - row_step : row - row_step + 1, :]
    image = dg * here - sx * values[at + 1] - before * values[at - 1]
    image = image - sy * roll(here, -y_step) - roll(sy * here, y_step)
    return image - sz * roll(here, -z_step) - roll(sz * here, z_step)


def fine_image(values, fine, plane):
    return apply_at(values, fine, plane, 1, plane, 64, 1, None)


def middle_image(values, middle, plane):
    return apply_at(values, middle, 2 * plane, 2, plane, 128, 2, None)


def planes_of(left, mid, right, first, last):
    parts = (left, mid, right)
    return {at: padded(parts[at // 4][at % 4]) for at in range(first, last)}


def down_kernel(left, mid, right, fine, middle, r1_out, send_out, strip_out):
    source = planes_of(left, mid, right, 1, 11)
    error = {at: fine[4, at : at + 1, :] * source[at] for at in range(1, 11)}
    rest = {at: source[at] - fine_image(error, fine, at) for at in range(2, 10)}
    source1, error1 = {}, {}
    for plane in range(1, 5):
        value = pair_y(pair_z(rest[2 * plane] + rest[2 * plane + 1]))
        source1[plane] = value
        r1_out[plane - 1] = value[0:4]
        error1[plane] = middle[4, 2 * plane : 2 * plane + 1, :] * value
    low = sum(source1[plane] - middle_image(error1, middle, plane) for plane in (2, 3))
    low = quad_y(quad_z(low))
    both = jnp.concatenate([low[0:4, 384:512], low[0:4, 640:768]], axis=0)
    for target in range(send_out.shape[0]):
        send_out[target] = both
    for at in range(2):
        tiles = [error1[2 + at][0:4, 128 * t : 128 * t + 128] for t in range(1, 9)]
        lane = lanes_of(tiles[0])
        half, odd = lane // 64, lane % 2
        for group in range(2):
            a, b, c, d = tiles[4 * group : 4 * group + 4]
            value = jnp.where(half == 0, jnp.where(odd == 0, a, b), jnp.where(odd == 0, c, d))
            strip_out[at, 4 * group : 4 * group + 4, :] = value


def line_kernel(lines, got, coefs, strips, send_out, solved):
    at_x, at_y = lax.axis_index("gx"), lax.axis_index("gy")
    factors, previous, previous_factor, previous_link = [], None, None, None
    for source in range(lines // 2):
        rows = coefs[source, 13:15, :]
        turned = roll(rows, 64)
        first = lanes_of(rows) < 64
        for part in range(2):
            line = 2 * source + part
            value = jnp.where(first, rows, turned) if part == 0 else jnp.where(first, turned, rows)
            link, main = value[0:1], value[1:2]
            right = got[source, 4 * part : 4 * part + 4, :]
            solved[line, 4:8, :] = right
            if line == 0:
                scale = 1.0 / main
                update = scale * right
            else:
                scale = 1.0 / (main - previous_link * previous_factor)
                update = scale * (right + previous_link * previous)
            previous, previous_factor, previous_link = update, link * scale, link
            solved[line, 0:4, :] = update
            factors.append(previous_factor)
    for line in range(lines - 2, -1, -1):
        previous = solved[line, 0:4, :] + factors[line] * previous
        solved[line, 0:4, :] = previous
    packed = jnp.zeros((8, 128), jnp.float32)
    for place in range(8):
        line = 2 * at_y - 3 + place
        valid = (line >= 0) & (line < lines)
        value = solved[jnp.clip(line, 0, lines - 1)]
        packed = packed + jnp.where(spot_of(value, place) & valid, value, 0.0)
    for target in range(send_out.shape[0]):
        send_out[target, 0:8, :] = packed
        send_out[target, 8:16, :] = strips[(at_x >= target).astype(jnp.int32)]


def up_kernel(
    got, coefs, r1, left, mid, right, sums, fine_far, middle_far, basis_far,
    pre_out, send_out, fine, middle, vmat, fine_done, middle_done, basis_done,
):
    middle_copy = pltpu.make_async_copy(middle_far, middle, middle_done)
    fine_copy = pltpu.make_async_copy(fine_far, fine, fine_done)
    basis_copy = pltpu.make_async_copy(basis_far, vmat, basis_done)
    middle_copy.start()
    fine_copy.start()
    basis_copy.start()
    at_x = lax.axis_index("gx")
    count = got.shape[0]
    error, source, links = {}, {}, {}
    for step in range(-3, 4):
        index = at_x + step
        valid = ((index >= 0) & (index < count)).astype(jnp.float32)
        kept = jnp.clip(index, 0, count - 1)
        rows = got[kept, 0:8, :] * valid
        error[step] = padded(rows[0:4])
        source[step] = padded(rows[4:8])
        near = coefs[kept] * valid
        links[step] = jnp.concatenate([unpacked_row(near, 0), near[13:16]], axis=0)
    lane = lanes_of(error[0])
    spot = lane % 4
    for reach in range(SWEEPS - 2, -1, -1):
        updated = dict(error)
        for step in range(-1 - reach, 2 + reach):
            here = error[step]
            sx, sy, sz, dg = (links[step][kind : kind + 1] for kind in range(4))
            up = jnp.where(spot < 3, roll(here, -1), roll(here, -61))
            flux = sy * here
            down = jnp.where(spot > 0, roll(flux, 1), roll(flux, 61))
            value = dg * here - sx * error[step + 1] - links[step - 1][0:1] * error[step - 1]
            value = value - sy * up - down - sz * roll(here, -4) - roll(sz * here, 4)
            updated[step] = here + relax_weight(dg) * (source[step] - value)
        error = updated
    blank = jnp.zeros((8, 128), jnp.float32)
    coarse = {}
    for step in range(-1, 2):
        tiles = []
        for place in range(2, 6):
            value = jnp.where(spot_of(error[step], place), error[step], 0.0)
            value = quad_z(pair_z(value))
            value = value + roll(value, 64)
            tiles += [value, value]
        coarse[step] = jnp.concatenate([blank] + tiles + [blank], axis=1)

    def strip(step):
        index = at_x + step
        valid = ((index >= 0) & (index < count)).astype(jnp.float32)
        rows = got[jnp.clip(index, 0, count - 1), 8:16, :] * valid
        tiles = []
        for group in range(2):
            part = padded(rows[4 * group : 4 * group + 4])
            for place in range(4):
                at = (lane // 64 == place // 2) & (lane % 2 == place % 2)
                value = pair_z(jnp.where(at, part, 0.0))
                tiles.append(value + roll(value, 64))
        return jnp.concatenate([blank] + tiles + [blank], axis=1)

    middle_copy.wait()
    error1, source1 = {0: strip(-1) + coarse[-1], 5: strip(1) + coarse[1]}, {}
    for plane in range(1, 5):
        source1[plane] = padded(r1[plane - 1])
        weight = middle[4, 2 * plane : 2 * plane + 1, :]
        error1[plane] = weight * source1[plane] + coarse[plane // 2 - 1]
    final1 = {}
    for plane in range(1, 5):
        weight = middle[4, 2 * plane : 2 * plane + 1, :]
        final1[plane] = error1[plane] + weight * (
            source1[plane] - middle_image(error1, middle, plane)
        )
    fine_copy.wait()
    source0 = planes_of(left, mid, right, 2, 10)
    error0 = {
        at: fine[4, at : at + 1, :] * source0[at] + final1[at // 2] for at in range(2, 10)
    }
    final0 = {}
    for at in range(3, 9):
        weight = fine[4, at : at + 1, :]
        final0[at] = error0[at] + weight * (source0[at] - fine_image(error0, fine, at))
    basis_copy.wait()
    both = jnp.zeros((8, ROWS), jnp.float32)
    for at in range(4):
        own = slice(OWN, OWN + 512)
        value = final0[4 + at][0:4, own]
        pre_out[at] = value
        vmat[at, BASIS:ROWS, :] = value
        value = jnp.concatenate([value, fine_image(final0, fine, 4 + at)[0:4, own]], axis=0)
        both = both + dot_nt(value, vmat[at])
    now = jnp.concatenate([both, jnp.zeros((8, 128 - ROWS), jnp.float32)], axis=1)
    for target in range(send_out.shape[0]):
        send_out[target, 0:8, :] = now
        send_out[target, 8:16, :] = sums[...]


def eliminate(matrix, steps):
    row = lax.broadcasted_iota(jnp.int32, matrix.shape, 0)
    for step in range(steps):
        pivot = matrix[step : step + 1, :] / matrix[step : step + 1, step : step + 1]
        column = matrix[:, step : step + 1]
        matrix = matrix - jnp.where(row > step, column, 0.0) * pivot
    diagonal = jnp.where(lanes_of(matrix) == row, matrix, 0.0)
    diagonal = jnp.sum(diagonal, axis=1, keepdims=True)
    scale = lax.rsqrt(jnp.where(row[:, 0:1] < steps, diagonal, 1.0))
    return matrix * scale


def ritz_kernel(
    cells, got, gathered, used, pre, basis_far, modes_out, dirs_out, ritz_out, corr_out,
    gram, field, basis_done,
):
    basis_copy = pltpu.make_async_copy(basis_far, field, basis_done)
    basis_copy.start()
    total = got[0]
    for source in range(1, got.shape[0]):
        total = total + got[source]
    total = total / cells
    gram[80:128, :] = jnp.zeros((48, 128), jnp.float32)
    for source in range(16):
        gram[5 * source : 5 * source + 5, :] = gathered[source, 0:5, :]
    gram = gram[...] / cells
    shape = (16, 128)
    row = lax.broadcasted_iota(jnp.int32, shape, 0)
    lane = lax.broadcasted_iota(jnp.int32, shape, 1)
    zero4 = jnp.zeros((4, 128), jnp.float32)
    corr = jnp.where(used[0:4, :] > 0, total[0:4], 0.0)
    corr_out[...] = roll(corr, -8)[:, 0:LOCKED]
    locked_part = jnp.concatenate([zero4, -corr, zero4, zero4], axis=0)
    ones = ((row < 4) & (lane == row)) | ((row >= 8) & (row < 12) & (lane == row - 4))
    pre_ones = (row >= 4) & (row < 8) & (lane == row + 64)
    on_basis = jnp.where(ones, 1.0, locked_part)
    weights = jnp.where(pre_ones, 1.0, on_basis)
    pre_lane = (lane >= 68) & (lane < 72)

    def from_pre(part):
        rows4 = jnp.concatenate([zero4, part, zero4, zero4], axis=0)
        rows4 = jnp.where(lane < 72, rows4, 0.0)
        return jnp.where(pre_lane, 0.5 * rows4, rows4)

    first = jnp.where(lane < 68, dot_nn(on_basis, gram), 0.0)
    side = from_pre(total[0:4])
    mass = dot_nt(first, on_basis) + dot_nt(side, weights) + dot_nt(weights, side)
    second = jnp.where(lane >= 68, dot_nn(locked_part, gram), 0.0)
    pair = gram[72:80]
    pair = jnp.concatenate([pair[0:4], zero4, pair[4:8], zero4], axis=0)
    pair = jnp.where(lane < 68, jnp.where(lane < 8, 0.5 * pair, pair), 0.0)
    side = from_pre(total[4:8])
    stiff = dot_nt(second, roll(locked_part, 60))
    stiff = stiff + dot_nt(pair, on_basis) + dot_nt(on_basis, pair)
    stiff = stiff + dot_nt(side, weights) + dot_nt(weights, side)
    eye = jnp.where((row < 12) & (lane == row + 64), 1.0, 0.0)
    wide = jnp.zeros((16, 112), jnp.float32)
    mass = jnp.concatenate([mass, wide], axis=1)
    stiff = jnp.concatenate([stiff, wide], axis=1)
    done = eliminate(mass + roll(stiff, 32) + eye, 12)
    inside = (row < 12) & (lane < 12)
    half = jnp.where(inside, roll(done, -32), 0.0)
    inverse = jnp.where(inside, roll(done, -64), 0.0)
    reduced = dot_nt(half, inverse) + dot_nt(inverse, half)
    reduced = 0.5 * jnp.concatenate([reduced, wide], axis=1)
    top = jnp.sum(jnp.where(lane == row, reduced, 0.0), axis=(0, 1), keepdims=True)
    square = jnp.concatenate([reduced, jnp.zeros((112, 128), jnp.float32)], axis=0)
    row8 = lax.broadcasted_iota(jnp.int32, (8, 128), 0)
    lane8 = lax.broadcasted_iota(jnp.int32, (8, 128), 1)
    first4 = row8 < 4
    basis_q = jnp.where(first4 & (lane8 == row8), 1.0, 0.0)
    for step in range(RITZ):
        raised = top * basis_q - dot_nn(basis_q, square)
        products = dot_nt(raised, raised)
        products = jnp.concatenate([products, jnp.zeros((8, 120), jnp.float32)], axis=1)
        joint = products + roll(raised, 32)
        basis_q = jnp.where(first4 & (lane8 < 12), roll(eliminate(joint, 4), -32), 0.0)
    ritz = jnp.sum(basis_q * dot_nn(basis_q, square), axis=1, keepdims=True)
    for part in range(ACTIVE):
        ritz_out[part] = ritz[part, 0]
    tall = jnp.concatenate([inverse, jnp.zeros((112, 128), jnp.float32)], axis=0)
    coefs = dot_nn(basis_q, tall)
    tail = jnp.where(lane8 >= 4, coefs, 0.0)
    both = jnp.concatenate([coefs[0:4], tail[0:4]], axis=0)
    weights = jnp.concatenate([weights, jnp.zeros((112, 128), jnp.float32)], axis=0)
    mix = dot_nn(both, weights)[:, 0:ROWS]
    basis_copy.wait()
    for at in range(4):
        field[at, BASIS:ROWS, :] = pre[at]
        value = dot_nn(mix, field[at])
        for part in range(4):
            modes_out[part, at : at + 1, :] = value[part : part + 1]
            dirs_out[part, at : at + 1, :] = value[4 + part : 5 + part]


def pair_shift(low, high, axis):
    count = lax.axis_size(axis)
    forward = [(at, at + 1) for at in range(count - 1)]
    backward = [(at + 1, at) for at in range(count - 1)]
    return lax.ppermute(high, axis, forward), lax.ppermute(low, axis, backward)


def spread(block, axis):
    count = lax.axis_size(axis)
    return lax.all_to_all(jnp.broadcast_to(block, (count,) + block.shape), axis, 0, 0)


def on_device(modes, directions, locked, perm_class, perm_table, locked_count):
    size_x, size_y = lax.axis_size("gx"), lax.axis_size("gy")
    lines = 2 * size_y
    cells = float(4 * 512 * size_x * size_y)
    classes = jnp.arange(perm_table.shape[0], dtype=jnp.int32)
    conduct = jnp.sum(
        jnp.where(perm_class[None] == classes[:, None, None], perm_table[:, None, None], 0.0),
        axis=0,
    )
    basis = jnp.concatenate([modes, directions, locked, jnp.zeros((4, 4, 512), jnp.float32)], 0)
    basis = jnp.transpose(basis, (1, 0, 2))

    def edge(field, cond):
        field = jnp.concatenate([field[:2, :BASIS], field[2:, :BASIS]], axis=2)
        return jnp.concatenate([field, cond.reshape(2, 6, 128)], axis=1)

    low, high = pair_shift(
        edge(basis[:, :, :64], conduct[:, :384]), edge(basis[:, :, 448:], conduct[:, 128:]), "gy"
    )
    cond_low = low[:, BASIS:].reshape(4, 384)
    cond_high = high[:, BASIS:].reshape(4, 384)
    conduct = jnp.concatenate([cond_low, conduct, cond_high], axis=1)
    rows = jnp.pad(conduct.reshape(10, 512), ((0, 2), (0, 0)))
    left, right = pair_shift(
        jnp.concatenate([basis[0, :BASIS], rows], 0),
        jnp.concatenate([basis[3, :BASIS], rows], 0),
        "gx",
    )
    cond_left = left[68:78].reshape(4, WIDE)
    cond_right = right[68:78].reshape(4, WIDE)
    fine, middle, image, used, send = kernel_call(
        functools.partial(coef_kernel, 4.0 / float(lines * lines)),
        [(5, 16, WIDE), (5, 16, WIDE), (4, 8, 512), (8, 128), (size_y, 16, 128)],
        locked_count, cond_left, conduct, cond_right, basis, left[:ROWS], right[:ROWS], low, high,
        scratch=[(16, WIDE), (128, 512), (80, 512), (5, 16, WIDE), (5, 16, WIDE)],
        scalars=1, far_out=(0, 1),
    )
    got_y = lax.all_to_all(send, "gy", 0, 0)
    (send,) = kernel_call(
        functools.partial(middle_kernel, lines), [(size_x, 16, 128)], got_y
    )
    got_x = lax.all_to_all(send, "gx", 0, 0)
    residual, res_low, res_high, sums = kernel_call(
        functools.partial(residual_kernel, cells),
        [(4, 4, 512), (4, 4, 384), (4, 4, 384), (8, 128)],
        got_x, used, basis, image,
    )
    low, high = pair_shift(res_low, res_high, "gy")
    mid = jnp.concatenate([low, residual, high], axis=2)
    left, right = pair_shift(mid, mid, "gx")
    r1, send, strips = kernel_call(
        down_kernel, [(4, 4, WIDE), (size_y, 8, 128), (2, 8, 128)], left, mid, right, fine, middle
    )
    (send,) = kernel_call(
        functools.partial(line_kernel, lines), [(size_x, 16, 128)],
        lax.all_to_all(send, "gy", 0, 0), got_y, strips,
        scratch=[(lines, 8, 128)],
    )
    precond, send = kernel_call(
        up_kernel, [(4, 4, 512), (size_y, 16, 128)],
        lax.all_to_all(send, "gx", 0, 0), got_x, r1, left, mid, right, sums, fine, middle, basis,
        scratch=[(5, 16, WIDE), (5, 16, WIDE), (4, ROWS, 512)], far=(7, 8, 9),
    )
    got_y = lax.all_to_all(send, "gy", 0, 0)
    got_x = spread(jnp.sum(got_y[:, :8], axis=0), "gx")
    new_modes, new_directions, ritz, corr = kernel_call(
        functools.partial(ritz_kernel, cells),
        [(4, 4, 512), (4, 4, 512), (4,), (4, LOCKED)],
        got_x, got_y[:, 8:], used, precond, basis,
        scratch=[(128, 128), (4, ROWS, 512)], far=(4,), results=True,
    )
    return (new_modes, new_directions, ritz, corr.T)


def solution(mesh):
    placed = (
        P(None, "gx", "gy"),
        P(None, "gx", "gy"),
        P(None, "gx", "gy"),
        P("gx", "gy"),
        P(),
        P(),
    )
    return jax.shard_map(
        on_device,
        mesh=mesh,
        in_specs=placed,
        out_specs=(P(None, "gx", "gy"), P(None, "gx", "gy"), P(), P()),
        check_vma=False,
    )
```

```python
import functools

import jax
import jax.numpy as jnp
from jax import lax
from jax.experimental import pallas as pl
from jax.experimental.pallas import tpu as pltpu
from jax.sharding import PartitionSpec as P

NZ = 64
ACTIVE = 4
LOCKED = 60
BASIS = 68
ROWS = 72
SWEEPS = 3
RITZ = 3
OMEGA = 0.6
EPSILON = 1e-06
PRECISE = lax.Precision.HIGHEST
WIDE = 1280
OWN = 384
INTERPRET = False


def kernel_call(
    body, out, *args, scratch=(), scalars=0, far=(), far_out=(), inputs=False, results=False
):
    specs, placed = [], []
    for at, value in enumerate(args):
        space = pltpu.SMEM if at < scalars else pl.ANY if at in far else pltpu.VMEM
        specs.append(pl.BlockSpec(memory_space=space))
        if space is pltpu.VMEM and not (inputs or INTERPRET):
            value = pltpu.with_memory_space_constraint(value, pltpu.VMEM)
        placed.append(value)
    shapes, stored = [], []
    for at, shape in enumerate(out):
        space = pltpu.SMEM if len(shape) == 1 else pl.ANY if at in far_out else pltpu.VMEM
        stored.append(pl.BlockSpec(memory_space=space))
        if space is pltpu.VMEM and not (results or INTERPRET):
            shapes.append(pltpu.VMEM(shape, jnp.float32))
        else:
            shapes.append(jax.ShapeDtypeStruct(shape, jnp.float32))
    copies = len(far) + len(far_out)
    held = [pltpu.VMEM(shape, jnp.float32) for shape in scratch]
    held += [pltpu.SemaphoreType.DMA] * copies
    return pl.pallas_call(
        body,
        out_shape=shapes,
        in_specs=specs,
        out_specs=stored,
        scratch_shapes=held,
        interpret=INTERPRET,
    )(*placed)


def roll(value, shift, axis=1):
    return pltpu.roll(value, shift % value.shape[axis], axis)


def lanes_of(value):
    return lax.broadcasted_iota(jnp.int32, value.shape, 1)


def pair_z(value):
    even = lanes_of(value) % 2 == 0
    return value + jnp.where(even, roll(value, -1), roll(value, 1))


def pair_y(value):
    first = lanes_of(value) % 128 < 64
    return value + jnp.where(first, roll(value, -64), roll(value, 64))


def quad_z(value):
    first = lanes_of(value) % 4 < 2
    return value + jnp.where(first, roll(value, -2), roll(value, 2))


def quad_y(value):
    odd = (lanes_of(value) // 128) % 2 == 1
    return value + jnp.where(odd, roll(value, -128), roll(value, 128))


def dot_nt(left, right):
    return lax.dot_general(
        left, right, (((1,), (1,)), ((), ())), precision=PRECISE, preferred_element_type=jnp.float32
    )


def dot_nn(left, right):
    return lax.dot_general(
        left, right, (((1,), (0,)), ((), ())), precision=PRECISE, preferred_element_type=jnp.float32
    )


def relax_weight(diagonal):
    inside = diagonal > 0
    return jnp.where(inside, OMEGA / jnp.where(inside, diagonal, 1.0), 0.0)


def joined(here, there):
    both = (here > 0) & (there > 0)
    return jnp.where(both, 2.0 * here * there / jnp.where(both, here + there, 1.0), 0.0)


def face(coupling, here, there):
    return coupling + jnp.where(there > 0, 0.0, 2.0 * here)


def input_kernel(table, modes, directions, locked, kinds, basis, conduct, low_out, high_out):
    value = jnp.zeros((4, 512), jnp.float32)
    kind = kinds[...]
    for at in range(table.shape[0]):
        value = jnp.where(kind == at, table[at], value)
    conduct[...] = value
    for at in range(4):
        basis[at, 0:4, :] = modes[:, at, :]
        basis[at, 4:8, :] = directions[:, at, :]
        basis[at, 8:BASIS, :] = locked[:, at, :]
        basis[at, BASIS:ROWS, :] = jnp.zeros((ROWS - BASIS, 512), jnp.float32)
    first = lax.broadcasted_iota(jnp.int32, (ROWS, 128), 1) < 64
    for at in range(2):
        near, far = basis[at, :, 0:128], basis[at + 2, :, 0:128]
        low_out[at, 0:ROWS, :] = jnp.where(first, near, roll(far, 64))
        near, far = basis[at, 0:8, 384:512], basis[at + 2, 0:8, 384:512]
        high_out[at, 0:8, :] = jnp.where(first[0:8], roll(near, 64), far)
        for part in range(6):
            row, lane = 2 * at + part // 3, 128 * (part % 3)
            low_out[at, BASIS + part : BASIS + part + 1, :] = value[row : row + 1, lane : lane + 128]
            lane += 128
            high_out[at, 8 + part : 9 + part, :] = value[row : row + 1, lane : lane + 128]


def coef_kernel(
    shift, count, cond_left, cond_mid, cond_right, basis, left, right, low, high,
    fine_far, middle_far, image_out, used_out, send_out, cond, vmat, umat, fine_out, middle_out,
    fine_done, middle_done,
):
    used = lanes_of(used_out)
    used_out[...] = jnp.where((used >= 8) & (used < 8 + count[0]), 1.0, 0.0)
    cond[0:4, :] = cond_left[...]
    cond[4:8, :] = cond_mid[...]
    cond[8:12, :] = cond_right[...]
    cond[12:16, :] = jnp.zeros((4, WIDE), jnp.float32)
    here = cond[...]
    z_at = lanes_of(here) % 64
    x_next, x_prev = roll(here, -1, 0), roll(here, 1, 0)
    y_next, y_prev = roll(here, -64), roll(here, 64)
    z_next = jnp.where(z_at < 63, roll(here, -1), 0.0)
    z_prev = jnp.where(z_at > 0, roll(here, 1), 0.0)
    tx, ty, tz = joined(here, x_next), joined(here, y_next), joined(here, z_next)
    y_faces = face(ty, here, y_next) + face(roll(ty, 64), here, y_prev)
    diagonal = face(tx, here, x_next) + face(roll(tx, 1, 0), here, x_prev) + y_faces
    diagonal = diagonal + face(tz, here, z_next) + face(roll(tz, 1), here, z_prev)
    for at, value in enumerate((diagonal, tx, ty, tz, relax_weight(diagonal))):
        fine_out[at] = value

    def pairs(value):
        return pair_y(pair_z(value))

    def pair_x(value):
        return value + roll(value, -1, 0)

    upper_y = lanes_of(here) % 128 >= 64
    sum_x = pairs(tx)
    odd_y = pair_x(pairs(jnp.where(upper_y, ty, 0.0)))
    odd_z = pair_x(pairs(jnp.where(z_at % 2 == 1, tz, 0.0)))
    even_y = pair_x(pairs(jnp.where(upper_y, 0.0, ty)))
    even_z = pair_x(pairs(jnp.where(z_at % 2 == 1, 0.0, tz)))
    tx1, ty1, tz1 = roll(sum_x, -1, 0), odd_y, odd_z
    diagonal1 = pair_x(pairs(diagonal)) - 2.0 * (sum_x + even_y + even_z)
    y_faces1 = pair_x(pairs(y_faces)) - 2.0 * even_y
    for at, value in enumerate((diagonal1, tx1, ty1, tz1, relax_weight(diagonal1))):
        middle_out[at] = value
    fine_copy = pltpu.make_async_copy(fine_out, fine_far, fine_done)
    middle_copy = pltpu.make_async_copy(middle_out, middle_far, middle_done)
    fine_copy.start()
    middle_copy.start()

    def quads(value):
        return quad_y(quad_z(value))

    def both_rows(value):
        return value + roll(value, -2, 0)

    upper_tile = (lanes_of(here) // 128) % 2 == 0
    sum_x1 = quads(tx1)
    ty2 = both_rows(quads(jnp.where(upper_tile, ty1, 0.0)))
    tz2 = both_rows(quads(jnp.where(z_at % 4 >= 2, tz1, 0.0)))
    inner_y = both_rows(quads(jnp.where(upper_tile, 0.0, ty1)))
    inner_z = both_rows(quads(jnp.where(z_at % 4 >= 2, 0.0, tz1)))
    tx2 = roll(sum_x1, -2, 0)
    diagonal2 = both_rows(quads(diagonal1)) - 2.0 * (sum_x1 + inner_y + inner_z)
    y_faces2 = both_rows(quads(y_faces1)) - 2.0 * inner_y
    line2 = y_faces2 + shift * (diagonal2 - y_faces2)
    coarse = []
    for value in (tx2, ty2, tz2, diagonal2, line2):
        first, second = value[4:5, 384:512], value[4:5, 640:768]
        coarse.append(jnp.where(lanes_of(first) < 64, first, second))

    gram = jnp.zeros((80, 128), jnp.float32)
    for at in range(4):
        plane = 4 + at
        row = slice(plane, plane + 1)
        below, above = low[at % 2, 0:8, :], high[at % 2, 0:ROWS, :]
        below = roll(below, 64) if at < 2 else below
        above = above if at < 2 else roll(above, 64)
        after = right[...] if at == 3 else basis[at + 1]
        before = left[0:8, :] if at == 0 else basis[at - 1, 0:8, :]
        wide = jnp.concatenate([below, basis[at, 0:8, :], above[0:8]], axis=1)
        dg, sx, sy, sz = (fine_out[kind, row, 256:1024] for kind in range(4))
        image = dg * wide - sy * roll(wide, -64) - roll(sy * wide, 64)
        image = (image - sz * roll(wide, -1) - roll(sz * wide, 1))[:, 128:640]
        image = image - sx[:, 128:640] * after[0:8]
        image = image - fine_out[1, plane - 1 : plane, OWN : OWN + 512] * before
        image_out[at] = image
        wide = jnp.concatenate([basis[at, 8:ROWS, :], above[8:ROWS]], axis=1)
        dg, sx, sy, sz = (fine_out[kind, row, OWN:1024] for kind in range(4))
        half = (0.5 * dg) * wide - sy * roll(wide, -64) - sz * roll(wide, -1)
        half = half[:, 0:512] - sx[:, 0:512] * after[8:ROWS]
        vmat[0:72, :] = basis[at]
        vmat[68:128, :] = half[0:60]
        umat[0:72, :] = basis[at]
        umat[72:80, :] = image
        gram = gram + dot_nt(umat[...], vmat[...])
    now = packed_rows(jnp.concatenate([gram[0:4], gram[72:76]], axis=0), [coarse[0], coarse[2]])
    rest = jnp.concatenate([coarse[1], coarse[4], coarse[3]], axis=0)
    for target in range(send_out.shape[0]):
        send_out[target, 0:8, :] = now
        send_out[target, 8:13, :] = gram[5 * target : 5 * target + 5]
        send_out[target, 13:16, :] = rest
    fine_copy.wait()
    middle_copy.wait()


def packed_rows(rows, extra):
    lane = lanes_of(rows)
    row = lax.broadcasted_iota(jnp.int32, rows.shape, 0)
    for at, value in enumerate(extra):
        for part in range(4):
            moved = roll(value, 96 - 32 * part)
            rows = jnp.where((row == 4 * at + part) & (lane >= 96), moved, rows)
    return rows


def unpacked_row(rows, at):
    lane = lanes_of(rows[0:1])
    value = roll(rows[4 * at : 4 * at + 1], -96)
    for part in range(1, 4):
        moved = roll(rows[4 * at + part : 4 * at + part + 1], 32 * part - 96)
        value = jnp.where(lane // 32 == part, moved, value)
    return value


def half_of(value, half, wanted):
    return value if half == wanted else roll(value, 64)


def spot_of(value, place):
    lane = lanes_of(value)
    return (lane // 64 == place // 4) & (lane % 4 == place % 4)


def middle_kernel(lines, got, send_out):
    at_y = lax.axis_index("gy")
    total = got[0]
    for source in range(1, got.shape[0]):
        total = total + got[source]
    packed = jnp.zeros((4, 128), jnp.float32)
    for place in range(8):
        source = at_y + (place - 3) // 2
        valid = (source >= 0) & (source < lines // 2)
        value = got[jnp.clip(source, 0, lines // 2 - 1)]
        tx, tz = unpacked_row(value, 0), unpacked_row(value, 1)
        value = jnp.concatenate([tx, value[13:14], tz, value[15:16]], axis=0)
        value = half_of(value, (place - 3) % 2, place // 4)
        packed = packed + jnp.where(spot_of(value, place) & valid, value, 0.0)
    now = packed_rows(total[0:8], [packed[0:1]])
    for target in range(send_out.shape[0]):
        send_out[target, 0:8, :] = now
        send_out[target, 8:13, :] = total[8:13]
        send_out[target, 13:16, :] = packed[1:4]


def residual_kernel(cells, got, used, basis, image, res_out, low_out, high_out, sums_out):
    total = got[0]
    for source in range(1, got.shape[0]):
        total = total + got[source]
    sums_out[...] = total[8:16]
    overlap, energy = total[0:4], total[4:8]
    lane = lanes_of(overlap)
    own = lane == lax.broadcasted_iota(jnp.int32, overlap.shape, 0)
    norm = jnp.sum(jnp.where(own, overlap, 0.0), axis=1, keepdims=True)
    top = jnp.sum(jnp.where(own, energy, 0.0), axis=1, keepdims=True)
    quotient = top / cells / (norm / cells + EPSILON)
    coupling = (energy - quotient * overlap) / cells
    weights = jnp.where(used[0:4, :] > 0, coupling, 0.0)
    weights = jnp.concatenate([weights, jnp.zeros((4, 128), jnp.float32)], axis=0)
    for at in range(4):
        field = basis[at]
        value = image[at][0:4] - quotient * field[0:4]
        value = value - dot_nn(weights[:, 0:ROWS], field)[0:4]
        res_out[at] = value
        low_out[at] = value[:, 0:384]
        high_out[at] = value[:, 128:512]


def padded(value):
    return jnp.concatenate([value, jnp.zeros(value.shape, jnp.float32)], axis=0)


def apply_at(values, coefs, row, row_step, at, y_step, z_step, keys):
    here = values[at]
    dg, sx, sy, sz = (coefs[kind, row : row + 1, :] for kind in range(4))
    before = coefs[1, row - row_step : row - row_step + 1, :]
    image = dg * here - sx * values[at + 1] - before * values[at - 1]
    image = image - sy * roll(here, -y_step) - roll(sy * here, y_step)
    return image - sz * roll(here, -z_step) - roll(sz * here, z_step)


def fine_image(values, fine, plane):
    return apply_at(values, fine, plane, 1, plane, 64, 1, None)


def middle_image(values, middle, plane):
    return apply_at(values, middle, 2 * plane, 2, plane, 128, 2, None)


def planes_of(left, mid, right, first, last):
    parts = (left, mid, right)
    return {at: padded(parts[at // 4][at % 4]) for at in range(first, last)}


def down_kernel(left, mid, right, fine, middle, r1_out, send_out, strip_out):
    source = planes_of(left, mid, right, 1, 11)
    error = {at: fine[4, at : at + 1, :] * source[at] for at in range(1, 11)}
    rest = {at: source[at] - fine_image(error, fine, at) for at in range(2, 10)}
    source1, error1 = {}, {}
    for plane in range(1, 5):
        value = pair_y(pair_z(rest[2 * plane] + rest[2 * plane + 1]))
        source1[plane] = value
        r1_out[plane - 1] = value[0:4]
        error1[plane] = middle[4, 2 * plane : 2 * plane + 1, :] * value
    low = sum(source1[plane] - middle_image(error1, middle, plane) for plane in (2, 3))
    low = quad_y(quad_z(low))
    both = jnp.concatenate([low[0:4, 384:512], low[0:4, 640:768]], axis=0)
    for target in range(send_out.shape[0]):
        send_out[target] = both
    for at in range(2):
        tiles = [error1[2 + at][0:4, 128 * t : 128 * t + 128] for t in range(1, 9)]
        lane = lanes_of(tiles[0])
        half, odd = lane // 64, lane % 2
        for group in range(2):
            a, b, c, d = tiles[4 * group : 4 * group + 4]
            value = jnp.where(half == 0, jnp.where(odd == 0, a, b), jnp.where(odd == 0, c, d))
            strip_out[at, 4 * group : 4 * group + 4, :] = value


def line_kernel(lines, got, coefs, strips, send_out, solved):
    at_x, at_y = lax.axis_index("gx"), lax.axis_index("gy")
    factors, previous, previous_factor, previous_link = [], None, None, None
    for source in range(lines // 2):
        rows = coefs[source, 13:15, :]
        turned = roll(rows, 64)
        first = lanes_of(rows) < 64
        for part in range(2):
            line = 2 * source + part
            value = jnp.where(first, rows, turned) if part == 0 else jnp.where(first, turned, rows)
            link, main = value[0:1], value[1:2]
            right = got[source, 4 * part : 4 * part + 4, :]
            solved[line, 4:8, :] = right
            if line == 0:
                scale = 1.0 / main
                update = scale * right
            else:
                scale = 1.0 / (main - previous_link * previous_factor)
                update = scale * (right + previous_link * previous)
            previous, previous_factor, previous_link = update, link * scale, link
            solved[line, 0:4, :] = update
            factors.append(previous_factor)
    for line in range(lines - 2, -1, -1):
        previous = solved[line, 0:4, :] + factors[line] * previous
        solved[line, 0:4, :] = previous
    packed = jnp.zeros((8, 128), jnp.float32)
    for place in range(8):
        line = 2 * at_y - 3 + place
        valid = (line >= 0) & (line < lines)
        value = solved[jnp.clip(line, 0, lines - 1)]
        packed = packed + jnp.where(spot_of(value, place) & valid, value, 0.0)
    for target in range(send_out.shape[0]):
        send_out[target, 0:8, :] = packed
        send_out[target, 8:16, :] = strips[(at_x >= target).astype(jnp.int32)]


def up_kernel(
    got, coefs, r1, left, mid, right, sums, fine_far, middle_far, basis_far,
    pre_out, send_out, fine, middle, vmat, fine_done, middle_done, basis_done,
):
    middle_copy = pltpu.make_async_copy(middle_far, middle, middle_done)
    fine_copy = pltpu.make_async_copy(fine_far, fine, fine_done)
    basis_copy = pltpu.make_async_copy(basis_far, vmat, basis_done)
    middle_copy.start()
    fine_copy.start()
    basis_copy.start()
    at_x = lax.axis_index("gx")
    count = got.shape[0]
    error, source, links = {}, {}, {}
    for step in range(-3, 4):
        index = at_x + step
        valid = ((index >= 0) & (index < count)).astype(jnp.float32)
        kept = jnp.clip(index, 0, count - 1)
        rows = got[kept, 0:8, :] * valid
        error[step] = padded(rows[0:4])
        source[step] = padded(rows[4:8])
        near = coefs[kept] * valid
        links[step] = jnp.concatenate([unpacked_row(near, 0), near[13:16]], axis=0)
    lane = lanes_of(error[0])
    spot = lane % 4
    for reach in range(SWEEPS - 2, -1, -1):
        updated = dict(error)
        for step in range(-1 - reach, 2 + reach):
            here = error[step]
            sx, sy, sz, dg = (links[step][kind : kind + 1] for kind in range(4))
            up = jnp.where(spot < 3, roll(here, -1), roll(here, -61))
            flux = sy * here
            down = jnp.where(spot > 0, roll(flux, 1), roll(flux, 61))
            value = dg * here - sx * error[step + 1] - links[step - 1][0:1] * error[step - 1]
            value = value - sy * up - down - sz * roll(here, -4) - roll(sz * here, 4)
            updated[step] = here + relax_weight(dg) * (source[step] - value)
        error = updated
    blank = jnp.zeros((8, 128), jnp.float32)
    coarse = {}
    for step in range(-1, 2):
        tiles = []
        for place in range(2, 6):
            value = jnp.where(spot_of(error[step], place), error[step], 0.0)
            value = quad_z(pair_z(value))
            value = value + roll(value, 64)
            tiles += [value, value]
        coarse[step] = jnp.concatenate([blank] + tiles + [blank], axis=1)

    def strip(step):
        index = at_x + step
        valid = ((index >= 0) & (index < count)).astype(jnp.float32)
        rows = got[jnp.clip(index, 0, count - 1), 8:16, :] * valid
        tiles = []
        for group in range(2):
            part = padded(rows[4 * group : 4 * group + 4])
            for place in range(4):
                at = (lane // 64 == place // 2) & (lane % 2 == place % 2)
                value = pair_z(jnp.where(at, part, 0.0))
                tiles.append(value + roll(value, 64))
        return jnp.concatenate([blank] + tiles + [blank], axis=1)

    middle_copy.wait()
    error1, source1 = {0: strip(-1) + coarse[-1], 5: strip(1) + coarse[1]}, {}
    for plane in range(1, 5):
        source1[plane] = padded(r1[plane - 1])
        weight = middle[4, 2 * plane : 2 * plane + 1, :]
        error1[plane] = weight * source1[plane] + coarse[plane // 2 - 1]
    final1 = {}
    for plane in range(1, 5):
        weight = middle[4, 2 * plane : 2 * plane + 1, :]
        final1[plane] = error1[plane] + weight * (
            source1[plane] - middle_image(error1, middle, plane)
        )
    fine_copy.wait()
    source0 = planes_of(left, mid, right, 2, 10)
    error0 = {
        at: fine[4, at : at + 1, :] * source0[at] + final1[at // 2] for at in range(2, 10)
    }
    final0 = {}
    for at in range(3, 9):
        weight = fine[4, at : at + 1, :]
        final0[at] = error0[at] + weight * (source0[at] - fine_image(error0, fine, at))
    basis_copy.wait()
    both = jnp.zeros((8, ROWS), jnp.float32)
    for at in range(4):
        own = slice(OWN, OWN + 512)
        value = final0[4 + at][0:4, own]
        pre_out[at] = value
        vmat[at, BASIS:ROWS, :] = value
        value = jnp.concatenate([value, fine_image(final0, fine, 4 + at)[0:4, own]], axis=0)
        both = both + dot_nt(value, vmat[at])
    now = jnp.concatenate([both, jnp.zeros((8, 128 - ROWS), jnp.float32)], axis=1)
    for target in range(send_out.shape[0]):
        send_out[target, 0:8, :] = now
        send_out[target, 8:16, :] = sums[...]


def eliminate(matrix, steps):
    row = lax.broadcasted_iota(jnp.int32, matrix.shape, 0)
    for step in range(steps):
        pivot = matrix[step : step + 1, :] / matrix[step : step + 1, step : step + 1]
        column = matrix[:, step : step + 1]
        matrix = matrix - jnp.where(row > step, column, 0.0) * pivot
    diagonal = jnp.where(lanes_of(matrix) == row, matrix, 0.0)
    diagonal = jnp.sum(diagonal, axis=1, keepdims=True)
    scale = lax.rsqrt(jnp.where(row[:, 0:1] < steps, diagonal, 1.0))
    return matrix * scale


def ritz_kernel(
    cells, got, gathered, used, pre, basis_far, modes_out, dirs_out, ritz_out, corr_out,
    gram, field, basis_done,
):
    basis_copy = pltpu.make_async_copy(basis_far, field, basis_done)
    basis_copy.start()
    total = got[0]
    for source in range(1, got.shape[0]):
        total = total + got[source]
    total = total / cells
    gram[80:128, :] = jnp.zeros((48, 128), jnp.float32)
    for source in range(16):
        gram[5 * source : 5 * source + 5, :] = gathered[source, 0:5, :]
    gram = gram[...] / cells
    shape = (16, 128)
    row = lax.broadcasted_iota(jnp.int32, shape, 0)
    lane = lax.broadcasted_iota(jnp.int32, shape, 1)
    zero4 = jnp.zeros((4, 128), jnp.float32)
    corr = jnp.where(used[0:4, :] > 0, total[0:4], 0.0)
    corr_out[...] = roll(corr, -8)[:, 0:LOCKED]
    locked_part = jnp.concatenate([zero4, -corr, zero4, zero4], axis=0)
    ones = ((row < 4) & (lane == row)) | ((row >= 8) & (row < 12) & (lane == row - 4))
    pre_ones = (row >= 4) & (row < 8) & (lane == row + 64)
    on_basis = jnp.where(ones, 1.0, locked_part)
    weights = jnp.where(pre_ones, 1.0, on_basis)
    pre_lane = (lane >= 68) & (lane < 72)

    def from_pre(part):
        rows4 = jnp.concatenate([zero4, part, zero4, zero4], axis=0)
        rows4 = jnp.where(lane < 72, rows4, 0.0)
        return jnp.where(pre_lane, 0.5 * rows4, rows4)

    products = dot_nn(jnp.concatenate([on_basis, locked_part], axis=0), gram)
    first = jnp.where(lane < 68, products[0:16], 0.0)
    second = roll(jnp.where(lane >= 68, products[16:32], 0.0), -60)
    pair = gram[72:80]
    pair = jnp.concatenate([pair[0:4], zero4, pair[4:8], zero4], axis=0)
    pair = jnp.where(lane < 68, jnp.where(lane < 8, 0.5 * pair, pair), 0.0)
    stacked = [0.5 * first + from_pre(total[0:4]), second + pair + from_pre(total[4:8])]
    stacked = jnp.concatenate(stacked, axis=0)
    straight = dot_nt(stacked, weights)
    turned = dot_nt(weights, stacked)
    mass = straight[0:16] + turned[:, 0:16]
    stiff = straight[16:32] + turned[:, 16:32]
    eye = jnp.where((row < 12) & (lane == row + 64), 1.0, 0.0)
    wide = jnp.zeros((16, 112), jnp.float32)
    mass = jnp.concatenate([mass, wide], axis=1)
    stiff = jnp.concatenate([stiff, wide], axis=1)
    done = eliminate(mass + roll(stiff, 32) + eye, 12)
    inside = (row < 12) & (lane < 12)
    half = jnp.where(inside, roll(done, -32), 0.0)
    inverse = jnp.where(inside, roll(done, -64), 0.0)
    reduced = dot_nt(half, inverse) + dot_nt(inverse, half)
    reduced = 0.5 * jnp.concatenate([reduced, wide], axis=1)
    top = jnp.sum(jnp.where(lane == row, reduced, 0.0), axis=(0, 1), keepdims=True)
    square = jnp.concatenate([reduced, jnp.zeros((112, 128), jnp.float32)], axis=0)
    row8 = lax.broadcasted_iota(jnp.int32, (8, 128), 0)
    lane8 = lax.broadcasted_iota(jnp.int32, (8, 128), 1)
    first4 = row8 < 4
    basis_q = jnp.where(first4 & (lane8 == row8), 1.0, 0.0)
    for step in range(RITZ):
        raised = top * basis_q - dot_nn(basis_q, square)
        products = dot_nt(raised, raised)
        products = jnp.concatenate([products, jnp.zeros((8, 120), jnp.float32)], axis=1)
        joint = products + roll(raised, 32)
        basis_q = jnp.where(first4 & (lane8 < 12), roll(eliminate(joint, 4), -32), 0.0)
    ritz = jnp.sum(basis_q * dot_nn(basis_q, square), axis=1, keepdims=True)
    for part in range(ACTIVE):
        ritz_out[part] = ritz[part, 0]
    tall = jnp.concatenate([inverse, jnp.zeros((112, 128), jnp.float32)], axis=0)
    coefs = dot_nn(basis_q, tall)
    tail = jnp.where(lane8 >= 4, coefs, 0.0)
    both = jnp.concatenate([coefs[0:4], tail[0:4]], axis=0)
    weights = jnp.concatenate([weights, jnp.zeros((112, 128), jnp.float32)], axis=0)
    mix = dot_nn(both, weights)[:, 0:ROWS]
    basis_copy.wait()
    for at in range(4):
        field[at, BASIS:ROWS, :] = pre[at]
        value = dot_nn(mix, field[at])
        for part in range(4):
            modes_out[part, at : at + 1, :] = value[part : part + 1]
            dirs_out[part, at : at + 1, :] = value[4 + part : 5 + part]


def pair_shift(low, high, axis):
    count = lax.axis_size(axis)
    forward = [(at, at + 1) for at in range(count - 1)]
    backward = [(at + 1, at) for at in range(count - 1)]
    return lax.ppermute(high, axis, forward), lax.ppermute(low, axis, backward)


def spread(block, axis):
    count = lax.axis_size(axis)
    return lax.all_to_all(jnp.broadcast_to(block, (count,) + block.shape), axis, 0, 0)


def on_device(modes, directions, locked, perm_class, perm_table, locked_count):
    size_x, size_y = lax.axis_size("gx"), lax.axis_size("gy")
    lines = 2 * size_y
    cells = float(4 * 512 * size_x * size_y)
    basis, conduct, low, high = kernel_call(
        input_kernel, [(4, ROWS, 512), (4, 512), (2, BASIS + 6, 128), (2, 14, 128)],
        perm_table, modes, directions, locked, perm_class, scalars=1, inputs=True,
    )
    low, high = pair_shift(low, high, "gy")
    cond_low = low[:, 8:].reshape(4, 384)
    cond_high = high[:, BASIS:].reshape(4, 384)
    conduct = jnp.concatenate([cond_low, conduct, cond_high], axis=1)
    rows = conduct.reshape(10, 512)
    left, right = pair_shift(
        jnp.concatenate([basis[0, :BASIS], rows, jnp.zeros((2, 512), jnp.float32)], 0),
        jnp.concatenate([basis[3, :8], rows, jnp.zeros((6, 512), jnp.float32)], 0),
        "gx",
    )
    cond_left = left[8:18].reshape(4, WIDE)
    cond_right = right[68:78].reshape(4, WIDE)
    fine, middle, image, used, send = kernel_call(
        functools.partial(coef_kernel, 4.0 / float(lines * lines)),
        [(5, 16, WIDE), (5, 16, WIDE), (4, 8, 512), (8, 128), (size_y, 16, 128)],
        locked_count, cond_left, conduct, cond_right, basis, left[:8], right[:ROWS], low, high,
        scratch=[(16, WIDE), (128, 512), (80, 512), (5, 16, WIDE), (5, 16, WIDE)],
        scalars=1, far_out=(0, 1),
    )
    got_y = lax.all_to_all(send, "gy", 0, 0)
    (send,) = kernel_call(
        functools.partial(middle_kernel, lines), [(size_x, 16, 128)], got_y
    )
    got_x = lax.all_to_all(send, "gx", 0, 0)
    residual, res_low, res_high, sums = kernel_call(
        functools.partial(residual_kernel, cells),
        [(4, 4, 512), (4, 4, 384), (4, 4, 384), (8, 128)],
        got_x, used, basis, image,
    )
    low, high = pair_shift(res_low, res_high, "gy")
    mid = jnp.concatenate([low, residual, high], axis=2)
    left, right = pair_shift(mid, mid, "gx")
    r1, send, strips = kernel_call(
        down_kernel, [(4, 4, WIDE), (size_y, 8, 128), (2, 8, 128)], left, mid, right, fine, middle
    )
    (send,) = kernel_call(
        functools.partial(line_kernel, lines), [(size_x, 16, 128)],
        lax.all_to_all(send, "gy", 0, 0), got_y, strips,
        scratch=[(lines, 8, 128)],
    )
    precond, send = kernel_call(
        up_kernel, [(4, 4, 512), (size_y, 16, 128)],
        lax.all_to_all(send, "gx", 0, 0), got_x, r1, left, mid, right, sums, fine, middle, basis,
        scratch=[(5, 16, WIDE), (5, 16, WIDE), (4, ROWS, 512)], far=(7, 8, 9),
    )
    got_y = lax.all_to_all(send, "gy", 0, 0)
    got_x = spread(jnp.sum(got_y[:, :8], axis=0), "gx")
    new_modes, new_directions, ritz, corr = kernel_call(
        functools.partial(ritz_kernel, cells),
        [(4, 4, 512), (4, 4, 512), (4,), (4, LOCKED)],
        got_x, got_y[:, 8:], used, precond, basis,
        scratch=[(128, 128), (4, ROWS, 512)], far=(4,), results=True,
    )
    return (new_modes, new_directions, ritz, corr.T)


def solution(mesh):
    placed = (
        P(None, "gx", "gy"),
        P(None, "gx", "gy"),
        P(None, "gx", "gy"),
        P("gx", "gy"),
        P(),
        P(),
    )
    return jax.shard_map(
        on_device,
        mesh=mesh,
        in_specs=placed,
        out_specs=(P(None, "gx", "gy"), P(None, "gx", "gy"), P(), P()),
        check_vma=False,
    )
```

```python
import functools

import jax
import jax.numpy as jnp
from jax import lax
from jax.experimental import pallas as pl
from jax.experimental.pallas import tpu as pltpu
from jax.sharding import PartitionSpec as P

NZ = 64
ACTIVE = 4
LOCKED = 60
BASIS = 68
ROWS = 72
SWEEPS = 3
RITZ = 3
OMEGA = 0.6
EPSILON = 1e-06
PRECISE = lax.Precision.HIGHEST
WIDE = 1280
OWN = 384
INTERPRET = False


def kernel_call(
    body, out, *args, scratch=(), scalars=0, far=(), far_out=(), inputs=False, results=False
):
    specs, placed = [], []
    for at, value in enumerate(args):
        space = pltpu.SMEM if at < scalars else pl.ANY if at in far else pltpu.VMEM
        specs.append(pl.BlockSpec(memory_space=space))
        if space is pltpu.VMEM and not (inputs or INTERPRET):
            value = pltpu.with_memory_space_constraint(value, pltpu.VMEM)
        placed.append(value)
    shapes, stored = [], []
    for at, shape in enumerate(out):
        space = pltpu.SMEM if len(shape) == 1 else pl.ANY if at in far_out else pltpu.VMEM
        stored.append(pl.BlockSpec(memory_space=space))
        if space is pltpu.VMEM and not (results or INTERPRET):
            shapes.append(pltpu.VMEM(shape, jnp.float32))
        else:
            shapes.append(jax.ShapeDtypeStruct(shape, jnp.float32))
    copies = len(far) + len(far_out)
    held = [pltpu.VMEM(shape, jnp.float32) for shape in scratch]
    held += [pltpu.SemaphoreType.DMA] * copies
    return pl.pallas_call(
        body,
        out_shape=shapes,
        in_specs=specs,
        out_specs=stored,
        scratch_shapes=held,
        interpret=INTERPRET,
    )(*placed)


def roll(value, shift, axis=1):
    return pltpu.roll(value, shift % value.shape[axis], axis)


def lanes_of(value):
    rows, lanes = value.shape
    tile = lax.broadcasted_iota(jnp.int32, (rows, 128), 1)
    return jnp.concatenate([tile] * (lanes // 128), axis=1)


def pair_z(value):
    even = lanes_of(value) % 2 == 0
    return value + jnp.where(even, roll(value, -1), roll(value, 1))


def pair_y(value):
    first = lanes_of(value) % 128 < 64
    return value + jnp.where(first, roll(value, -64), roll(value, 64))


def quad_z(value):
    first = lanes_of(value) % 4 < 2
    return value + jnp.where(first, roll(value, -2), roll(value, 2))


def quad_y(value):
    first = (lax.broadcasted_iota(jnp.int32, value.shape, 1) // 128) % 2 == 0
    return value + jnp.where(first, roll(value, -128), roll(value, 128))


def dot_nt(left, right):
    return lax.dot_general(
        left, right, (((1,), (1,)), ((), ())), precision=PRECISE, preferred_element_type=jnp.float32
    )


def dot_nn(left, right):
    return lax.dot_general(
        left, right, (((1,), (0,)), ((), ())), precision=PRECISE, preferred_element_type=jnp.float32
    )


def relax_weight(diagonal):
    inside = diagonal > 0
    return jnp.where(inside, OMEGA / jnp.where(inside, diagonal, 1.0), 0.0)


def joined(here, there):
    both = (here > 0) & (there > 0)
    return jnp.where(both, 2.0 * here * there / jnp.where(both, here + there, 1.0), 0.0)


def face(coupling, here, there):
    return coupling + jnp.where(there > 0, 0.0, 2.0 * here)


def input_kernel(table, modes, directions, locked, kinds, basis, conduct, low_out, high_out):
    value = jnp.zeros((4, 512), jnp.float32)
    kind = kinds[...]
    for at in range(table.shape[0]):
        value = jnp.where(kind == at, table[at], value)
    conduct[...] = value
    for at in range(4):
        basis[at, 0:4, :] = modes[:, at, :]
        basis[at, 4:8, :] = directions[:, at, :]
        basis[at, 8:BASIS, :] = locked[:, at, :]
        basis[at, BASIS:ROWS, :] = jnp.zeros((ROWS - BASIS, 512), jnp.float32)
    first = lax.broadcasted_iota(jnp.int32, (ROWS, 128), 1) < 64
    for at in range(2):
        near, far = basis[at, :, 0:128], basis[at + 2, :, 0:128]
        low_out[at, 0:ROWS, :] = jnp.where(first, near, roll(far, 64))
        near, far = basis[at, 0:8, 384:512], basis[at + 2, 0:8, 384:512]
        high_out[at, 0:8, :] = jnp.where(first[0:8], roll(near, 64), far)
        for part in range(6):
            row, lane = 2 * at + part // 3, 128 * (part % 3)
            low_out[at, BASIS + part : BASIS + part + 1, :] = value[row : row + 1, lane : lane + 128]
            lane += 128
            high_out[at, 8 + part : 9 + part, :] = value[row : row + 1, lane : lane + 128]


def coef_kernel(
    shift, count, cond_left, cond_mid, cond_right, basis, left, right, low, high,
    fine_far, middle_far, image_out, used_out, send_out, cond, vmat, umat, fine_out, middle_out,
    fine_done, middle_done,
):
    used = lanes_of(used_out)
    used_out[...] = jnp.where((used >= 8) & (used < 8 + count[0]), 1.0, 0.0)
    cond[0:4, :] = cond_left[...]
    cond[4:8, :] = cond_mid[...]
    cond[8:12, :] = cond_right[...]
    cond[12:16, :] = jnp.zeros((4, WIDE), jnp.float32)
    here = cond[...]
    z_at = lanes_of(here) % 64
    x_next, x_prev = roll(here, -1, 0), roll(here, 1, 0)
    y_next, y_prev = roll(here, -64), roll(here, 64)
    z_next = jnp.where(z_at < 63, roll(here, -1), 0.0)
    z_prev = jnp.where(z_at > 0, roll(here, 1), 0.0)
    tx, ty, tz = joined(here, x_next), joined(here, y_next), joined(here, z_next)
    y_faces = face(ty, here, y_next) + face(roll(ty, 64), here, y_prev)
    diagonal = face(tx, here, x_next) + face(roll(tx, 1, 0), here, x_prev) + y_faces
    diagonal = diagonal + face(tz, here, z_next) + face(roll(tz, 1), here, z_prev)
    for at, value in enumerate((diagonal, tx, ty, tz, relax_weight(diagonal))):
        fine_out[at] = value

    def pairs(value):
        return pair_y(pair_z(value))

    def pair_x(value):
        return value + roll(value, -1, 0)

    lower_y, lower_z = lanes_of(here) % 128 < 64, z_at % 2 == 0
    inner = jnp.where(lower_y, ty, 0.0)
    sum_x = pairs(tx)
    ty1 = pair_x(pairs(ty - inner))
    tz1 = pair_x(pairs(jnp.where(lower_z, 0.0, tz)))
    tx1 = roll(sum_x, -1, 0)
    diagonal1 = pair_x(pairs(diagonal - 2.0 * (inner + jnp.where(lower_z, tz, 0.0))))
    diagonal1 = diagonal1 - 2.0 * sum_x
    for at, value in enumerate((diagonal1, tx1, ty1, tz1, relax_weight(diagonal1))):
        middle_out[at] = value
    fine_copy = pltpu.make_async_copy(fine_out, fine_far, fine_done)
    middle_copy = pltpu.make_async_copy(middle_out, middle_far, middle_done)
    fine_copy.start()
    middle_copy.start()

    def own(value):
        return value[0:8, OWN : OWN + 512]

    def quads(value):
        value = quad_y(quad_z(value))
        return value[4:5] + value[6:7]

    y_faces1 = pair_x(pairs(own(y_faces - 2.0 * inner)))
    tx1, ty1, tz1, diagonal1 = own(tx1), own(ty1), own(tz1), own(diagonal1)
    lane = lanes_of(tx1)
    lower_y = (lax.broadcasted_iota(jnp.int32, tx1.shape, 1) // 128) % 2 == 0
    lower_z = lane % 4 < 2
    inner = jnp.where(lower_y, ty1, 0.0)
    across = quad_y(quad_z(tx1))
    tx2 = across[6:7]
    ty2 = quads(ty1 - inner)
    tz2 = quads(jnp.where(lower_z, 0.0, tz1))
    diagonal2 = quads(diagonal1 - 2.0 * (inner + jnp.where(lower_z, tz1, 0.0)))
    diagonal2 = diagonal2 - 2.0 * across[4:5]
    y_faces2 = quads(y_faces1 - 2.0 * inner)
    line2 = y_faces2 + shift * (diagonal2 - y_faces2)
    coarse = []
    for value in (tx2, ty2, tz2, diagonal2, line2):
        first, second = value[:, 0:128], value[:, 256:384]
        coarse.append(jnp.where(lanes_of(first) < 64, first, second))

    gram = jnp.zeros((80, 128), jnp.float32)
    for at in range(4):
        plane = 4 + at
        row = slice(plane, plane + 1)
        below, above = low[at % 2, 0:8, :], high[at % 2, 0:ROWS, :]
        below = roll(below, 64) if at < 2 else below
        above = above if at < 2 else roll(above, 64)
        after = right[...] if at == 3 else basis[at + 1]
        before = left[0:8, :] if at == 0 else basis[at - 1, 0:8, :]
        wide = jnp.concatenate([below, basis[at, 0:8, :], above[0:8]], axis=1)
        dg, sx, sy, sz = (fine_out[kind, row, 256:1024] for kind in range(4))
        image = dg * wide - sy * roll(wide, -64) - roll(sy * wide, 64)
        image = (image - sz * roll(wide, -1) - roll(sz * wide, 1))[:, 128:640]
        image = image - sx[:, 128:640] * after[0:8]
        image = image - fine_out[1, plane - 1 : plane, OWN : OWN + 512] * before
        image_out[at] = image
        wide = jnp.concatenate([basis[at, 8:ROWS, :], above[8:ROWS]], axis=1)
        dg, sx, sy, sz = (fine_out[kind, row, OWN:1024] for kind in range(4))
        half = (0.5 * dg) * wide - sy * roll(wide, -64) - sz * roll(wide, -1)
        half = half[:, 0:512] - sx[:, 0:512] * after[8:ROWS]
        vmat[0:72, :] = basis[at]
        vmat[68:128, :] = half[0:60]
        umat[0:72, :] = basis[at]
        umat[72:80, :] = image
        gram = gram + dot_nt(umat[...], vmat[...])
    now = packed_rows(jnp.concatenate([gram[0:4], gram[72:76]], axis=0), [coarse[0], coarse[2]])
    rest = jnp.concatenate([coarse[1], coarse[4], coarse[3]], axis=0)
    for target in range(send_out.shape[0]):
        send_out[target, 0:8, :] = now
        send_out[target, 8:13, :] = gram[5 * target : 5 * target + 5]
        send_out[target, 13:16, :] = rest
    fine_copy.wait()
    middle_copy.wait()


def packed_rows(rows, extra):
    lane = lanes_of(rows)
    row = lax.broadcasted_iota(jnp.int32, rows.shape, 0)
    for at, value in enumerate(extra):
        for part in range(4):
            moved = roll(value, 96 - 32 * part)
            rows = jnp.where((row == 4 * at + part) & (lane >= 96), moved, rows)
    return rows


def unpacked_row(rows, at):
    lane = lanes_of(rows[0:1])
    value = roll(rows[4 * at : 4 * at + 1], -96)
    for part in range(1, 4):
        moved = roll(rows[4 * at + part : 4 * at + part + 1], 32 * part - 96)
        value = jnp.where(lane // 32 == part, moved, value)
    return value


def half_of(value, half, wanted):
    return value if half == wanted else roll(value, 64)


def spot_of(value, place):
    lane = lanes_of(value)
    return (lane // 64 == place // 4) & (lane % 4 == place % 4)


def middle_kernel(lines, got, send_out):
    at_y = lax.axis_index("gy")
    total = got[0]
    for source in range(1, got.shape[0]):
        total = total + got[source]
    packed = jnp.zeros((4, 128), jnp.float32)
    for place in range(8):
        source = at_y + (place - 3) // 2
        valid = (source >= 0) & (source < lines // 2)
        value = got[jnp.clip(source, 0, lines // 2 - 1)]
        tx, tz = unpacked_row(value, 0), unpacked_row(value, 1)
        value = jnp.concatenate([tx, value[13:14], tz, value[15:16]], axis=0)
        value = half_of(value, (place - 3) % 2, place // 4)
        packed = packed + jnp.where(spot_of(value, place) & valid, value, 0.0)
    now = packed_rows(total[0:8], [packed[0:1]])
    for target in range(send_out.shape[0]):
        send_out[target, 0:8, :] = now
        send_out[target, 8:13, :] = total[8:13]
        send_out[target, 13:16, :] = packed[1:4]


def residual_kernel(cells, got, used, basis, image, res_out, low_out, high_out, sums_out):
    total = got[0]
    for source in range(1, got.shape[0]):
        total = total + got[source]
    sums_out[...] = total[8:16]
    overlap, energy = total[0:4], total[4:8]
    lane = lanes_of(overlap)
    own = lane == lax.broadcasted_iota(jnp.int32, overlap.shape, 0)
    norm = jnp.sum(jnp.where(own, overlap, 0.0), axis=1, keepdims=True)
    top = jnp.sum(jnp.where(own, energy, 0.0), axis=1, keepdims=True)
    quotient = top / cells / (norm / cells + EPSILON)
    coupling = (energy - quotient * overlap) / cells
    weights = jnp.where(used[0:4, :] > 0, coupling, 0.0)
    weights = jnp.concatenate([weights, jnp.zeros((4, 128), jnp.float32)], axis=0)
    for at in range(4):
        field = basis[at]
        value = image[at][0:4] - quotient * field[0:4]
        value = value - dot_nn(weights[:, 0:ROWS], field)[0:4]
        res_out[at] = value
        low_out[at] = value[:, 0:384]
        high_out[at] = value[:, 128:512]


def padded(value):
    return jnp.concatenate([value, jnp.zeros(value.shape, jnp.float32)], axis=0)


def apply_at(values, coefs, row, row_step, at, y_step, z_step, lanes):
    here = values[at]
    dg, sx, sy, sz = (coefs[kind, row : row + 1, lanes] for kind in range(4))
    before = coefs[1, row - row_step : row - row_step + 1, lanes]
    image = dg * here - sx * values[at + 1] - before * values[at - 1]
    image = image - sy * roll(here, -y_step) - roll(sy * here, y_step)
    return image - sz * roll(here, -z_step) - roll(sz * here, z_step)


def fine_image(values, fine, plane, lanes=slice(0, WIDE)):
    return apply_at(values, fine, plane, 1, plane, 64, 1, lanes)


def middle_image(values, middle, plane):
    return apply_at(values, middle, 2 * plane, 2, plane, 128, 2, slice(0, WIDE))


def planes_of(left, mid, right, first, last):
    parts = [left[at] for at in range(3)] + [mid[at] for at in range(4)]
    parts += [right[at] for at in range(3)]
    return {at: padded(parts[at - 1]) for at in range(first, last)}


def down_kernel(left, mid, right, fine, middle, r1_out, send_out, strip_out):
    source = planes_of(left, mid, right, 1, 11)
    error = {at: fine[4, at : at + 1, :] * source[at] for at in range(1, 11)}
    rest = {at: source[at] - fine_image(error, fine, at) for at in range(2, 10)}
    source1, error1 = {}, {}
    for plane in range(1, 5):
        value = pair_y(pair_z(rest[2 * plane] + rest[2 * plane + 1]))
        source1[plane] = value
        r1_out[plane - 1] = value[0:4]
        error1[plane] = middle[4, 2 * plane : 2 * plane + 1, :] * value
    low = sum(source1[plane] - middle_image(error1, middle, plane) for plane in (2, 3))
    low = quad_y(quad_z(low[:, OWN : OWN + 512]))
    both = jnp.concatenate([low[0:4, 0:128], low[0:4, 256:384]], axis=0)
    for target in range(send_out.shape[0]):
        send_out[target] = both
    for at in range(2):
        tiles = [error1[2 + at][0:4, 128 * t : 128 * t + 128] for t in range(1, 9)]
        lane = lanes_of(tiles[0])
        half, odd = lane // 64, lane % 2
        for group in range(2):
            a, b, c, d = tiles[4 * group : 4 * group + 4]
            value = jnp.where(half == 0, jnp.where(odd == 0, a, b), jnp.where(odd == 0, c, d))
            strip_out[at, 4 * group : 4 * group + 4, :] = value


def line_kernel(lines, got, coefs, strips, send_out, solved):
    at_x, at_y = lax.axis_index("gx"), lax.axis_index("gy")
    factors, previous, previous_factor, previous_link = [], None, None, None
    for source in range(lines // 2):
        rows = coefs[source, 13:15, :]
        turned = roll(rows, 64)
        first = lanes_of(rows) < 64
        for part in range(2):
            line = 2 * source + part
            value = jnp.where(first, rows, turned) if part == 0 else jnp.where(first, turned, rows)
            link, main = value[0:1], value[1:2]
            right = got[source, 4 * part : 4 * part + 4, :]
            solved[line, 4:8, :] = right
            if line == 0:
                scale = 1.0 / main
                update = scale * right
            else:
                scale = 1.0 / (main - previous_link * previous_factor)
                update = scale * (right + previous_link * previous)
            previous, previous_factor, previous_link = update, link * scale, link
            solved[line, 0:4, :] = update
            factors.append(previous_factor)
    for line in range(lines - 2, -1, -1):
        previous = solved[line, 0:4, :] + factors[line] * previous
        solved[line, 0:4, :] = previous
    packed = jnp.zeros((8, 128), jnp.float32)
    for place in range(8):
        line = 2 * at_y - 3 + place
        valid = (line >= 0) & (line < lines)
        value = solved[jnp.clip(line, 0, lines - 1)]
        packed = packed + jnp.where(spot_of(value, place) & valid, value, 0.0)
    for target in range(send_out.shape[0]):
        send_out[target, 0:8, :] = packed
        send_out[target, 8:16, :] = strips[(at_x >= target).astype(jnp.int32)]


def up_kernel(
    got, coefs, r1, left, mid, right, sums, fine_far, middle_far, basis_far,
    pre_out, send_out, fine, middle, vmat, fine_done, middle_done, basis_done,
):
    middle_copy = pltpu.make_async_copy(middle_far, middle, middle_done)
    fine_copy = pltpu.make_async_copy(fine_far, fine, fine_done)
    basis_copy = pltpu.make_async_copy(basis_far, vmat, basis_done)
    middle_copy.start()
    fine_copy.start()
    basis_copy.start()
    at_x = lax.axis_index("gx")
    count = got.shape[0]
    error, source, links = {}, {}, {}
    for step in range(-3, 4):
        index = at_x + step
        valid = ((index >= 0) & (index < count)).astype(jnp.float32)
        kept = jnp.clip(index, 0, count - 1)
        rows = got[kept, 0:8, :] * valid
        error[step] = padded(rows[0:4])
        source[step] = padded(rows[4:8])
        near = coefs[kept] * valid
        links[step] = jnp.concatenate([unpacked_row(near, 0), near[13:16]], axis=0)
    lane = lanes_of(error[0])
    spot = lane % 4
    for reach in range(SWEEPS - 2, -1, -1):
        updated = dict(error)
        for step in range(-1 - reach, 2 + reach):
            here = error[step]
            sx, sy, sz, dg = (links[step][kind : kind + 1] for kind in range(4))
            up = jnp.where(spot < 3, roll(here, -1), roll(here, -61))
            flux = sy * here
            down = jnp.where(spot > 0, roll(flux, 1), roll(flux, 61))
            value = dg * here - sx * error[step + 1] - links[step - 1][0:1] * error[step - 1]
            value = value - sy * up - down - sz * roll(here, -4) - roll(sz * here, 4)
            updated[step] = here + relax_weight(dg) * (source[step] - value)
        error = updated
    blank = jnp.zeros((8, 128), jnp.float32)
    coarse = {}
    for step in range(-1, 2):
        tiles = []
        for place in range(2, 6):
            value = jnp.where(spot_of(error[step], place), error[step], 0.0)
            value = quad_z(pair_z(value))
            value = value + roll(value, 64)
            tiles += [value, value]
        coarse[step] = jnp.concatenate([blank] + tiles + [blank], axis=1)

    def strip(step):
        index = at_x + step
        valid = ((index >= 0) & (index < count)).astype(jnp.float32)
        rows = got[jnp.clip(index, 0, count - 1), 8:16, :] * valid
        tiles = []
        for group in range(2):
            part = padded(rows[4 * group : 4 * group + 4])
            for place in range(4):
                at = (lane // 64 == place // 2) & (lane % 2 == place % 2)
                value = pair_z(jnp.where(at, part, 0.0))
                tiles.append(value + roll(value, 64))
        return jnp.concatenate([blank] + tiles + [blank], axis=1)

    middle_copy.wait()
    error1, source1 = {0: strip(-1) + coarse[-1], 5: strip(1) + coarse[1]}, {}
    for plane in range(1, 5):
        source1[plane] = padded(r1[plane - 1])
        weight = middle[4, 2 * plane : 2 * plane + 1, :]
        error1[plane] = weight * source1[plane] + coarse[plane // 2 - 1]
    final1 = {}
    for plane in range(1, 5):
        weight = middle[4, 2 * plane : 2 * plane + 1, :]
        final1[plane] = error1[plane] + weight * (
            source1[plane] - middle_image(error1, middle, plane)
        )
    fine_copy.wait()
    lanes = slice(256, 1024)
    source0 = planes_of(left, mid, right, 2, 10)
    source0 = {at: value[:, lanes] for at, value in source0.items()}
    error0 = {
        at: fine[4, at : at + 1, lanes] * source0[at] + final1[at // 2][:, lanes]
        for at in range(2, 10)
    }
    final0 = {}
    for at in range(3, 9):
        weight = fine[4, at : at + 1, lanes]
        final0[at] = error0[at] + weight * (source0[at] - fine_image(error0, fine, at, lanes))
    basis_copy.wait()
    both = jnp.zeros((8, ROWS), jnp.float32)
    for at in range(4):
        own = slice(128, 640)
        value = final0[4 + at][0:4, own]
        pre_out[at] = value
        vmat[at, BASIS:ROWS, :] = value
        value = jnp.concatenate([value, fine_image(final0, fine, 4 + at, lanes)[0:4, own]], axis=0)
        both = both + dot_nt(value, vmat[at])
    now = jnp.concatenate([both, jnp.zeros((8, 128 - ROWS), jnp.float32)], axis=1)
    for target in range(send_out.shape[0]):
        send_out[target, 0:8, :] = now
        send_out[target, 8:16, :] = sums[...]


def eliminate(matrix, steps):
    row = lax.broadcasted_iota(jnp.int32, matrix.shape, 0)
    for step in range(steps):
        pivot = matrix[step : step + 1, :] / matrix[step : step + 1, step : step + 1]
        column = matrix[:, step : step + 1]
        matrix = matrix - jnp.where(row > step, column, 0.0) * pivot
    diagonal = jnp.where(lanes_of(matrix) == row, matrix, 0.0)
    diagonal = jnp.sum(diagonal, axis=1, keepdims=True)
    scale = lax.rsqrt(jnp.where(row[:, 0:1] < steps, diagonal, 1.0))
    return matrix * scale


def small_product(left, right, count):
    terms = [left[:, at : at + 1] * right[at : at + 1, :] for at in range(count)]
    while len(terms) > 1:
        terms = [sum(terms[at : at + 2]) for at in range(0, len(terms), 2)]
    return terms[0]


def ritz_kernel(
    cells, got, gathered, used, pre, basis_far, modes_out, dirs_out, ritz_out, corr_out,
    gram, field, basis_done,
):
    basis_copy = pltpu.make_async_copy(basis_far, field, basis_done)
    basis_copy.start()
    total = got[0]
    for source in range(1, got.shape[0]):
        total = total + got[source]
    total = total / cells
    gram[80:128, :] = jnp.zeros((48, 128), jnp.float32)
    for source in range(16):
        gram[5 * source : 5 * source + 5, :] = gathered[source, 0:5, :]
    gram = gram[...] / cells
    shape = (16, 128)
    row = lax.broadcasted_iota(jnp.int32, shape, 0)
    lane = lax.broadcasted_iota(jnp.int32, shape, 1)
    zero4 = jnp.zeros((4, 128), jnp.float32)
    corr = jnp.where(used[0:4, :] > 0, total[0:4], 0.0)
    corr_out[...] = roll(corr, -8)[:, 0:LOCKED]
    locked_part = jnp.concatenate([zero4, -corr, zero4, zero4], axis=0)
    ones = ((row < 4) & (lane == row)) | ((row >= 8) & (row < 12) & (lane == row - 4))
    pre_ones = (row >= 4) & (row < 8) & (lane == row + 64)
    on_basis = jnp.where(ones, 1.0, locked_part)
    weights = jnp.where(pre_ones, 1.0, on_basis)
    pre_lane = (lane >= 68) & (lane < 72)

    def from_pre(part):
        rows4 = jnp.concatenate([zero4, part, zero4, zero4], axis=0)
        rows4 = jnp.where(lane < 72, rows4, 0.0)
        return jnp.where(pre_lane, 0.5 * rows4, rows4)

    products = dot_nn(jnp.concatenate([on_basis, locked_part], axis=0), gram)
    first = jnp.where(lane < 68, products[0:16], 0.0)
    second = roll(jnp.where(lane >= 68, products[16:32], 0.0), -60)
    pair = gram[72:80]
    pair = jnp.concatenate([pair[0:4], zero4, pair[4:8], zero4], axis=0)
    pair = jnp.where(lane < 68, jnp.where(lane < 8, 0.5 * pair, pair), 0.0)
    stacked = [0.5 * first + from_pre(total[0:4]), second + pair + from_pre(total[4:8])]
    stacked = jnp.concatenate(stacked, axis=0)
    straight = dot_nt(stacked, weights)
    turned = dot_nt(weights, stacked)
    mass = straight[0:16] + turned[:, 0:16]
    stiff = straight[16:32] + turned[:, 16:32]
    eye = jnp.where((row < 12) & (lane == row + 64), 1.0, 0.0)
    wide = jnp.zeros((16, 112), jnp.float32)
    mass = jnp.concatenate([mass, wide], axis=1)
    stiff = jnp.concatenate([stiff, wide], axis=1)
    done = eliminate(mass + roll(stiff, 32) + eye, 12)
    inside = (row < 12) & (lane < 12)
    half = jnp.where(inside, roll(done, -32), 0.0)
    inverse = jnp.where(inside, roll(done, -64), 0.0)
    reduced = dot_nt(half, inverse) + dot_nt(inverse, half)
    reduced = 0.5 * jnp.concatenate([reduced, wide], axis=1)
    top = jnp.sum(jnp.where(lane == row, reduced, 0.0), axis=(0, 1), keepdims=True)
    row8 = lax.broadcasted_iota(jnp.int32, (8, 128), 0)
    lane8 = lax.broadcasted_iota(jnp.int32, (8, 128), 1)
    first4 = row8 < 4
    basis_q = jnp.where(first4 & (lane8 == row8), 1.0, 0.0)
    for step in range(RITZ):
        raised = top * basis_q - small_product(basis_q, reduced, 12)
        joint = roll(raised, 32)
        for part in range(ACTIVE):
            column = jnp.sum(raised * raised[part : part + 1, :], axis=1, keepdims=True)
            joint = joint + jnp.where(lane8 == part, column, 0.0)
        basis_q = jnp.where(first4 & (lane8 < 12), roll(eliminate(joint, 4), -32), 0.0)
    ritz = jnp.sum(basis_q * small_product(basis_q, reduced, 12), axis=1, keepdims=True)
    for part in range(ACTIVE):
        ritz_out[part] = ritz[part, 0]
    coefs = small_product(basis_q, inverse, 12)
    tail = jnp.where(lane8 >= 4, coefs, 0.0)
    both = jnp.concatenate([coefs[0:4], tail[0:4]], axis=0)
    mix = small_product(both, weights, 12)[:, 0:ROWS]
    basis_copy.wait()
    for at in range(4):
        field[at, BASIS:ROWS, :] = pre[at]
        value = dot_nn(mix, field[at])
        for part in range(4):
            modes_out[part, at : at + 1, :] = value[part : part + 1]
            dirs_out[part, at : at + 1, :] = value[4 + part : 5 + part]


def pair_shift(low, high, axis):
    count = lax.axis_size(axis)
    forward = [(at, at + 1) for at in range(count - 1)]
    backward = [(at + 1, at) for at in range(count - 1)]
    above = lax.ppermute(low, axis, backward)
    return lax.ppermute(high, axis, forward), above


def spread(block, axis):
    count = lax.axis_size(axis)
    return lax.all_to_all(jnp.broadcast_to(block, (count,) + block.shape), axis, 0, 0)


def on_device(modes, directions, locked, perm_class, perm_table, locked_count):
    size_x, size_y = lax.axis_size("gx"), lax.axis_size("gy")
    lines = 2 * size_y
    cells = float(4 * 512 * size_x * size_y)
    basis, conduct, low, high = kernel_call(
        input_kernel, [(4, ROWS, 512), (4, 512), (2, BASIS + 6, 128), (2, 14, 128)],
        perm_table, modes, directions, locked, perm_class, scalars=1, inputs=True,
    )
    low, high = pair_shift(low, high, "gy")
    cond_low = low[:, 8:].reshape(4, 384)
    cond_high = high[:, BASIS:].reshape(4, 384)
    conduct = jnp.concatenate([cond_low, conduct, cond_high], axis=1)
    rows = conduct.reshape(10, 512)
    left, right = pair_shift(
        jnp.concatenate([basis[0, :BASIS], rows, jnp.zeros((2, 512), jnp.float32)], 0),
        jnp.concatenate([basis[3, :8], rows, jnp.zeros((6, 512), jnp.float32)], 0),
        "gx",
    )
    cond_left = left[8:18].reshape(4, WIDE)
    cond_right = right[68:78].reshape(4, WIDE)
    fine, middle, image, used, send = kernel_call(
        functools.partial(coef_kernel, 4.0 / float(lines * lines)),
        [(5, 16, WIDE), (5, 16, WIDE), (4, 8, 512), (8, 128), (size_y, 16, 128)],
        locked_count, cond_left, conduct, cond_right, basis, left[:8], right[:ROWS], low, high,
        scratch=[(16, WIDE), (128, 512), (80, 512), (5, 16, WIDE), (5, 16, WIDE)],
        scalars=1, far_out=(0, 1),
    )
    got_y = lax.all_to_all(send, "gy", 0, 0)
    (send,) = kernel_call(
        functools.partial(middle_kernel, lines), [(size_x, 16, 128)], got_y
    )
    got_x = lax.all_to_all(send, "gx", 0, 0)
    residual, res_low, res_high, sums = kernel_call(
        functools.partial(residual_kernel, cells),
        [(4, 4, 512), (4, 4, 384), (4, 4, 384), (8, 128)],
        got_x, used, basis, image,
    )
    low, high = pair_shift(res_low, res_high, "gy")
    mid = jnp.concatenate([low, residual, high], axis=2)
    left, right = pair_shift(mid[:3], mid[1:], "gx")
    r1, send, strips = kernel_call(
        down_kernel, [(4, 4, WIDE), (size_y, 8, 128), (2, 8, 128)], left, mid, right, fine, middle
    )
    (send,) = kernel_call(
        functools.partial(line_kernel, lines), [(size_x, 16, 128)],
        lax.all_to_all(send, "gy", 0, 0), got_y, strips,
        scratch=[(lines, 8, 128)],
    )
    precond, send = kernel_call(
        up_kernel, [(4, 4, 512), (size_y, 16, 128)],
        lax.all_to_all(send, "gx", 0, 0), got_x, r1, left, mid, right, sums, fine, middle, basis,
        scratch=[(5, 16, WIDE), (5, 16, WIDE), (4, ROWS, 512)], far=(7, 8, 9),
    )
    got_y = lax.all_to_all(send, "gy", 0, 0)
    got_x = spread(jnp.sum(got_y[:, :8], axis=0), "gx")
    new_modes, new_directions, ritz, corr = kernel_call(
        functools.partial(ritz_kernel, cells),
        [(4, 4, 512), (4, 4, 512), (4,), (4, LOCKED)],
        got_x, got_y[:, 8:], used, precond, basis,
        scratch=[(128, 128), (4, ROWS, 512)], far=(4,), results=True,
    )
    return (new_modes, new_directions, ritz, corr.T)


def solution(mesh):
    placed = (
        P(None, "gx", "gy"),
        P(None, "gx", "gy"),
        P(None, "gx", "gy"),
        P("gx", "gy"),
        P(),
        P(),
    )
    return jax.shard_map(
        on_device,
        mesh=mesh,
        in_specs=placed,
        out_specs=(P(None, "gx", "gy"), P(None, "gx", "gy"), P(), P()),
        check_vma=False,
    )
```

```python
import functools

import jax
import jax.numpy as jnp
from jax import lax
from jax.experimental import pallas as pl
from jax.experimental.pallas import tpu as pltpu
from jax.sharding import PartitionSpec as P

NZ = 64
ACTIVE = 4
LOCKED = 60
BASIS = 68
ROWS = 72
SWEEPS = 3
RITZ = 3
OMEGA = 0.6
EPSILON = 1e-06
PRECISE = lax.Precision.HIGHEST
WIDE = 1280
OWN = 384
INTERPRET = False


def kernel_call(
    body, out, *args, scratch=(), scalars=0, far=(), far_out=(), inputs=False, results=False,
    copies=0,
):
    specs, placed = [], []
    for at, value in enumerate(args):
        space = pltpu.SMEM if at < scalars else pl.ANY if at in far else pltpu.VMEM
        specs.append(pl.BlockSpec(memory_space=space))
        if space is pltpu.VMEM and not (inputs or INTERPRET):
            value = pltpu.with_memory_space_constraint(value, pltpu.VMEM)
        placed.append(value)
    shapes, stored = [], []
    for at, shape in enumerate(out):
        space = pltpu.SMEM if len(shape) == 1 else pl.ANY if at in far_out else pltpu.VMEM
        stored.append(pl.BlockSpec(memory_space=space))
        if space is pltpu.VMEM and not (results or INTERPRET):
            shapes.append(pltpu.VMEM(shape, jnp.float32))
        else:
            shapes.append(jax.ShapeDtypeStruct(shape, jnp.float32))
    copies = copies or len(far) + len(far_out)
    held = [pltpu.VMEM(shape, jnp.float32) for shape in scratch]
    held += [pltpu.SemaphoreType.DMA] * copies
    return pl.pallas_call(
        body,
        out_shape=shapes,
        in_specs=specs,
        out_specs=stored,
        scratch_shapes=held,
        interpret=INTERPRET,
    )(*placed)


def roll(value, shift, axis=1):
    return pltpu.roll(value, shift % value.shape[axis], axis)


def lanes_of(value):
    rows, lanes = value.shape
    tile = lax.broadcasted_iota(jnp.int32, (rows, 128), 1)
    return jnp.concatenate([tile] * (lanes // 128), axis=1)


def pair_z(value):
    even = lanes_of(value) % 2 == 0
    return value + jnp.where(even, roll(value, -1), roll(value, 1))


def pair_y(value):
    first = lanes_of(value) % 128 < 64
    return value + jnp.where(first, roll(value, -64), roll(value, 64))


def quad_z(value):
    first = lanes_of(value) % 4 < 2
    return value + jnp.where(first, roll(value, -2), roll(value, 2))


def quad_y(value):
    first = (lax.broadcasted_iota(jnp.int32, value.shape, 1) // 128) % 2 == 0
    return value + jnp.where(first, roll(value, -128), roll(value, 128))


def dot_nt(left, right):
    return lax.dot_general(
        left, right, (((1,), (1,)), ((), ())), precision=PRECISE, preferred_element_type=jnp.float32
    )


def dot_nn(left, right):
    return lax.dot_general(
        left, right, (((1,), (0,)), ((), ())), precision=PRECISE, preferred_element_type=jnp.float32
    )


def relax_weight(diagonal):
    inside = diagonal > 0
    return jnp.where(inside, OMEGA / jnp.where(inside, diagonal, 1.0), 0.0)


def joined(here, there):
    both = (here > 0) & (there > 0)
    return jnp.where(both, 2.0 * here * there / jnp.where(both, here + there, 1.0), 0.0)


def face(coupling, here, there):
    return coupling + jnp.where(there > 0, 0.0, 2.0 * here)


def input_kernel(table, modes, directions, locked, kinds, basis, low_out, high_out):
    value = jnp.zeros((4, 512), jnp.float32)
    kind = kinds[...]
    for at in range(table.shape[0]):
        value = jnp.where(kind == at, table[at], value)
    for at in range(4):
        basis[at, 0:4, :] = modes[:, at, :]
        basis[at, 4:8, :] = directions[:, at, :]
        basis[at, 8:BASIS, :] = locked[:, at, :]
        basis[at, BASIS:ROWS, :] = jnp.zeros((ROWS - BASIS, 512), jnp.float32)
        basis[at, BASIS : BASIS + 1, :] = value[at : at + 1]
        low_out[at] = basis[at, :, 0:384]
        high_out[at] = basis[at, :, 128:512]


def coef_kernel(
    shift, count, cond_left, cond_right, basis, left, right, locked_right,
    fine_far, middle_far, image_out, used_out, send_out, cond, vmat, umat, fine_out, middle_out,
    fine_done, middle_done,
):
    used = lanes_of(used_out)
    used_out[...] = jnp.where((used >= 8) & (used < 8 + count[0]), 1.0, 0.0)
    cond[0:4, :] = cond_left[...]
    for at in range(4):
        cond[4 + at : 5 + at, :] = basis[at, BASIS : BASIS + 1, :]
    cond[8:12, :] = cond_right[...]
    cond[12:16, :] = jnp.zeros((4, WIDE), jnp.float32)
    here = cond[...]
    z_at = lanes_of(here) % 64
    x_next, x_prev = roll(here, -1, 0), roll(here, 1, 0)
    y_next, y_prev = roll(here, -64), roll(here, 64)
    z_next = jnp.where(z_at < 63, roll(here, -1), 0.0)
    z_prev = jnp.where(z_at > 0, roll(here, 1), 0.0)
    tx, ty, tz = joined(here, x_next), joined(here, y_next), joined(here, z_next)
    y_faces = face(ty, here, y_next) + face(roll(ty, 64), here, y_prev)
    diagonal = face(tx, here, x_next) + face(roll(tx, 1, 0), here, x_prev) + y_faces
    diagonal = diagonal + face(tz, here, z_next) + face(roll(tz, 1), here, z_prev)
    for at, value in enumerate((diagonal, tx, ty, tz, relax_weight(diagonal))):
        fine_out[at] = value

    def pairs(value):
        return pair_y(pair_z(value))

    def pair_x(value):
        return value + roll(value, -1, 0)

    lower_y, lower_z = lanes_of(here) % 128 < 64, z_at % 2 == 0
    inner = jnp.where(lower_y, ty, 0.0)
    sum_x = pairs(tx)
    ty1 = pair_x(pairs(ty - inner))
    tz1 = pair_x(pairs(jnp.where(lower_z, 0.0, tz)))
    tx1 = roll(sum_x, -1, 0)
    diagonal1 = pair_x(pairs(diagonal - 2.0 * (inner + jnp.where(lower_z, tz, 0.0))))
    diagonal1 = diagonal1 - 2.0 * sum_x
    for at, value in enumerate((diagonal1, tx1, ty1, tz1, relax_weight(diagonal1))):
        middle_out[at] = value
    fine_copy = pltpu.make_async_copy(fine_out, fine_far, fine_done)
    middle_copy = pltpu.make_async_copy(middle_out, middle_far, middle_done)
    fine_copy.start()
    middle_copy.start()

    def own(value):
        return value[0:8, OWN : OWN + 512]

    def quads(value):
        value = quad_y(quad_z(value))
        return value[4:5] + value[6:7]

    y_faces1 = pair_x(pairs(own(y_faces - 2.0 * inner)))
    tx1, ty1, tz1, diagonal1 = own(tx1), own(ty1), own(tz1), own(diagonal1)
    lane = lanes_of(tx1)
    lower_y = (lax.broadcasted_iota(jnp.int32, tx1.shape, 1) // 128) % 2 == 0
    lower_z = lane % 4 < 2
    inner = jnp.where(lower_y, ty1, 0.0)
    across = quad_y(quad_z(tx1))
    tx2 = across[6:7]
    ty2 = quads(ty1 - inner)
    tz2 = quads(jnp.where(lower_z, 0.0, tz1))
    diagonal2 = quads(diagonal1 - 2.0 * (inner + jnp.where(lower_z, tz1, 0.0)))
    diagonal2 = diagonal2 - 2.0 * across[4:5]
    y_faces2 = quads(y_faces1 - 2.0 * inner)
    line2 = y_faces2 + shift * (diagonal2 - y_faces2)
    coarse = []
    for value in (tx2, ty2, tz2, diagonal2, line2):
        first, second = value[:, 0:128], value[:, 256:384]
        coarse.append(jnp.where(lanes_of(first) < 64, first, second))

    gram = jnp.zeros((80, 128), jnp.float32)
    for at in range(4):
        plane = 4 + at
        row = slice(plane, plane + 1)
        wide = basis[at, 0:8, :]
        after = right[...] if at == 3 else basis[at + 1, 0:8, :]
        before = left[...] if at == 0 else basis[at - 1, 0:8, :]
        dg, sx, sy, sz = (fine_out[kind, row, :] for kind in range(4))
        image = dg * wide - sy * roll(wide, -64) - roll(sy * wide, 64)
        image = image - sz * roll(wide, -1) - roll(sz * wide, 1)
        image = image - sx * after - fine_out[1, plane - 1 : plane, :] * before
        image_out[at] = image
        image = image[:, OWN : OWN + 512]
        wide = basis[at, 8:ROWS, OWN:1024]
        after = locked_right[...] if at == 3 else basis[at + 1, 8:ROWS, OWN : OWN + 512]
        dg, sx, sy, sz = (fine_out[kind, row, OWN:1024] for kind in range(4))
        half = (0.5 * dg) * wide - sy * roll(wide, -64) - sz * roll(wide, -1)
        half = half[:, 0:512] - sx[:, 0:512] * after
        vmat[0:72, :] = basis[at, :, OWN : OWN + 512]
        vmat[68:128, :] = half[0:60]
        umat[0:72, :] = basis[at, :, OWN : OWN + 512]
        umat[72:80, :] = image
        gram = gram + dot_nt(umat[...], vmat[...])
    now = packed_rows(jnp.concatenate([gram[0:4], gram[72:76]], axis=0), [coarse[0], coarse[2]])
    rest = jnp.concatenate([coarse[1], coarse[4], coarse[3]], axis=0)
    for target in range(send_out.shape[0]):
        send_out[target, 0:8, :] = now
        send_out[target, 8:13, :] = gram[5 * target : 5 * target + 5]
        send_out[target, 13:16, :] = rest
    fine_copy.wait()
    middle_copy.wait()


def packed_rows(rows, extra):
    lane = lanes_of(rows)
    row = lax.broadcasted_iota(jnp.int32, rows.shape, 0)
    for at, value in enumerate(extra):
        for part in range(4):
            moved = roll(value, 96 - 32 * part)
            rows = jnp.where((row == 4 * at + part) & (lane >= 96), moved, rows)
    return rows


def unpacked_row(rows, at):
    lane = lanes_of(rows[0:1])
    value = roll(rows[4 * at : 4 * at + 1], -96)
    for part in range(1, 4):
        moved = roll(rows[4 * at + part : 4 * at + part + 1], 32 * part - 96)
        value = jnp.where(lane // 32 == part, moved, value)
    return value


def half_of(value, half, wanted):
    return value if half == wanted else roll(value, 64)


def spot_of(value, place):
    lane = lanes_of(value)
    return (lane // 64 == place // 4) & (lane % 4 == place % 4)


def middle_kernel(lines, got, send_out):
    at_y = lax.axis_index("gy")
    total = got[0]
    for source in range(1, got.shape[0]):
        total = total + got[source]
    packed = jnp.zeros((4, 128), jnp.float32)
    for place in range(8):
        source = at_y + (place - 3) // 2
        valid = (source >= 0) & (source < lines // 2)
        value = got[jnp.clip(source, 0, lines // 2 - 1)]
        tx, tz = unpacked_row(value, 0), unpacked_row(value, 1)
        value = jnp.concatenate([tx, value[13:14], tz, value[15:16]], axis=0)
        value = half_of(value, (place - 3) % 2, place // 4)
        packed = packed + jnp.where(spot_of(value, place) & valid, value, 0.0)
    now = packed_rows(total[0:8], [packed[0:1]])
    for target in range(send_out.shape[0]):
        send_out[target, 0:8, :] = now
        send_out[target, 8:13, :] = total[8:13]
        send_out[target, 13:16, :] = packed[1:4]


def residual_kernel(cells, got, used, image, basis_far, res_out, sums_out, basis, done, *more):
    done = (done,) + more
    copies = [
        pltpu.make_async_copy(basis_far.at[at], basis.at[at], done[at]) for at in range(4)
    ]
    for copy in copies:
        copy.start()
    total = got[0]
    for source in range(1, got.shape[0]):
        total = total + got[source]
    sums_out[...] = total[8:16]
    overlap, energy = total[0:4], total[4:8]
    lane = lanes_of(overlap)
    own = lane == lax.broadcasted_iota(jnp.int32, overlap.shape, 0)
    norm = jnp.sum(jnp.where(own, overlap, 0.0), axis=1, keepdims=True)
    top = jnp.sum(jnp.where(own, energy, 0.0), axis=1, keepdims=True)
    quotient = top / cells / (norm / cells + EPSILON)
    coupling = (energy - quotient * overlap) / cells
    weights = jnp.where(used[0:4, :] > 0, coupling, 0.0)
    weights = jnp.concatenate([weights, jnp.zeros((4, 128), jnp.float32)], axis=0)
    for at in range(4):
        copies[at].wait()
        field = basis[at]
        value = image[at, 0:4, :] - quotient * field[0:4]
        res_out[at] = value - dot_nn(weights[:, 0:ROWS], field)[0:4]


def padded(value):
    return jnp.concatenate([value, jnp.zeros(value.shape, jnp.float32)], axis=0)


def apply_at(values, coefs, row, row_step, at, y_step, z_step, lanes):
    here = values[at]
    dg, sx, sy, sz = (coefs[kind, row : row + 1, lanes] for kind in range(4))
    before = coefs[1, row - row_step : row - row_step + 1, lanes]
    image = dg * here - sx * values[at + 1] - before * values[at - 1]
    image = image - sy * roll(here, -y_step) - roll(sy * here, y_step)
    return image - sz * roll(here, -z_step) - roll(sz * here, z_step)


def fine_image(values, fine, plane, lanes=slice(0, WIDE)):
    return apply_at(values, fine, plane, 1, plane, 64, 1, lanes)


def middle_image(values, middle, plane):
    return apply_at(values, middle, 2 * plane, 2, plane, 128, 2, slice(0, WIDE))


def planes_of(left, mid, right, first, last):
    parts = [left[at] for at in range(3)] + [mid[at] for at in range(4)]
    parts += [right[at] for at in range(3)]
    return {at: padded(parts[at - 1]) for at in range(first, last)}


def down_kernel(left, mid, right, fine, middle, r1_out, send_out, strip_out):
    source = planes_of(left, mid, right, 1, 11)
    error = {at: fine[4, at : at + 1, :] * source[at] for at in range(1, 11)}
    rest = {at: source[at] - fine_image(error, fine, at) for at in range(2, 10)}
    source1, error1 = {}, {}
    for plane in range(1, 5):
        value = pair_y(pair_z(rest[2 * plane] + rest[2 * plane + 1]))
        source1[plane] = value
        r1_out[plane - 1] = value[0:4]
        error1[plane] = middle[4, 2 * plane : 2 * plane + 1, :] * value
    low = sum(source1[plane] - middle_image(error1, middle, plane) for plane in (2, 3))
    low = quad_y(quad_z(low[:, OWN : OWN + 512]))
    both = jnp.concatenate([low[0:4, 0:128], low[0:4, 256:384]], axis=0)
    for target in range(send_out.shape[0]):
        send_out[target] = both
    for at in range(2):
        tiles = [error1[2 + at][0:4, 128 * t : 128 * t + 128] for t in range(1, 9)]
        lane = lanes_of(tiles[0])
        half, odd = lane // 64, lane % 2
        for group in range(2):
            a, b, c, d = tiles[4 * group : 4 * group + 4]
            value = jnp.where(half == 0, jnp.where(odd == 0, a, b), jnp.where(odd == 0, c, d))
            strip_out[at, 4 * group : 4 * group + 4, :] = value


def line_kernel(lines, got, coefs, strips, send_out, solved):
    at_x, at_y = lax.axis_index("gx"), lax.axis_index("gy")
    factors, previous, previous_factor, previous_link = [], None, None, None
    for source in range(lines // 2):
        rows = coefs[source, 13:15, :]
        turned = roll(rows, 64)
        first = lanes_of(rows) < 64
        for part in range(2):
            line = 2 * source + part
            value = jnp.where(first, rows, turned) if part == 0 else jnp.where(first, turned, rows)
            link, main = value[0:1], value[1:2]
            right = got[source, 4 * part : 4 * part + 4, :]
            solved[line, 4:8, :] = right
            if line == 0:
                scale = 1.0 / main
                update = scale * right
            else:
                scale = 1.0 / (main - previous_link * previous_factor)
                update = scale * (right + previous_link * previous)
            previous, previous_factor, previous_link = update, link * scale, link
            solved[line, 0:4, :] = update
            factors.append(previous_factor)
    for line in range(lines - 2, -1, -1):
        previous = solved[line, 0:4, :] + factors[line] * previous
        solved[line, 0:4, :] = previous
    packed = jnp.zeros((8, 128), jnp.float32)
    for place in range(8):
        line = 2 * at_y - 3 + place
        valid = (line >= 0) & (line < lines)
        value = solved[jnp.clip(line, 0, lines - 1)]
        packed = packed + jnp.where(spot_of(value, place) & valid, value, 0.0)
    for target in range(send_out.shape[0]):
        send_out[target, 0:8, :] = packed
        send_out[target, 8:16, :] = strips[(at_x >= target).astype(jnp.int32)]


def up_kernel(
    got, coefs, r1, left, mid, right, sums, fine_far, middle_far, basis_far,
    pre_out, send_out, fine, middle, vmat, fine_done, middle_done, basis_done,
):
    middle_copy = pltpu.make_async_copy(middle_far, middle, middle_done)
    fine_copy = pltpu.make_async_copy(fine_far, fine, fine_done)
    own = basis_far.at[:, :, OWN : OWN + 512]
    basis_copy = pltpu.make_async_copy(own, vmat, basis_done)
    middle_copy.start()
    fine_copy.start()
    basis_copy.start()
    at_x = lax.axis_index("gx")
    count = got.shape[0]
    error, source, links = {}, {}, {}
    for step in range(-3, 4):
        index = at_x + step
        valid = ((index >= 0) & (index < count)).astype(jnp.float32)
        kept = jnp.clip(index, 0, count - 1)
        rows = got[kept, 0:8, :] * valid
        error[step] = padded(rows[0:4])
        source[step] = padded(rows[4:8])
        near = coefs[kept] * valid
        links[step] = jnp.concatenate([unpacked_row(near, 0), near[13:16]], axis=0)
    lane = lanes_of(error[0])
    spot = lane % 4
    for reach in range(SWEEPS - 2, -1, -1):
        updated = dict(error)
        for step in range(-1 - reach, 2 + reach):
            here = error[step]
            sx, sy, sz, dg = (links[step][kind : kind + 1] for kind in range(4))
            up = jnp.where(spot < 3, roll(here, -1), roll(here, -61))
            flux = sy * here
            down = jnp.where(spot > 0, roll(flux, 1), roll(flux, 61))
            value = dg * here - sx * error[step + 1] - links[step - 1][0:1] * error[step - 1]
            value = value - sy * up - down - sz * roll(here, -4) - roll(sz * here, 4)
            updated[step] = here + relax_weight(dg) * (source[step] - value)
        error = updated
    blank = jnp.zeros((8, 128), jnp.float32)
    coarse = {}
    for step in range(-1, 2):
        tiles = []
        for place in range(2, 6):
            value = jnp.where(spot_of(error[step], place), error[step], 0.0)
            value = quad_z(pair_z(value))
            value = value + roll(value, 64)
            tiles += [value, value]
        coarse[step] = jnp.concatenate([blank] + tiles + [blank], axis=1)

    def strip(step):
        index = at_x + step
        valid = ((index >= 0) & (index < count)).astype(jnp.float32)
        rows = got[jnp.clip(index, 0, count - 1), 8:16, :] * valid
        tiles = []
        for group in range(2):
            part = padded(rows[4 * group : 4 * group + 4])
            for place in range(4):
                at = (lane // 64 == place // 2) & (lane % 2 == place % 2)
                value = pair_z(jnp.where(at, part, 0.0))
                tiles.append(value + roll(value, 64))
        return jnp.concatenate([blank] + tiles + [blank], axis=1)

    middle_copy.wait()
    error1, source1 = {0: strip(-1) + coarse[-1], 5: strip(1) + coarse[1]}, {}
    for plane in range(1, 5):
        source1[plane] = padded(r1[plane - 1])
        weight = middle[4, 2 * plane : 2 * plane + 1, :]
        error1[plane] = weight * source1[plane] + coarse[plane // 2 - 1]
    final1 = {}
    for plane in range(1, 5):
        weight = middle[4, 2 * plane : 2 * plane + 1, :]
        final1[plane] = error1[plane] + weight * (
            source1[plane] - middle_image(error1, middle, plane)
        )
    fine_copy.wait()
    lanes = slice(256, 1024)
    source0 = planes_of(left, mid, right, 2, 10)
    source0 = {at: value[:, lanes] for at, value in source0.items()}
    error0 = {
        at: fine[4, at : at + 1, lanes] * source0[at] + final1[at // 2][:, lanes]
        for at in range(2, 10)
    }
    final0 = {}
    for at in range(3, 9):
        weight = fine[4, at : at + 1, lanes]
        final0[at] = error0[at] + weight * (source0[at] - fine_image(error0, fine, at, lanes))
    basis_copy.wait()
    both = jnp.zeros((8, ROWS), jnp.float32)
    for at in range(4):
        own = slice(128, 640)
        value = final0[4 + at][0:4, own]
        pre_out[at] = value
        vmat[at, BASIS:ROWS, :] = value
        value = jnp.concatenate([value, fine_image(final0, fine, 4 + at, lanes)[0:4, own]], axis=0)
        both = both + dot_nt(value, vmat[at])
    now = jnp.concatenate([both, jnp.zeros((8, 128 - ROWS), jnp.float32)], axis=1)
    for target in range(send_out.shape[0]):
        send_out[target, 0:8, :] = now
        send_out[target, 8:16, :] = sums[...]


def eliminate(matrix, steps):
    row = lax.broadcasted_iota(jnp.int32, matrix.shape, 0)
    for step in range(steps):
        pivot = matrix[step : step + 1, :] / matrix[step : step + 1, step : step + 1]
        column = matrix[:, step : step + 1]
        matrix = matrix - jnp.where(row > step, column, 0.0) * pivot
    diagonal = jnp.where(lanes_of(matrix) == row, matrix, 0.0)
    diagonal = jnp.sum(diagonal, axis=1, keepdims=True)
    scale = lax.rsqrt(jnp.where(row[:, 0:1] < steps, diagonal, 1.0))
    return matrix * scale


def small_product(left, right, count):
    terms = [left[:, at : at + 1] * right[at : at + 1, :] for at in range(count)]
    while len(terms) > 1:
        terms = [sum(terms[at : at + 2]) for at in range(0, len(terms), 2)]
    return terms[0]


def ritz_kernel(
    cells, got, gathered, used, pre, basis_far, modes_out, dirs_out, ritz_out, corr_out,
    gram, field, basis_done,
):
    own = basis_far.at[:, :, OWN : OWN + 512]
    basis_copy = pltpu.make_async_copy(own, field, basis_done)
    basis_copy.start()
    total = got[0]
    for source in range(1, got.shape[0]):
        total = total + got[source]
    total = total / cells
    gram[80:128, :] = jnp.zeros((48, 128), jnp.float32)
    for source in range(16):
        gram[5 * source : 5 * source + 5, :] = gathered[source, 0:5, :]
    gram = gram[...] / cells
    shape = (16, 128)
    row = lax.broadcasted_iota(jnp.int32, shape, 0)
    lane = lax.broadcasted_iota(jnp.int32, shape, 1)
    zero4 = jnp.zeros((4, 128), jnp.float32)
    corr = jnp.where(used[0:4, :] > 0, total[0:4], 0.0)
    corr_out[...] = roll(corr, -8)[:, 0:LOCKED]
    locked_part = jnp.concatenate([zero4, -corr, zero4, zero4], axis=0)
    ones = ((row < 4) & (lane == row)) | ((row >= 8) & (row < 12) & (lane == row - 4))
    pre_ones = (row >= 4) & (row < 8) & (lane == row + 64)
    on_basis = jnp.where(ones, 1.0, locked_part)
    weights = jnp.where(pre_ones, 1.0, on_basis)
    pre_lane = (lane >= 68) & (lane < 72)

    def from_pre(part):
        rows4 = jnp.concatenate([zero4, part, zero4, zero4], axis=0)
        rows4 = jnp.where(lane < 72, rows4, 0.0)
        return jnp.where(pre_lane, 0.5 * rows4, rows4)

    products = dot_nn(jnp.concatenate([on_basis, locked_part], axis=0), gram)
    first = jnp.where(lane < 68, products[0:16], 0.0)
    second = roll(jnp.where(lane >= 68, products[16:32], 0.0), -60)
    pair = gram[72:80]
    pair = jnp.concatenate([pair[0:4], zero4, pair[4:8], zero4], axis=0)
    pair = jnp.where(lane < 68, jnp.where(lane < 8, 0.5 * pair, pair), 0.0)
    stacked = [0.5 * first + from_pre(total[0:4]), second + pair + from_pre(total[4:8])]
    stacked = jnp.concatenate(stacked, axis=0)
    straight = dot_nt(stacked, weights)
    turned = dot_nt(weights, stacked)
    mass = straight[0:16] + turned[:, 0:16]
    stiff = straight[16:32] + turned[:, 16:32]
    eye = jnp.where((row < 12) & (lane == row + 64), 1.0, 0.0)
    wide = jnp.zeros((16, 112), jnp.float32)
    mass = jnp.concatenate([mass, wide], axis=1)
    stiff = jnp.concatenate([stiff, wide], axis=1)
    done = eliminate(mass + roll(stiff, 32) + eye, 12)
    inside = (row < 12) & (lane < 12)
    half = jnp.where(inside, roll(done, -32), 0.0)
    inverse = jnp.where(inside, roll(done, -64), 0.0)
    reduced = dot_nt(half, inverse) + dot_nt(inverse, half)
    reduced = 0.5 * jnp.concatenate([reduced, wide], axis=1)
    top = jnp.sum(jnp.where(lane == row, reduced, 0.0), axis=(0, 1), keepdims=True)
    row8 = lax.broadcasted_iota(jnp.int32, (8, 128), 0)
    lane8 = lax.broadcasted_iota(jnp.int32, (8, 128), 1)
    first4 = row8 < 4
    basis_q = jnp.where(first4 & (lane8 == row8), 1.0, 0.0)
    for step in range(RITZ):
        raised = top * basis_q - small_product(basis_q, reduced, 12)
        joint = roll(raised, 32)
        for part in range(ACTIVE):
            column = jnp.sum(raised * raised[part : part + 1, :], axis=1, keepdims=True)
            joint = joint + jnp.where(lane8 == part, column, 0.0)
        basis_q = jnp.where(first4 & (lane8 < 12), roll(eliminate(joint, 4), -32), 0.0)
    ritz = jnp.sum(basis_q * small_product(basis_q, reduced, 12), axis=1, keepdims=True)
    for part in range(ACTIVE):
        ritz_out[part] = ritz[part, 0]
    coefs = small_product(basis_q, inverse, 12)
    tail = jnp.where(lane8 >= 4, coefs, 0.0)
    both = jnp.concatenate([coefs[0:4], tail[0:4]], axis=0)
    mix = small_product(both, weights, 12)[:, 0:ROWS]
    basis_copy.wait()
    for at in range(4):
        field[at, BASIS:ROWS, :] = pre[at]
        value = dot_nn(mix, field[at])
        for part in range(4):
            modes_out[part, at : at + 1, :] = value[part : part + 1]
            dirs_out[part, at : at + 1, :] = value[4 + part : 5 + part]


def pair_shift(low, high, axis):
    count = lax.axis_size(axis)
    forward = [(at, at + 1) for at in range(count - 1)]
    backward = [(at + 1, at) for at in range(count - 1)]
    above = lax.ppermute(low, axis, backward)
    return lax.ppermute(high, axis, forward), above


def spread(block, axis):
    count = lax.axis_size(axis)
    return lax.all_to_all(jnp.broadcast_to(block, (count,) + block.shape), axis, 0, 0)


def on_device(modes, directions, locked, perm_class, perm_table, locked_count):
    size_x, size_y = lax.axis_size("gx"), lax.axis_size("gy")
    lines = 2 * size_y
    cells = float(4 * 512 * size_x * size_y)
    basis, low, high = kernel_call(
        input_kernel, [(4, ROWS, 512), (4, ROWS, 384), (4, ROWS, 384)],
        perm_table, modes, directions, locked, perm_class, scalars=1, inputs=True,
    )
    low, high = pair_shift(low, high, "gy")
    basis = jnp.concatenate([low, basis, high], axis=2)
    conduct = basis[:, BASIS].reshape(10, 512)
    left, right = pair_shift(
        jnp.concatenate(
            [basis[0, 8:, OWN : OWN + 512], basis[0, :8].reshape(20, 512), conduct], 0
        ),
        jnp.concatenate([basis[3, :8].reshape(20, 512), conduct], 0),
        "gx",
    )
    fine, middle, image, used, send = kernel_call(
        functools.partial(coef_kernel, 4.0 / float(lines * lines)),
        [(5, 16, WIDE), (5, 16, WIDE), (4, 8, WIDE), (8, 128), (size_y, 16, 128)],
        locked_count, left[20:30].reshape(4, WIDE), right[84:94].reshape(4, WIDE), basis,
        left[:20].reshape(8, WIDE), right[64:84].reshape(8, WIDE), right[:64],
        scratch=[(16, WIDE), (128, 512), (80, 512), (5, 16, WIDE), (5, 16, WIDE)],
        scalars=1, far_out=(0, 1),
    )
    got_y = lax.all_to_all(send, "gy", 0, 0)
    (send,) = kernel_call(
        functools.partial(middle_kernel, lines), [(size_x, 16, 128)], got_y
    )
    got_x = lax.all_to_all(send, "gx", 0, 0)
    mid, sums = kernel_call(
        functools.partial(residual_kernel, cells), [(4, 4, WIDE), (8, 128)],
        got_x, used, image, basis,
        scratch=[(4, ROWS, WIDE)], far=(3,), copies=4,
    )
    left, right = pair_shift(mid[:3], mid[1:], "gx")
    r1, send, strips = kernel_call(
        down_kernel, [(4, 4, WIDE), (size_y, 8, 128), (2, 8, 128)], left, mid, right, fine, middle
    )
    (send,) = kernel_call(
        functools.partial(line_kernel, lines), [(size_x, 16, 128)],
        lax.all_to_all(send, "gy", 0, 0), got_y, strips,
        scratch=[(lines, 8, 128)],
    )
    precond, send = kernel_call(
        up_kernel, [(4, 4, 512), (size_y, 16, 128)],
        lax.all_to_all(send, "gx", 0, 0), got_x, r1, left, mid, right, sums, fine, middle, basis,
        scratch=[(5, 16, WIDE), (5, 16, WIDE), (4, ROWS, 512)], far=(7, 8, 9),
    )
    got_y = lax.all_to_all(send, "gy", 0, 0)
    got_x = spread(jnp.sum(got_y[:, :8], axis=0), "gx")
    new_modes, new_directions, ritz, corr = kernel_call(
        functools.partial(ritz_kernel, cells),
        [(4, 4, 512), (4, 4, 512), (4,), (4, LOCKED)],
        got_x, got_y[:, 8:], used, precond, basis,
        scratch=[(128, 128), (4, ROWS, 512)], far=(4,), results=True,
    )
    return (new_modes, new_directions, ritz, corr.T)


def solution(mesh):
    placed = (
        P(None, "gx", "gy"),
        P(None, "gx", "gy"),
        P(None, "gx", "gy"),
        P("gx", "gy"),
        P(),
        P(),
    )
    return jax.shard_map(
        on_device,
        mesh=mesh,
        in_specs=placed,
        out_specs=(P(None, "gx", "gy"), P(None, "gx", "gy"), P(), P()),
        check_vma=False,
    )
```

```python
import functools

import jax
import jax.numpy as jnp
from jax import lax
from jax.experimental import pallas as pl
from jax.experimental.pallas import tpu as pltpu
from jax.sharding import PartitionSpec as P

NZ = 64
ACTIVE = 4
LOCKED = 60
BASIS = 68
ROWS = 72
SWEEPS = 3
RITZ = 3
OMEGA = 0.6
EPSILON = 1e-06
PRECISE = lax.Precision.HIGHEST
WIDE = 1280
OWN = 384
INTERPRET = False


def kernel_call(
    body, out, *args, scratch=(), scalars=0, far=(), far_out=(), inputs=False, results=False,
    copies=0,
):
    specs, placed = [], []
    for at, value in enumerate(args):
        space = pltpu.SMEM if at < scalars else pl.ANY if at in far else pltpu.VMEM
        specs.append(pl.BlockSpec(memory_space=space))
        if space is pltpu.VMEM and not (inputs or INTERPRET):
            value = pltpu.with_memory_space_constraint(value, pltpu.VMEM)
        placed.append(value)
    shapes, stored = [], []
    for at, shape in enumerate(out):
        space = pltpu.SMEM if len(shape) == 1 else pl.ANY if at in far_out else pltpu.VMEM
        stored.append(pl.BlockSpec(memory_space=space))
        if space is pltpu.VMEM and not (results or INTERPRET):
            shapes.append(pltpu.VMEM(shape, jnp.float32))
        else:
            shapes.append(jax.ShapeDtypeStruct(shape, jnp.float32))
    copies = copies or len(far) + len(far_out)
    held = [pltpu.VMEM(shape, jnp.float32) for shape in scratch]
    held += [pltpu.SemaphoreType.DMA] * copies
    return pl.pallas_call(
        body,
        out_shape=shapes,
        in_specs=specs,
        out_specs=stored,
        scratch_shapes=held,
        interpret=INTERPRET,
    )(*placed)


def roll(value, shift, axis=1):
    return pltpu.roll(value, shift % value.shape[axis], axis)


def lanes_of(value):
    rows, lanes = value.shape
    tile = lax.broadcasted_iota(jnp.int32, (rows, 128), 1)
    return jnp.concatenate([tile] * (lanes // 128), axis=1)


def pair_z(value):
    even = lanes_of(value) % 2 == 0
    return value + jnp.where(even, roll(value, -1), roll(value, 1))


def pair_y(value):
    first = lanes_of(value) % 128 < 64
    return value + jnp.where(first, roll(value, -64), roll(value, 64))


def quad_z(value):
    first = lanes_of(value) % 4 < 2
    return value + jnp.where(first, roll(value, -2), roll(value, 2))


def quad_y(value):
    first = (lax.broadcasted_iota(jnp.int32, value.shape, 1) // 128) % 2 == 0
    return value + jnp.where(first, roll(value, -128), roll(value, 128))


def dot_nt(left, right):
    return lax.dot_general(
        left, right, (((1,), (1,)), ((), ())), precision=PRECISE, preferred_element_type=jnp.float32
    )


def dot_nn(left, right):
    return lax.dot_general(
        left, right, (((1,), (0,)), ((), ())), precision=PRECISE, preferred_element_type=jnp.float32
    )


def relax_weight(diagonal):
    inside = diagonal > 0
    return jnp.where(inside, OMEGA * pl.reciprocal(jnp.where(inside, diagonal, 1.0)), 0.0)


def joined(here, there):
    both = (here > 0) & (there > 0)
    scale = pl.reciprocal(jnp.where(both, here + there, 1.0))
    return jnp.where(both, 2.0 * here * there * scale, 0.0)


def face(coupling, here, there):
    return coupling + jnp.where(there > 0, 0.0, 2.0 * here)


def input_kernel(table, modes, directions, locked, kinds, basis, low_out, high_out):
    value = jnp.zeros((4, 512), jnp.float32)
    kind = kinds[...]
    for at in range(table.shape[0]):
        value = jnp.where(kind == at, table[at], value)
    for at in range(4):
        basis[at, 0:4, :] = modes[:, at, :]
        basis[at, 4:8, :] = directions[:, at, :]
        basis[at, 8:BASIS, :] = locked[:, at, :]
        basis[at, BASIS:ROWS, :] = jnp.zeros((ROWS - BASIS, 512), jnp.float32)
        basis[at, BASIS : BASIS + 1, :] = value[at : at + 1]
        low_out[at] = basis[at, :, 0:384]
        high_out[at] = basis[at, :, 128:512]


def coef_kernel(
    shift, count, cond_left, cond_right, basis, left, right, locked_right,
    fine_far, middle_far, image_out, used_out, send_out, cond, vmat, umat, fine_out, middle_out,
    fine_done, middle_done,
):
    used = lanes_of(used_out)
    used_out[...] = jnp.where((used >= 8) & (used < 8 + count[0]), 1.0, 0.0)
    cond[0:4, :] = cond_left[...]
    for at in range(4):
        cond[4 + at : 5 + at, :] = basis[at, BASIS : BASIS + 1, :]
    cond[8:12, :] = cond_right[...]
    cond[12:16, :] = jnp.zeros((4, WIDE), jnp.float32)
    here = cond[...]
    z_at = lanes_of(here) % 64
    x_next, x_prev = roll(here, -1, 0), roll(here, 1, 0)
    y_next, y_prev = roll(here, -64), roll(here, 64)
    z_next = jnp.where(z_at < 63, roll(here, -1), 0.0)
    z_prev = jnp.where(z_at > 0, roll(here, 1), 0.0)
    tx, ty, tz = joined(here, x_next), joined(here, y_next), joined(here, z_next)
    y_faces = face(ty, here, y_next) + face(roll(ty, 64), here, y_prev)
    diagonal = face(tx, here, x_next) + face(roll(tx, 1, 0), here, x_prev) + y_faces
    diagonal = diagonal + face(tz, here, z_next) + face(roll(tz, 1), here, z_prev)
    for at, value in enumerate((diagonal, tx, ty, tz, relax_weight(diagonal))):
        fine_out[at] = value

    def pairs(value):
        return pair_y(pair_z(value))

    def pair_x(value):
        return value + roll(value, -1, 0)

    lower_y, lower_z = lanes_of(here) % 128 < 64, z_at % 2 == 0
    inner = jnp.where(lower_y, ty, 0.0)
    sum_x = pairs(tx)
    ty1 = pair_x(pairs(ty - inner))
    tz1 = pair_x(pairs(jnp.where(lower_z, 0.0, tz)))
    tx1 = roll(sum_x, -1, 0)
    diagonal1 = pair_x(pairs(diagonal - 2.0 * (inner + jnp.where(lower_z, tz, 0.0))))
    diagonal1 = diagonal1 - 2.0 * sum_x
    for at, value in enumerate((diagonal1, tx1, ty1, tz1, relax_weight(diagonal1))):
        middle_out[at] = value
    fine_copy = pltpu.make_async_copy(fine_out, fine_far, fine_done)
    middle_copy = pltpu.make_async_copy(middle_out, middle_far, middle_done)
    fine_copy.start()
    middle_copy.start()

    def own(value):
        return value[0:8, OWN : OWN + 512]

    def quads(value):
        value = quad_y(quad_z(value))
        return value[4:5] + value[6:7]

    y_faces1 = pair_x(pairs(own(y_faces - 2.0 * inner)))
    tx1, ty1, tz1, diagonal1 = own(tx1), own(ty1), own(tz1), own(diagonal1)
    lane = lanes_of(tx1)
    lower_y = (lax.broadcasted_iota(jnp.int32, tx1.shape, 1) // 128) % 2 == 0
    lower_z = lane % 4 < 2
    inner = jnp.where(lower_y, ty1, 0.0)
    across = quad_y(quad_z(tx1))
    tx2 = across[6:7]
    ty2 = quads(ty1 - inner)
    tz2 = quads(jnp.where(lower_z, 0.0, tz1))
    diagonal2 = quads(diagonal1 - 2.0 * (inner + jnp.where(lower_z, tz1, 0.0)))
    diagonal2 = diagonal2 - 2.0 * across[4:5]
    y_faces2 = quads(y_faces1 - 2.0 * inner)
    line2 = y_faces2 + shift * (diagonal2 - y_faces2)
    coarse = []
    for value in (tx2, ty2, tz2, diagonal2, line2):
        first, second = value[:, 0:128], value[:, 256:384]
        coarse.append(jnp.where(lanes_of(first) < 64, first, second))

    gram = jnp.zeros((80, 128), jnp.float32)
    for at in range(4):
        plane = 4 + at
        row = slice(plane, plane + 1)
        wide = basis[at, 0:8, :]
        after = right[...] if at == 3 else basis[at + 1, 0:8, :]
        before = left[...] if at == 0 else basis[at - 1, 0:8, :]
        dg, sx, sy, sz = (fine_out[kind, row, :] for kind in range(4))
        image = dg * wide - sy * roll(wide, -64) - roll(sy * wide, 64)
        image = image - sz * roll(wide, -1) - roll(sz * wide, 1)
        image = image - sx * after - fine_out[1, plane - 1 : plane, :] * before
        image_out[at] = image
        image = image[:, OWN : OWN + 512]
        wide = basis[at, 8:ROWS, OWN:1024]
        after = locked_right[...] if at == 3 else basis[at + 1, 8:ROWS, OWN : OWN + 512]
        dg, sx, sy, sz = (fine_out[kind, row, OWN:1024] for kind in range(4))
        half = (0.5 * dg) * wide - sy * roll(wide, -64) - sz * roll(wide, -1)
        half = half[:, 0:512] - sx[:, 0:512] * after
        vmat[0:72, :] = basis[at, :, OWN : OWN + 512]
        vmat[68:128, :] = half[0:60]
        umat[0:72, :] = basis[at, :, OWN : OWN + 512]
        umat[72:80, :] = image
        gram = gram + dot_nt(umat[...], vmat[...])
    now = packed_rows(jnp.concatenate([gram[0:4], gram[72:76]], axis=0), [coarse[0], coarse[2]])
    rest = jnp.concatenate([coarse[1], coarse[4], coarse[3]], axis=0)
    for target in range(send_out.shape[0]):
        send_out[target, 0:8, :] = now
        send_out[target, 8:13, :] = gram[5 * target : 5 * target + 5]
        send_out[target, 13:16, :] = rest
    fine_copy.wait()
    middle_copy.wait()


def packed_rows(rows, extra):
    lane = lanes_of(rows)
    row = lax.broadcasted_iota(jnp.int32, rows.shape, 0)
    for at, value in enumerate(extra):
        for part in range(4):
            moved = roll(value, 96 - 32 * part)
            rows = jnp.where((row == 4 * at + part) & (lane >= 96), moved, rows)
    return rows


def unpacked_row(rows, at):
    lane = lanes_of(rows[0:1])
    value = roll(rows[4 * at : 4 * at + 1], -96)
    for part in range(1, 4):
        moved = roll(rows[4 * at + part : 4 * at + part + 1], 32 * part - 96)
        value = jnp.where(lane // 32 == part, moved, value)
    return value


def half_of(value, half, wanted):
    return value if half == wanted else roll(value, 64)


def spot_of(value, place):
    lane = lanes_of(value)
    return (lane // 64 == place // 4) & (lane % 4 == place % 4)


def middle_kernel(lines, got, send_out):
    at_y = lax.axis_index("gy")
    total = got[0]
    for source in range(1, got.shape[0]):
        total = total + got[source]
    packed = jnp.zeros((4, 128), jnp.float32)
    for place in range(8):
        source = at_y + (place - 3) // 2
        valid = (source >= 0) & (source < lines // 2)
        value = got[jnp.clip(source, 0, lines // 2 - 1)]
        tx, tz = unpacked_row(value, 0), unpacked_row(value, 1)
        value = jnp.concatenate([tx, value[13:14], tz, value[15:16]], axis=0)
        value = half_of(value, (place - 3) % 2, place // 4)
        packed = packed + jnp.where(spot_of(value, place) & valid, value, 0.0)
    now = packed_rows(total[0:8], [packed[0:1]])
    for target in range(send_out.shape[0]):
        send_out[target, 0:8, :] = now
        send_out[target, 8:13, :] = total[8:13]
        send_out[target, 13:16, :] = packed[1:4]


def residual_kernel(cells, got, used, image, basis, res_out, sums_out):
    total = got[0]
    for source in range(1, got.shape[0]):
        total = total + got[source]
    sums_out[...] = total[8:16]
    overlap, energy = total[0:4], total[4:8]
    lane = lanes_of(overlap)
    own = lane == lax.broadcasted_iota(jnp.int32, overlap.shape, 0)
    norm = jnp.sum(jnp.where(own, overlap, 0.0), axis=1, keepdims=True)
    top = jnp.sum(jnp.where(own, energy, 0.0), axis=1, keepdims=True)
    quotient = top / cells / (norm / cells + EPSILON)
    coupling = (energy - quotient * overlap) / cells
    weights = jnp.where(used[0:4, :] > 0, coupling, 0.0)
    weights = jnp.concatenate([weights, jnp.zeros((4, 128), jnp.float32)], axis=0)
    for at in range(4):
        field = basis[at]
        value = image[at, 0:4, :] - quotient * field[0:4]
        res_out[at] = value - dot_nn(weights[:, 0:ROWS], field)[0:4]


def padded(value):
    return jnp.concatenate([value, jnp.zeros(value.shape, jnp.float32)], axis=0)


def apply_at(values, coefs, row, row_step, at, y_step, z_step, lanes):
    here = values[at]
    dg, sx, sy, sz = (coefs[kind, row : row + 1, lanes] for kind in range(4))
    before = coefs[1, row - row_step : row - row_step + 1, lanes]
    image = dg * here - sx * values[at + 1] - before * values[at - 1]
    image = image - sy * roll(here, -y_step) - roll(sy * here, y_step)
    return image - sz * roll(here, -z_step) - roll(sz * here, z_step)


def fine_image(values, fine, plane, lanes=slice(0, WIDE)):
    return apply_at(values, fine, plane, 1, plane, 64, 1, lanes)


def middle_image(values, middle, plane):
    return apply_at(values, middle, 2 * plane, 2, plane, 128, 2, slice(0, WIDE))


def planes_of(left, mid, right, first, last):
    parts = [left[at] for at in range(3)] + [mid[at] for at in range(4)]
    parts += [right[at] for at in range(3)]
    return {at: padded(parts[at - 1]) for at in range(first, last)}


def down_kernel(left, mid, right, fine, middle, r1_out, send_out, strip_out):
    source = planes_of(left, mid, right, 1, 11)
    error = {at: fine[4, at : at + 1, :] * source[at] for at in range(1, 11)}
    rest = {at: source[at] - fine_image(error, fine, at) for at in range(2, 10)}
    source1, error1 = {}, {}
    for plane in range(1, 5):
        value = pair_y(pair_z(rest[2 * plane] + rest[2 * plane + 1]))
        source1[plane] = value
        r1_out[plane - 1] = value[0:4]
        error1[plane] = middle[4, 2 * plane : 2 * plane + 1, :] * value
    low = sum(source1[plane] - middle_image(error1, middle, plane) for plane in (2, 3))
    low = quad_y(quad_z(low[:, OWN : OWN + 512]))
    both = jnp.concatenate([low[0:4, 0:128], low[0:4, 256:384]], axis=0)
    for target in range(send_out.shape[0]):
        send_out[target] = both
    for at in range(2):
        tiles = [error1[2 + at][0:4, 128 * t : 128 * t + 128] for t in range(1, 9)]
        lane = lanes_of(tiles[0])
        half, odd = lane // 64, lane % 2
        for group in range(2):
            a, b, c, d = tiles[4 * group : 4 * group + 4]
            value = jnp.where(half == 0, jnp.where(odd == 0, a, b), jnp.where(odd == 0, c, d))
            strip_out[at, 4 * group : 4 * group + 4, :] = value


def line_kernel(lines, got, coefs, strips, send_out, solved):
    at_x, at_y = lax.axis_index("gx"), lax.axis_index("gy")
    factors, previous, previous_factor, previous_link = [], None, None, None
    for source in range(lines // 2):
        rows = coefs[source, 13:15, :]
        turned = roll(rows, 64)
        first = lanes_of(rows) < 64
        for part in range(2):
            line = 2 * source + part
            value = jnp.where(first, rows, turned) if part == 0 else jnp.where(first, turned, rows)
            link, main = value[0:1], value[1:2]
            right = got[source, 4 * part : 4 * part + 4, :]
            solved[line, 4:8, :] = right
            if line == 0:
                scale = pl.reciprocal(main)
                update = scale * right
            else:
                scale = pl.reciprocal(main - previous_link * previous_factor)
                update = scale * (right + previous_link * previous)
            previous, previous_factor, previous_link = update, link * scale, link
            solved[line, 0:4, :] = update
            factors.append(previous_factor)
    for line in range(lines - 2, -1, -1):
        previous = solved[line, 0:4, :] + factors[line] * previous
        solved[line, 0:4, :] = previous
    packed = jnp.zeros((8, 128), jnp.float32)
    for place in range(8):
        line = 2 * at_y - 3 + place
        valid = (line >= 0) & (line < lines)
        value = solved[jnp.clip(line, 0, lines - 1)]
        packed = packed + jnp.where(spot_of(value, place) & valid, value, 0.0)
    for target in range(send_out.shape[0]):
        send_out[target, 0:8, :] = packed
        send_out[target, 8:16, :] = strips[(at_x >= target).astype(jnp.int32)]


def up_kernel(
    got, coefs, r1, left, mid, right, sums, fine_far, middle_far, basis_far,
    pre_out, send_out, fine, middle, vmat, fine_done, middle_done, basis_done,
):
    middle_copy = pltpu.make_async_copy(middle_far, middle, middle_done)
    fine_copy = pltpu.make_async_copy(fine_far, fine, fine_done)
    own = basis_far.at[:, :, OWN : OWN + 512]
    basis_copy = pltpu.make_async_copy(own, vmat, basis_done)
    middle_copy.start()
    fine_copy.start()
    basis_copy.start()
    at_x = lax.axis_index("gx")
    count = got.shape[0]
    error, source, links = {}, {}, {}
    for step in range(-3, 4):
        index = at_x + step
        valid = ((index >= 0) & (index < count)).astype(jnp.float32)
        kept = jnp.clip(index, 0, count - 1)
        rows = got[kept, 0:8, :] * valid
        error[step] = padded(rows[0:4])
        source[step] = padded(rows[4:8])
        near = coefs[kept] * valid
        links[step] = jnp.concatenate([unpacked_row(near, 0), near[13:16]], axis=0)
    lane = lanes_of(error[0])
    spot = lane % 4
    for reach in range(SWEEPS - 2, -1, -1):
        updated = dict(error)
        for step in range(-1 - reach, 2 + reach):
            here = error[step]
            sx, sy, sz, dg = (links[step][kind : kind + 1] for kind in range(4))
            up = jnp.where(spot < 3, roll(here, -1), roll(here, -61))
            flux = sy * here
            down = jnp.where(spot > 0, roll(flux, 1), roll(flux, 61))
            value = dg * here - sx * error[step + 1] - links[step - 1][0:1] * error[step - 1]
            value = value - sy * up - down - sz * roll(here, -4) - roll(sz * here, 4)
            updated[step] = here + relax_weight(dg) * (source[step] - value)
        error = updated
    blank = jnp.zeros((8, 128), jnp.float32)
    coarse = {}
    for step in range(-1, 2):
        tiles = []
        for place in range(2, 6):
            value = jnp.where(spot_of(error[step], place), error[step], 0.0)
            value = quad_z(pair_z(value))
            value = value + roll(value, 64)
            tiles += [value, value]
        coarse[step] = jnp.concatenate([blank] + tiles + [blank], axis=1)

    def strip(step):
        index = at_x + step
        valid = ((index >= 0) & (index < count)).astype(jnp.float32)
        rows = got[jnp.clip(index, 0, count - 1), 8:16, :] * valid
        tiles = []
        for group in range(2):
            part = padded(rows[4 * group : 4 * group + 4])
            for place in range(4):
                at = (lane // 64 == place // 2) & (lane % 2 == place % 2)
                value = pair_z(jnp.where(at, part, 0.0))
                tiles.append(value + roll(value, 64))
        return jnp.concatenate([blank] + tiles + [blank], axis=1)

    middle_copy.wait()
    error1, source1 = {0: strip(-1) + coarse[-1], 5: strip(1) + coarse[1]}, {}
    for plane in range(1, 5):
        source1[plane] = padded(r1[plane - 1])
        weight = middle[4, 2 * plane : 2 * plane + 1, :]
        error1[plane] = weight * source1[plane] + coarse[plane // 2 - 1]
    final1 = {}
    for plane in range(1, 5):
        weight = middle[4, 2 * plane : 2 * plane + 1, :]
        final1[plane] = error1[plane] + weight * (
            source1[plane] - middle_image(error1, middle, plane)
        )
    fine_copy.wait()
    lanes = slice(256, 1024)
    source0 = planes_of(left, mid, right, 2, 10)
    source0 = {at: value[:, lanes] for at, value in source0.items()}
    error0 = {
        at: fine[4, at : at + 1, lanes] * source0[at] + final1[at // 2][:, lanes]
        for at in range(2, 10)
    }
    final0 = {}
    for at in range(3, 9):
        weight = fine[4, at : at + 1, lanes]
        final0[at] = error0[at] + weight * (source0[at] - fine_image(error0, fine, at, lanes))
    basis_copy.wait()
    both = jnp.zeros((8, ROWS), jnp.float32)
    for at in range(4):
        own = slice(128, 640)
        value = final0[4 + at][0:4, own]
        pre_out[at] = value
        vmat[at, BASIS:ROWS, :] = value
        value = jnp.concatenate([value, fine_image(final0, fine, 4 + at, lanes)[0:4, own]], axis=0)
        both = both + dot_nt(value, vmat[at])
    now = jnp.concatenate([both, jnp.zeros((8, 128 - ROWS), jnp.float32)], axis=1)
    for target in range(send_out.shape[0]):
        send_out[target, 0:8, :] = now
        send_out[target, 8:16, :] = sums[...]


def eliminate(matrix, steps):
    row = lax.broadcasted_iota(jnp.int32, matrix.shape, 0)
    for start in range(0, steps, 4):
        columns = [
            jnp.broadcast_to(matrix[:, at : at + 1], matrix.shape) for at in range(start, start + 4)
        ]
        for part in range(4):
            step = start + part
            column = columns[part]
            factor = jnp.where(row > step, column * pl.reciprocal(column[step : step + 1, :]), 0.0)
            matrix = matrix - factor * matrix[step : step + 1, :]
            for other in range(part + 1, 4):
                value = columns[other]
                columns[other] = value - factor * value[step : step + 1, :]
    diagonal = jnp.where(lanes_of(matrix) == row, matrix, 0.0)
    diagonal = jnp.sum(diagonal, axis=1, keepdims=True)
    scale = lax.rsqrt(jnp.where(row[:, 0:1] < steps, diagonal, 1.0))
    return matrix * scale


def small_product(left, right, count):
    terms = [left[:, at : at + 1] * right[at : at + 1, :] for at in range(count)]
    while len(terms) > 1:
        terms = [sum(terms[at : at + 2]) for at in range(0, len(terms), 2)]
    return terms[0]


def ritz_kernel(
    cells, got, gathered, used, pre, basis_far, modes_out, dirs_out, ritz_out, corr_out,
    gram, field, basis_done,
):
    own = basis_far.at[:, :, OWN : OWN + 512]
    basis_copy = pltpu.make_async_copy(own, field, basis_done)
    basis_copy.start()
    total = got[0]
    for source in range(1, got.shape[0]):
        total = total + got[source]
    total = total / cells
    gram[80:128, :] = jnp.zeros((48, 128), jnp.float32)
    for source in range(16):
        gram[5 * source : 5 * source + 5, :] = gathered[source, 0:5, :]
    gram = gram[...] / cells
    shape = (16, 128)
    row = lax.broadcasted_iota(jnp.int32, shape, 0)
    lane = lax.broadcasted_iota(jnp.int32, shape, 1)
    zero4 = jnp.zeros((4, 128), jnp.float32)
    corr = jnp.where(used[0:4, :] > 0, total[0:4], 0.0)
    corr_out[...] = roll(corr, -8)[:, 0:LOCKED]
    locked_part = jnp.concatenate([zero4, -corr, zero4, zero4], axis=0)
    ones = ((row < 4) & (lane == row)) | ((row >= 8) & (row < 12) & (lane == row - 4))
    pre_ones = (row >= 4) & (row < 8) & (lane == row + 64)
    on_basis = jnp.where(ones, 1.0, locked_part)
    weights = jnp.where(pre_ones, 1.0, on_basis)
    pre_lane = (lane >= 68) & (lane < 72)

    def from_pre(part):
        rows4 = jnp.concatenate([zero4, part, zero4, zero4], axis=0)
        rows4 = jnp.where(lane < 72, rows4, 0.0)
        return jnp.where(pre_lane, 0.5 * rows4, rows4)

    products = dot_nn(jnp.concatenate([on_basis, locked_part], axis=0), gram)
    first = jnp.where(lane < 68, products[0:16], 0.0)
    second = roll(jnp.where(lane >= 68, products[16:32], 0.0), -60)
    pair = gram[72:80]
    pair = jnp.concatenate([pair[0:4], zero4, pair[4:8], zero4], axis=0)
    pair = jnp.where(lane < 68, jnp.where(lane < 8, 0.5 * pair, pair), 0.0)
    stacked = [0.5 * first + from_pre(total[0:4]), second + pair + from_pre(total[4:8])]
    stacked = jnp.concatenate(stacked, axis=0)
    straight = dot_nt(stacked, weights)
    turned = dot_nt(weights, stacked)
    mass = straight[0:16] + turned[:, 0:16]
    stiff = straight[16:32] + turned[:, 16:32]
    eye = jnp.where((row < 12) & (lane == row + 64), 1.0, 0.0)
    wide = jnp.zeros((16, 112), jnp.float32)
    mass = jnp.concatenate([mass, wide], axis=1)
    stiff = jnp.concatenate([stiff, wide], axis=1)
    done = eliminate(mass + roll(stiff, 32) + eye, 12)
    inside = (row < 12) & (lane < 12)
    half = jnp.where(inside, roll(done, -32), 0.0)
    inverse = jnp.where(inside, roll(done, -64), 0.0)
    reduced = dot_nt(half, inverse) + dot_nt(inverse, half)
    reduced = 0.5 * jnp.concatenate([reduced, wide], axis=1)
    top = jnp.sum(jnp.where(lane == row, reduced, 0.0), axis=(0, 1), keepdims=True)
    row8 = lax.broadcasted_iota(jnp.int32, (8, 128), 0)
    lane8 = lax.broadcasted_iota(jnp.int32, (8, 128), 1)
    first4 = row8 < 4
    basis_q = jnp.where(first4 & (lane8 == row8), 1.0, 0.0)
    for step in range(RITZ):
        raised = top * basis_q - small_product(basis_q, reduced, 12)
        joint = roll(raised, 32)
        for part in range(ACTIVE):
            column = jnp.sum(raised * raised[part : part + 1, :], axis=1, keepdims=True)
            joint = joint + jnp.where(lane8 == part, column, 0.0)
        basis_q = jnp.where(first4 & (lane8 < 12), roll(eliminate(joint, 4), -32), 0.0)
    ritz = jnp.sum(basis_q * small_product(basis_q, reduced, 12), axis=1, keepdims=True)
    for part in range(ACTIVE):
        ritz_out[part] = ritz[part, 0]
    coefs = small_product(basis_q, inverse, 12)
    tail = jnp.where(lane8 >= 4, coefs, 0.0)
    both = jnp.concatenate([coefs[0:4], tail[0:4]], axis=0)
    mix = small_product(both, weights, 12)[:, 0:ROWS]
    basis_copy.wait()
    for at in range(4):
        field[at, BASIS:ROWS, :] = pre[at]
        value = dot_nn(mix, field[at])
        for part in range(4):
            modes_out[part, at : at + 1, :] = value[part : part + 1]
            dirs_out[part, at : at + 1, :] = value[4 + part : 5 + part]


def pair_shift(low, high, axis):
    count = lax.axis_size(axis)
    forward = [(at, at + 1) for at in range(count - 1)]
    backward = [(at + 1, at) for at in range(count - 1)]
    above = lax.ppermute(low, axis, backward)
    return lax.ppermute(high, axis, forward), above


def spread(block, axis):
    count = lax.axis_size(axis)
    return lax.all_to_all(jnp.broadcast_to(block, (count,) + block.shape), axis, 0, 0)


def on_device(modes, directions, locked, perm_class, perm_table, locked_count):
    size_x, size_y = lax.axis_size("gx"), lax.axis_size("gy")
    lines = 2 * size_y
    cells = float(4 * 512 * size_x * size_y)
    basis, low, high = kernel_call(
        input_kernel, [(4, ROWS, 512), (4, ROWS, 384), (4, ROWS, 384)],
        perm_table, modes, directions, locked, perm_class, scalars=1, inputs=True,
    )
    low, high = pair_shift(low, high, "gy")
    basis = jnp.concatenate([low, basis, high], axis=2)
    conduct = basis[:, BASIS].reshape(10, 512)
    left, right = pair_shift(
        jnp.concatenate(
            [basis[0, 8:, OWN : OWN + 512], basis[0, :8].reshape(20, 512), conduct], 0
        ),
        jnp.concatenate([basis[3, :8].reshape(20, 512), conduct], 0),
        "gx",
    )
    fine, middle, image, used, send = kernel_call(
        functools.partial(coef_kernel, 4.0 / float(lines * lines)),
        [(5, 16, WIDE), (5, 16, WIDE), (4, 8, WIDE), (8, 128), (size_y, 16, 128)],
        locked_count, left[20:30].reshape(4, WIDE), right[84:94].reshape(4, WIDE), basis,
        left[:20].reshape(8, WIDE), right[64:84].reshape(8, WIDE), right[:64],
        scratch=[(16, WIDE), (128, 512), (80, 512), (5, 16, WIDE), (5, 16, WIDE)],
        scalars=1, far_out=(0, 1),
    )
    got_y = lax.all_to_all(send, "gy", 0, 0)
    (send,) = kernel_call(
        functools.partial(middle_kernel, lines), [(size_x, 16, 128)], got_y
    )
    got_x = lax.all_to_all(send, "gx", 0, 0)
    mid, sums = kernel_call(
        functools.partial(residual_kernel, cells), [(4, 4, WIDE), (8, 128)],
        got_x, used, image, basis,
    )
    left, right = pair_shift(mid[:3], mid[1:], "gx")
    r1, send, strips = kernel_call(
        down_kernel, [(4, 4, WIDE), (size_y, 8, 128), (2, 8, 128)], left, mid, right, fine, middle
    )
    (send,) = kernel_call(
        functools.partial(line_kernel, lines), [(size_x, 16, 128)],
        lax.all_to_all(send, "gy", 0, 0), got_y, strips,
        scratch=[(lines, 8, 128)],
    )
    precond, send = kernel_call(
        up_kernel, [(4, 4, 512), (size_y, 16, 128)],
        lax.all_to_all(send, "gx", 0, 0), got_x, r1, left, mid, right, sums, fine, middle, basis,
        scratch=[(5, 16, WIDE), (5, 16, WIDE), (4, ROWS, 512)], far=(7, 8, 9),
    )
    got_y = lax.all_to_all(send, "gy", 0, 0)
    got_x = spread(jnp.sum(got_y[:, :8], axis=0), "gx")
    new_modes, new_directions, ritz, corr = kernel_call(
        functools.partial(ritz_kernel, cells),
        [(4, 4, 512), (4, 4, 512), (4,), (4, LOCKED)],
        got_x, got_y[:, 8:], used, precond, basis,
        scratch=[(128, 128), (4, ROWS, 512)], far=(4,), results=True,
    )
    return (new_modes, new_directions, ritz, corr.T)


def solution(mesh):
    placed = (
        P(None, "gx", "gy"),
        P(None, "gx", "gy"),
        P(None, "gx", "gy"),
        P("gx", "gy"),
        P(),
        P(),
    )
    return jax.shard_map(
        on_device,
        mesh=mesh,
        in_specs=placed,
        out_specs=(P(None, "gx", "gy"), P(None, "gx", "gy"), P(), P()),
        check_vma=False,
    )
```

```python
import functools

import jax
import jax.numpy as jnp
from jax import lax
from jax.experimental import pallas as pl
from jax.experimental.pallas import tpu as pltpu
from jax.sharding import PartitionSpec as P

NZ = 64
ACTIVE = 4
LOCKED = 60
BASIS = 68
ROWS = 72
SWEEPS = 3
RITZ = 3
OMEGA = 0.6
EPSILON = 1e-06
PRECISE = lax.Precision.HIGHEST
WIDE = 1280
OWN = 384
INTERPRET = False


def kernel_call(
    body, out, *args, scratch=(), scalars=0, far=(), far_out=(), inputs=False, results=False,
    copies=0,
):
    specs, placed = [], []
    for at, value in enumerate(args):
        space = pltpu.SMEM if at < scalars else pl.ANY if at in far else pltpu.VMEM
        specs.append(pl.BlockSpec(memory_space=space))
        if space is pltpu.VMEM and not (inputs or INTERPRET):
            value = pltpu.with_memory_space_constraint(value, pltpu.VMEM)
        placed.append(value)
    shapes, stored = [], []
    for at, shape in enumerate(out):
        space = pltpu.SMEM if len(shape) == 1 else pl.ANY if at in far_out else pltpu.VMEM
        stored.append(pl.BlockSpec(memory_space=space))
        if space is pltpu.VMEM and not (results or INTERPRET):
            shapes.append(pltpu.VMEM(shape, jnp.float32))
        else:
            shapes.append(jax.ShapeDtypeStruct(shape, jnp.float32))
    copies = copies or len(far) + len(far_out)
    held = [pltpu.VMEM(shape, jnp.float32) for shape in scratch]
    held += [pltpu.SemaphoreType.DMA] * copies
    return pl.pallas_call(
        body,
        out_shape=shapes,
        in_specs=specs,
        out_specs=stored,
        scratch_shapes=held,
        interpret=INTERPRET,
    )(*placed)


def roll(value, shift, axis=1):
    return pltpu.roll(value, shift % value.shape[axis], axis)


def lanes_of(value):
    rows, lanes = value.shape
    tile = lax.broadcasted_iota(jnp.int32, (rows, 128), 1)
    return jnp.concatenate([tile] * (lanes // 128), axis=1)


def pair_z(value):
    even = lanes_of(value) % 2 == 0
    return value + jnp.where(even, roll(value, -1), roll(value, 1))


def pair_y(value):
    first = lanes_of(value) % 128 < 64
    return value + jnp.where(first, roll(value, -64), roll(value, 64))


def quad_z(value):
    first = lanes_of(value) % 4 < 2
    return value + jnp.where(first, roll(value, -2), roll(value, 2))


def quad_y(value):
    first = (lax.broadcasted_iota(jnp.int32, value.shape, 1) // 128) % 2 == 0
    return value + jnp.where(first, roll(value, -128), roll(value, 128))


def dot_nt(left, right):
    return lax.dot_general(
        left, right, (((1,), (1,)), ((), ())), precision=PRECISE, preferred_element_type=jnp.float32
    )


def dot_nn(left, right):
    return lax.dot_general(
        left, right, (((1,), (0,)), ((), ())), precision=PRECISE, preferred_element_type=jnp.float32
    )


def relax_weight(diagonal):
    inside = diagonal > 0
    return jnp.where(inside, OMEGA * pl.reciprocal(jnp.where(inside, diagonal, 1.0)), 0.0)


def joined(here, there):
    both = (here > 0) & (there > 0)
    scale = pl.reciprocal(jnp.where(both, here + there, 1.0))
    return jnp.where(both, 2.0 * here * there * scale, 0.0)


def face(coupling, here, there):
    return coupling + jnp.where(there > 0, 0.0, 2.0 * here)


def input_kernel(table, modes, directions, locked, kinds, basis, low_out, high_out):
    value = jnp.zeros((4, 512), jnp.float32)
    kind = kinds[...]
    for at in range(table.shape[0]):
        value = jnp.where(kind == at, table[at], value)
    for at in range(4):
        basis[at, 0:4, :] = modes[:, at, :]
        basis[at, 4:8, :] = directions[:, at, :]
        basis[at, 8:BASIS, :] = locked[:, at, :]
        basis[at, BASIS:ROWS, :] = jnp.zeros((ROWS - BASIS, 512), jnp.float32)
        basis[at, BASIS : BASIS + 1, :] = value[at : at + 1]
        low_out[at] = basis[at, :, 0:384]
        high_out[at] = basis[at, :, 128:512]


def coef_kernel(
    shift, count, cond_left, cond_right, basis, left, right, locked_right,
    fine_far, middle_far, image_out, used_out, send_out, cond, vmat, umat, fine_out, middle_out,
    fine_done, middle_done,
):
    used = lanes_of(used_out)
    used_out[...] = jnp.where((used >= 8) & (used < 8 + count[0]), 1.0, 0.0)
    cond[0:4, :] = cond_left[...]
    for at in range(4):
        cond[4 + at : 5 + at, :] = basis[at, BASIS : BASIS + 1, :]
    cond[8:12, :] = cond_right[...]
    cond[12:16, :] = jnp.zeros((4, WIDE), jnp.float32)
    here = cond[...]
    z_at = lanes_of(here) % 64
    x_next, x_prev = roll(here, -1, 0), roll(here, 1, 0)
    y_next, y_prev = roll(here, -64), roll(here, 64)
    z_next = jnp.where(z_at < 63, roll(here, -1), 0.0)
    z_prev = jnp.where(z_at > 0, roll(here, 1), 0.0)
    tx, ty, tz = joined(here, x_next), joined(here, y_next), joined(here, z_next)
    y_faces = face(ty, here, y_next) + face(roll(ty, 64), here, y_prev)
    diagonal = face(tx, here, x_next) + face(roll(tx, 1, 0), here, x_prev) + y_faces
    diagonal = diagonal + face(tz, here, z_next) + face(roll(tz, 1), here, z_prev)
    for at, value in enumerate((diagonal, tx, ty, tz, relax_weight(diagonal))):
        fine_out[at] = value

    def pairs(value):
        return pair_y(pair_z(value))

    def pair_x(value):
        return value + roll(value, -1, 0)

    lower_y, lower_z = lanes_of(here) % 128 < 64, z_at % 2 == 0
    inner = jnp.where(lower_y, ty, 0.0)
    sum_x = pairs(tx)
    ty1 = pair_x(pairs(ty - inner))
    tz1 = pair_x(pairs(jnp.where(lower_z, 0.0, tz)))
    tx1 = roll(sum_x, -1, 0)
    diagonal1 = pair_x(pairs(diagonal - 2.0 * (inner + jnp.where(lower_z, tz, 0.0))))
    diagonal1 = diagonal1 - 2.0 * sum_x
    for at, value in enumerate((diagonal1, tx1, ty1, tz1, relax_weight(diagonal1))):
        middle_out[at] = value
    fine_copy = pltpu.make_async_copy(fine_out, fine_far, fine_done)
    middle_copy = pltpu.make_async_copy(middle_out, middle_far, middle_done)
    fine_copy.start()
    middle_copy.start()

    def own(value):
        return value[0:8, OWN : OWN + 512]

    def quads(value):
        value = quad_y(quad_z(value))
        return value[4:5] + value[6:7]

    y_faces1 = pair_x(pairs(own(y_faces - 2.0 * inner)))
    tx1, ty1, tz1, diagonal1 = own(tx1), own(ty1), own(tz1), own(diagonal1)
    lane = lanes_of(tx1)
    lower_y = (lax.broadcasted_iota(jnp.int32, tx1.shape, 1) // 128) % 2 == 0
    lower_z = lane % 4 < 2
    inner = jnp.where(lower_y, ty1, 0.0)
    across = quad_y(quad_z(tx1))
    tx2 = across[6:7]
    ty2 = quads(ty1 - inner)
    tz2 = quads(jnp.where(lower_z, 0.0, tz1))
    diagonal2 = quads(diagonal1 - 2.0 * (inner + jnp.where(lower_z, tz1, 0.0)))
    diagonal2 = diagonal2 - 2.0 * across[4:5]
    y_faces2 = quads(y_faces1 - 2.0 * inner)
    line2 = y_faces2 + shift * (diagonal2 - y_faces2)
    coarse = []
    for value in (tx2, ty2, tz2, diagonal2, line2):
        first, second = value[:, 0:128], value[:, 256:384]
        coarse.append(jnp.where(lanes_of(first) < 64, first, second))

    gram = jnp.zeros((80, 128), jnp.float32)
    for at in range(4):
        plane = 4 + at
        row = slice(plane, plane + 1)
        wide = basis[at, 0:8, :]
        after = right[...] if at == 3 else basis[at + 1, 0:8, :]
        before = left[...] if at == 0 else basis[at - 1, 0:8, :]
        dg, sx, sy, sz = (fine_out[kind, row, :] for kind in range(4))
        image = dg * wide - sy * roll(wide, -64) - roll(sy * wide, 64)
        image = image - sz * roll(wide, -1) - roll(sz * wide, 1)
        image = image - sx * after - fine_out[1, plane - 1 : plane, :] * before
        image_out[at] = image
        image = image[:, OWN : OWN + 512]
        wide = basis[at, 8:ROWS, OWN:1024]
        after = locked_right[...] if at == 3 else basis[at + 1, 8:ROWS, OWN : OWN + 512]
        dg, sx, sy, sz = (fine_out[kind, row, OWN:1024] for kind in range(4))
        half = (0.5 * dg) * wide - sy * roll(wide, -64) - sz * roll(wide, -1)
        half = half[:, 0:512] - sx[:, 0:512] * after
        vmat[0:72, :] = basis[at, :, OWN : OWN + 512]
        vmat[68:128, :] = half[0:60]
        umat[0:72, :] = basis[at, :, OWN : OWN + 512]
        umat[72:80, :] = image
        gram = gram + dot_nt(umat[...], vmat[...])
    now = packed_rows(jnp.concatenate([gram[0:4], gram[72:76]], axis=0), [coarse[0], coarse[2]])
    rest = jnp.concatenate([coarse[1], coarse[4], coarse[3]], axis=0)
    for target in range(send_out.shape[0]):
        send_out[target, 0:8, :] = now
        send_out[target, 8:13, :] = gram[5 * target : 5 * target + 5]
        send_out[target, 13:16, :] = rest
    fine_copy.wait()
    middle_copy.wait()


def packed_rows(rows, extra):
    lane = lanes_of(rows)
    row = lax.broadcasted_iota(jnp.int32, rows.shape, 0)
    for at, value in enumerate(extra):
        for part in range(4):
            moved = roll(value, 96 - 32 * part)
            rows = jnp.where((row == 4 * at + part) & (lane >= 96), moved, rows)
    return rows


def unpacked_row(rows, at):
    lane = lanes_of(rows[0:1])
    value = roll(rows[4 * at : 4 * at + 1], -96)
    for part in range(1, 4):
        moved = roll(rows[4 * at + part : 4 * at + part + 1], 32 * part - 96)
        value = jnp.where(lane // 32 == part, moved, value)
    return value


def half_of(value, half, wanted):
    return value if half == wanted else roll(value, 64)


def spot_of(value, place):
    lane = lanes_of(value)
    return (lane // 64 == place // 4) & (lane % 4 == place % 4)


def middle_kernel(lines, got, send_out):
    at_y = lax.axis_index("gy")
    total = got[0]
    for source in range(1, got.shape[0]):
        total = total + got[source]
    packed = jnp.zeros((4, 128), jnp.float32)
    for place in range(8):
        source = at_y + (place - 3) // 2
        valid = (source >= 0) & (source < lines // 2)
        value = got[jnp.clip(source, 0, lines // 2 - 1)]
        tx, tz = unpacked_row(value, 0), unpacked_row(value, 1)
        value = jnp.concatenate([tx, value[13:14], tz, value[15:16]], axis=0)
        value = half_of(value, (place - 3) % 2, place // 4)
        packed = packed + jnp.where(spot_of(value, place) & valid, value, 0.0)
    now = packed_rows(total[0:8], [packed[0:1]])
    for target in range(send_out.shape[0]):
        send_out[target, 0:8, :] = now
        send_out[target, 8:13, :] = total[8:13]
        send_out[target, 13:16, :] = packed[1:4]


def residual_kernel(cells, got, used, image, basis, res_out, sums_out):
    total = got[0]
    for source in range(1, got.shape[0]):
        total = total + got[source]
    sums_out[...] = total[8:16]
    overlap, energy = total[0:4], total[4:8]
    lane = lanes_of(overlap)
    own = lane == lax.broadcasted_iota(jnp.int32, overlap.shape, 0)
    norm = jnp.sum(jnp.where(own, overlap, 0.0), axis=1, keepdims=True)
    top = jnp.sum(jnp.where(own, energy, 0.0), axis=1, keepdims=True)
    quotient = top / cells / (norm / cells + EPSILON)
    coupling = (energy - quotient * overlap) / cells
    weights = jnp.where(used[0:4, :] > 0, coupling, 0.0)
    weights = jnp.concatenate([weights, jnp.zeros((4, 128), jnp.float32)], axis=0)
    for at in range(4):
        field = basis[at]
        value = image[at, 0:4, :] - quotient * field[0:4]
        res_out[at] = value - dot_nn(weights[:, 0:ROWS], field)[0:4]


def padded(value):
    return jnp.concatenate([value, jnp.zeros(value.shape, jnp.float32)], axis=0)


def apply_at(values, coefs, row, row_step, at, y_step, z_step, lanes):
    here = values[at]
    dg, sx, sy, sz = (coefs[kind, row : row + 1, lanes] for kind in range(4))
    before = coefs[1, row - row_step : row - row_step + 1, lanes]
    image = dg * here - sx * values[at + 1] - before * values[at - 1]
    image = image - sy * roll(here, -y_step) - roll(sy * here, y_step)
    return image - sz * roll(here, -z_step) - roll(sz * here, z_step)


def fine_image(values, fine, plane, lanes=slice(0, WIDE)):
    return apply_at(values, fine, plane, 1, plane, 64, 1, lanes)


def middle_image(values, middle, plane):
    return apply_at(values, middle, 2 * plane, 2, plane, 128, 2, slice(0, WIDE))


def planes_of(left, mid, right, first, last):
    parts = [left[at] for at in range(3)] + [mid[at] for at in range(4)]
    parts += [right[at] for at in range(3)]
    return {at: padded(parts[at - 1]) for at in range(first, last)}


def down_kernel(left, mid, right, fine, middle, r1_out, send_out, strip_out):
    source = planes_of(left, mid, right, 1, 11)
    error = {at: fine[4, at : at + 1, :] * source[at] for at in range(1, 11)}
    rest = {at: source[at] - fine_image(error, fine, at) for at in range(2, 10)}
    source1, error1 = {}, {}
    for plane in range(1, 5):
        value = pair_y(pair_z(rest[2 * plane] + rest[2 * plane + 1]))
        source1[plane] = value
        r1_out[plane - 1] = value[0:4]
        error1[plane] = middle[4, 2 * plane : 2 * plane + 1, :] * value
    low = sum(source1[plane] - middle_image(error1, middle, plane) for plane in (2, 3))
    low = quad_y(quad_z(low[:, OWN : OWN + 512]))
    both = jnp.concatenate([low[0:4, 0:128], low[0:4, 256:384]], axis=0)
    for target in range(send_out.shape[0]):
        send_out[target] = both
    for at in range(2):
        tiles = [error1[2 + at][0:4, 128 * t : 128 * t + 128] for t in range(1, 9)]
        lane = lanes_of(tiles[0])
        half, odd = lane // 64, lane % 2
        for group in range(2):
            a, b, c, d = tiles[4 * group : 4 * group + 4]
            value = jnp.where(half == 0, jnp.where(odd == 0, a, b), jnp.where(odd == 0, c, d))
            strip_out[at, 4 * group : 4 * group + 4, :] = value


def line_kernel(lines, got, coefs, strips, send_out, solved):
    at_x, at_y = lax.axis_index("gx"), lax.axis_index("gy")
    factors, previous, previous_factor, previous_link = [], None, None, None
    for source in range(lines // 2):
        rows = coefs[source, 13:15, :]
        turned = roll(rows, 64)
        first = lanes_of(rows) < 64
        for part in range(2):
            line = 2 * source + part
            value = jnp.where(first, rows, turned) if part == 0 else jnp.where(first, turned, rows)
            link, main = value[0:1], value[1:2]
            right = got[source, 4 * part : 4 * part + 4, :]
            solved[line, 4:8, :] = right
            if line == 0:
                scale = pl.reciprocal(main)
                update = scale * right
            else:
                scale = pl.reciprocal(main - previous_link * previous_factor)
                update = scale * (right + previous_link * previous)
            previous, previous_factor, previous_link = update, link * scale, link
            solved[line, 0:4, :] = update
            factors.append(previous_factor)
    for line in range(lines - 2, -1, -1):
        previous = solved[line, 0:4, :] + factors[line] * previous
        solved[line, 0:4, :] = previous
    packed = jnp.zeros((8, 128), jnp.float32)
    for place in range(8):
        line = 2 * at_y - 3 + place
        valid = (line >= 0) & (line < lines)
        value = solved[jnp.clip(line, 0, lines - 1)]
        packed = packed + jnp.where(spot_of(value, place) & valid, value, 0.0)
    for target in range(send_out.shape[0]):
        send_out[target, 0:8, :] = packed
        send_out[target, 8:16, :] = strips[(at_x >= target).astype(jnp.int32)]


def up_kernel(
    got, coefs, r1, left, mid, right, fine_far, middle_far, basis_far,
    pre_out, send_out, fine, middle, vmat, fine_done, middle_done, basis_done,
):
    middle_copy = pltpu.make_async_copy(middle_far, middle, middle_done)
    fine_copy = pltpu.make_async_copy(fine_far, fine, fine_done)
    own = basis_far.at[:, :, OWN : OWN + 512]
    basis_copy = pltpu.make_async_copy(own, vmat, basis_done)
    middle_copy.start()
    fine_copy.start()
    basis_copy.start()
    at_x = lax.axis_index("gx")
    count = got.shape[0]
    error, source, links = {}, {}, {}
    for step in range(-3, 4):
        index = at_x + step
        valid = ((index >= 0) & (index < count)).astype(jnp.float32)
        kept = jnp.clip(index, 0, count - 1)
        rows = got[kept, 0:8, :] * valid
        error[step] = padded(rows[0:4])
        source[step] = padded(rows[4:8])
        near = coefs[kept] * valid
        links[step] = jnp.concatenate([unpacked_row(near, 0), near[13:16]], axis=0)
    lane = lanes_of(error[0])
    spot = lane % 4
    for reach in range(SWEEPS - 2, -1, -1):
        updated = dict(error)
        for step in range(-1 - reach, 2 + reach):
            here = error[step]
            sx, sy, sz, dg = (links[step][kind : kind + 1] for kind in range(4))
            up = jnp.where(spot < 3, roll(here, -1), roll(here, -61))
            flux = sy * here
            down = jnp.where(spot > 0, roll(flux, 1), roll(flux, 61))
            value = dg * here - sx * error[step + 1] - links[step - 1][0:1] * error[step - 1]
            value = value - sy * up - down - sz * roll(here, -4) - roll(sz * here, 4)
            updated[step] = here + relax_weight(dg) * (source[step] - value)
        error = updated
    blank = jnp.zeros((8, 128), jnp.float32)
    coarse = {}
    for step in range(-1, 2):
        tiles = []
        for place in range(2, 6):
            value = jnp.where(spot_of(error[step], place), error[step], 0.0)
            value = quad_z(pair_z(value))
            value = value + roll(value, 64)
            tiles += [value, value]
        coarse[step] = jnp.concatenate([blank] + tiles + [blank], axis=1)

    def strip(step):
        index = at_x + step
        valid = ((index >= 0) & (index < count)).astype(jnp.float32)
        rows = got[jnp.clip(index, 0, count - 1), 8:16, :] * valid
        tiles = []
        for group in range(2):
            part = padded(rows[4 * group : 4 * group + 4])
            for place in range(4):
                at = (lane // 64 == place // 2) & (lane % 2 == place % 2)
                value = pair_z(jnp.where(at, part, 0.0))
                tiles.append(value + roll(value, 64))
        return jnp.concatenate([blank] + tiles + [blank], axis=1)

    middle_copy.wait()
    error1, source1 = {0: strip(-1) + coarse[-1], 5: strip(1) + coarse[1]}, {}
    for plane in range(1, 5):
        source1[plane] = padded(r1[plane - 1])
        weight = middle[4, 2 * plane : 2 * plane + 1, :]
        error1[plane] = weight * source1[plane] + coarse[plane // 2 - 1]
    final1 = {}
    for plane in range(1, 5):
        weight = middle[4, 2 * plane : 2 * plane + 1, :]
        final1[plane] = error1[plane] + weight * (
            source1[plane] - middle_image(error1, middle, plane)
        )
    fine_copy.wait()
    lanes = slice(256, 1024)
    source0 = planes_of(left, mid, right, 2, 10)
    source0 = {at: value[:, lanes] for at, value in source0.items()}
    error0 = {
        at: fine[4, at : at + 1, lanes] * source0[at] + final1[at // 2][:, lanes]
        for at in range(2, 10)
    }
    final0 = {}
    for at in range(3, 9):
        weight = fine[4, at : at + 1, lanes]
        final0[at] = error0[at] + weight * (source0[at] - fine_image(error0, fine, at, lanes))
    basis_copy.wait()
    both = jnp.zeros((8, ROWS), jnp.float32)
    for at in range(4):
        own = slice(128, 640)
        value = final0[4 + at][0:4, own]
        pre_out[at] = value
        vmat[at, BASIS:ROWS, :] = value
        value = jnp.concatenate([value, fine_image(final0, fine, 4 + at, lanes)[0:4, own]], axis=0)
        both = both + dot_nt(value, vmat[at])
    now = jnp.concatenate([both, jnp.zeros((8, 128 - ROWS), jnp.float32)], axis=1)
    for target in range(send_out.shape[0]):
        send_out[target] = now


def eliminate(matrix, steps):
    row = lax.broadcasted_iota(jnp.int32, matrix.shape, 0)
    for start in range(0, steps, 4):
        columns = [
            jnp.broadcast_to(matrix[:, at : at + 1], matrix.shape) for at in range(start, start + 4)
        ]
        for part in range(4):
            step = start + part
            column = columns[part]
            factor = jnp.where(row > step, column * pl.reciprocal(column[step : step + 1, :]), 0.0)
            matrix = matrix - factor * matrix[step : step + 1, :]
            for other in range(part + 1, 4):
                value = columns[other]
                columns[other] = value - factor * value[step : step + 1, :]
    diagonal = jnp.where(lanes_of(matrix) == row, matrix, 0.0)
    diagonal = jnp.sum(diagonal, axis=1, keepdims=True)
    scale = lax.rsqrt(jnp.where(row[:, 0:1] < steps, diagonal, 1.0))
    return matrix * scale


def small_product(left, right, count):
    terms = [left[:, at : at + 1] * right[at : at + 1, :] for at in range(count)]
    while len(terms) > 1:
        terms = [sum(terms[at : at + 2]) for at in range(0, len(terms), 2)]
    return terms[0]


def ritz_kernel(
    cells, got, used, pre, basis_far, modes_out, dirs_out, ritz_out, corr_out,
    gram, field, basis_done,
):
    own = basis_far.at[:, :, OWN : OWN + 512]
    basis_copy = pltpu.make_async_copy(own, field, basis_done)
    basis_copy.start()
    total = got[0, 0:8, :]
    for source in range(1, got.shape[0]):
        total = total + got[source, 0:8, :]
    total = total / cells
    gram[80:128, :] = jnp.zeros((48, 128), jnp.float32)
    for source in range(16):
        gram[5 * source : 5 * source + 5, :] = got[source, 8:13, :]
    gram = gram[...] / cells
    shape = (16, 128)
    row = lax.broadcasted_iota(jnp.int32, shape, 0)
    lane = lax.broadcasted_iota(jnp.int32, shape, 1)
    zero4 = jnp.zeros((4, 128), jnp.float32)
    corr = jnp.where(used[0:4, :] > 0, total[0:4], 0.0)
    corr_out[...] = roll(corr, -8)[:, 0:LOCKED]
    locked_part = jnp.concatenate([zero4, -corr, zero4, zero4], axis=0)
    ones = ((row < 4) & (lane == row)) | ((row >= 8) & (row < 12) & (lane == row - 4))
    pre_ones = (row >= 4) & (row < 8) & (lane == row + 64)
    on_basis = jnp.where(ones, 1.0, locked_part)
    weights = jnp.where(pre_ones, 1.0, on_basis)
    pre_lane = (lane >= 68) & (lane < 72)

    def from_pre(part):
        rows4 = jnp.concatenate([zero4, part, zero4, zero4], axis=0)
        rows4 = jnp.where(lane < 72, rows4, 0.0)
        return jnp.where(pre_lane, 0.5 * rows4, rows4)

    products = dot_nn(jnp.concatenate([on_basis, locked_part], axis=0), gram)
    first = jnp.where(lane < 68, products[0:16], 0.0)
    second = roll(jnp.where(lane >= 68, products[16:32], 0.0), -60)
    pair = gram[72:80]
    pair = jnp.concatenate([pair[0:4], zero4, pair[4:8], zero4], axis=0)
    pair = jnp.where(lane < 68, jnp.where(lane < 8, 0.5 * pair, pair), 0.0)
    stacked = [0.5 * first + from_pre(total[0:4]), second + pair + from_pre(total[4:8])]
    stacked = jnp.concatenate(stacked, axis=0)
    straight = dot_nt(stacked, weights)
    turned = dot_nt(weights, stacked)
    mass = straight[0:16] + turned[:, 0:16]
    stiff = straight[16:32] + turned[:, 16:32]
    eye = jnp.where((row < 12) & (lane == row + 64), 1.0, 0.0)
    wide = jnp.zeros((16, 112), jnp.float32)
    mass = jnp.concatenate([mass, wide], axis=1)
    stiff = jnp.concatenate([stiff, wide], axis=1)
    done = eliminate(mass + roll(stiff, 32) + eye, 12)
    inside = (row < 12) & (lane < 12)
    half = jnp.where(inside, roll(done, -32), 0.0)
    inverse = jnp.where(inside, roll(done, -64), 0.0)
    reduced = dot_nt(half, inverse) + dot_nt(inverse, half)
    reduced = 0.5 * jnp.concatenate([reduced, wide], axis=1)
    top = jnp.sum(jnp.where(lane == row, reduced, 0.0), axis=(0, 1), keepdims=True)
    row8 = lax.broadcasted_iota(jnp.int32, (8, 128), 0)
    lane8 = lax.broadcasted_iota(jnp.int32, (8, 128), 1)
    first4 = row8 < 4
    basis_q = jnp.where(first4 & (lane8 == row8), 1.0, 0.0)
    for step in range(RITZ):
        raised = top * basis_q - small_product(basis_q, reduced, 12)
        joint = roll(raised, 32)
        for part in range(ACTIVE):
            column = jnp.sum(raised * raised[part : part + 1, :], axis=1, keepdims=True)
            joint = joint + jnp.where(lane8 == part, column, 0.0)
        basis_q = jnp.where(first4 & (lane8 < 12), roll(eliminate(joint, 4), -32), 0.0)
    ritz = jnp.sum(basis_q * small_product(basis_q, reduced, 12), axis=1, keepdims=True)
    for part in range(ACTIVE):
        ritz_out[part] = ritz[part, 0]
    coefs = small_product(basis_q, inverse, 12)
    tail = jnp.where(lane8 >= 4, coefs, 0.0)
    both = jnp.concatenate([coefs[0:4], tail[0:4]], axis=0)
    mix = small_product(both, weights, 12)[:, 0:ROWS]
    basis_copy.wait()
    for at in range(4):
        field[at, BASIS:ROWS, :] = pre[at]
        value = dot_nn(mix, field[at])
        for part in range(4):
            modes_out[part, at : at + 1, :] = value[part : part + 1]
            dirs_out[part, at : at + 1, :] = value[4 + part : 5 + part]


def pair_shift(low, high, axis):
    count = lax.axis_size(axis)
    forward = [(at, at + 1) for at in range(count - 1)]
    backward = [(at + 1, at) for at in range(count - 1)]
    above = lax.ppermute(low, axis, backward)
    return lax.ppermute(high, axis, forward), above


def spread(block, axis):
    count = lax.axis_size(axis)
    return lax.all_to_all(jnp.broadcast_to(block, (count,) + block.shape), axis, 0, 0)


def on_device(modes, directions, locked, perm_class, perm_table, locked_count):
    size_x, size_y = lax.axis_size("gx"), lax.axis_size("gy")
    lines = 2 * size_y
    cells = float(4 * 512 * size_x * size_y)
    basis, low, high = kernel_call(
        input_kernel, [(4, ROWS, 512), (4, ROWS, 384), (4, ROWS, 384)],
        perm_table, modes, directions, locked, perm_class, scalars=1, inputs=True,
    )
    low, high = pair_shift(low, high, "gy")
    basis = jnp.concatenate([low, basis, high], axis=2)
    conduct = basis[:, BASIS].reshape(10, 512)
    left, right = pair_shift(
        jnp.concatenate(
            [basis[0, 8:, OWN : OWN + 512], basis[0, :8].reshape(20, 512), conduct], 0
        ),
        jnp.concatenate([basis[3, :8].reshape(20, 512), conduct], 0),
        "gx",
    )
    fine, middle, image, used, send = kernel_call(
        functools.partial(coef_kernel, 4.0 / float(lines * lines)),
        [(5, 16, WIDE), (5, 16, WIDE), (4, 8, WIDE), (8, 128), (size_y, 16, 128)],
        locked_count, left[20:30].reshape(4, WIDE), right[84:94].reshape(4, WIDE), basis,
        left[:20].reshape(8, WIDE), right[64:84].reshape(8, WIDE), right[:64],
        scratch=[(16, WIDE), (128, 512), (80, 512), (5, 16, WIDE), (5, 16, WIDE)],
        scalars=1, far_out=(0, 1),
    )
    got_y = lax.all_to_all(send, "gy", 0, 0)
    (send,) = kernel_call(
        functools.partial(middle_kernel, lines), [(size_x, 16, 128)], got_y
    )
    got_x = lax.all_to_all(send, "gx", 0, 0)
    mid, sums = kernel_call(
        functools.partial(residual_kernel, cells), [(4, 4, WIDE), (8, 128)],
        got_x, used, image, basis,
    )
    left, right = pair_shift(mid[:3], mid[1:], "gx")
    r1, send, strips = kernel_call(
        down_kernel, [(4, 4, WIDE), (size_y, 8, 128), (2, 8, 128)], left, mid, right, fine, middle
    )
    (send,) = kernel_call(
        functools.partial(line_kernel, lines), [(size_x, 16, 128)],
        lax.all_to_all(send, "gy", 0, 0), got_y, strips,
        scratch=[(lines, 8, 128)],
    )
    precond, send = kernel_call(
        up_kernel, [(4, 4, 512), (size_x, 8, 128)],
        lax.all_to_all(send, "gx", 0, 0), got_x, r1, left, mid, right, fine, middle, basis,
        scratch=[(5, 16, WIDE), (5, 16, WIDE), (4, ROWS, 512)], far=(6, 7, 8),
    )
    total = jnp.sum(lax.all_to_all(send, "gx", 0, 0), axis=0)
    got_y = spread(jnp.concatenate([total, sums], axis=0), "gy")
    new_modes, new_directions, ritz, corr = kernel_call(
        functools.partial(ritz_kernel, cells),
        [(4, 4, 512), (4, 4, 512), (4,), (4, LOCKED)],
        got_y, used, precond, basis,
        scratch=[(128, 128), (4, ROWS, 512)], far=(3,), results=True,
    )
    return (new_modes, new_directions, ritz, corr.T)


def solution(mesh):
    placed = (
        P(None, "gx", "gy"),
        P(None, "gx", "gy"),
        P(None, "gx", "gy"),
        P("gx", "gy"),
        P(),
        P(),
    )
    return jax.shard_map(
        on_device,
        mesh=mesh,
        in_specs=placed,
        out_specs=(P(None, "gx", "gy"), P(None, "gx", "gy"), P(), P()),
        check_vma=False,
    )
```

```python
import functools

import jax
import jax.numpy as jnp
from jax import lax
from jax.experimental import pallas as pl
from jax.experimental.pallas import tpu as pltpu
from jax.sharding import PartitionSpec as P

NZ = 64
ACTIVE = 4
LOCKED = 60
BASIS = 68
ROWS = 72
SWEEPS = 3
RITZ = 3
OMEGA = 0.6
EPSILON = 1e-06
PRECISE = lax.Precision.HIGHEST
WIDE = 1280
OWN = 384
INTERPRET = False


def kernel_call(
    body, out, *args, scratch=(), scalars=0, far=(), far_out=(), inputs=False, results=False,
    copies=0,
):
    specs, placed = [], []
    for at, value in enumerate(args):
        space = pltpu.SMEM if at < scalars else pl.ANY if at in far else pltpu.VMEM
        specs.append(pl.BlockSpec(memory_space=space))
        if space is pltpu.VMEM and not (inputs or INTERPRET):
            value = pltpu.with_memory_space_constraint(value, pltpu.VMEM)
        placed.append(value)
    shapes, stored = [], []
    for at, shape in enumerate(out):
        space = pltpu.SMEM if len(shape) == 1 else pl.ANY if at in far_out else pltpu.VMEM
        stored.append(pl.BlockSpec(memory_space=space))
        if space is pltpu.VMEM and not (results or INTERPRET):
            shapes.append(pltpu.VMEM(shape, jnp.float32))
        else:
            shapes.append(jax.ShapeDtypeStruct(shape, jnp.float32))
    copies = copies or len(far) + len(far_out)
    held = [pltpu.VMEM(shape, jnp.float32) for shape in scratch]
    held += [pltpu.SemaphoreType.DMA] * copies
    return pl.pallas_call(
        body,
        out_shape=shapes,
        in_specs=specs,
        out_specs=stored,
        scratch_shapes=held,
        interpret=INTERPRET,
    )(*placed)


def roll(value, shift, axis=1):
    return pltpu.roll(value, shift % value.shape[axis], axis)


def lanes_of(value):
    rows, lanes = value.shape
    tile = lax.broadcasted_iota(jnp.int32, (rows, 128), 1)
    return jnp.concatenate([tile] * (lanes // 128), axis=1)


def pair_z(value):
    even = lanes_of(value) % 2 == 0
    return value + jnp.where(even, roll(value, -1), roll(value, 1))


def pair_y(value):
    first = lanes_of(value) % 128 < 64
    return value + jnp.where(first, roll(value, -64), roll(value, 64))


def quad_z(value):
    first = lanes_of(value) % 4 < 2
    return value + jnp.where(first, roll(value, -2), roll(value, 2))


def quad_y(value):
    first = (lax.broadcasted_iota(jnp.int32, value.shape, 1) // 128) % 2 == 0
    return value + jnp.where(first, roll(value, -128), roll(value, 128))


def dot_nt(left, right):
    return lax.dot_general(
        left, right, (((1,), (1,)), ((), ())), precision=PRECISE, preferred_element_type=jnp.float32
    )


def dot_nn(left, right):
    return lax.dot_general(
        left, right, (((1,), (0,)), ((), ())), precision=PRECISE, preferred_element_type=jnp.float32
    )


def relax_weight(diagonal):
    inside = diagonal > 0
    return jnp.where(inside, OMEGA * pl.reciprocal(jnp.where(inside, diagonal, 1.0)), 0.0)


def joined(here, there):
    both = (here > 0) & (there > 0)
    scale = pl.reciprocal(jnp.where(both, here + there, 1.0))
    return jnp.where(both, 2.0 * here * there * scale, 0.0)


def face(coupling, here, there):
    return coupling + jnp.where(there > 0, 0.0, 2.0 * here)


def input_kernel(table, modes, directions, locked, kinds, basis, low_out, high_out):
    value = jnp.zeros((4, 512), jnp.float32)
    kind = kinds[...]
    for at in range(table.shape[0]):
        value = jnp.where(kind == at, table[at], value)
    for at in range(4):
        basis[at, 0:4, :] = modes[:, at, :]
        basis[at, 4:8, :] = directions[:, at, :]
        basis[at, 8:BASIS, :] = locked[:, at, :]
        basis[at, BASIS:ROWS, :] = jnp.zeros((ROWS - BASIS, 512), jnp.float32)
        basis[at, BASIS : BASIS + 1, :] = value[at : at + 1]
        low_out[at] = basis[at, :, 0:384]
        high_out[at] = basis[at, :, 128:512]


def coef_kernel(
    shift, count, cond_left, cond_right, basis, left, right, locked_right,
    fine_far, middle_far, image_out, used_out, send_out, cond, vmat, umat, fine_out, middle_out,
    fine_done, middle_done,
):
    used = lanes_of(used_out)
    used_out[...] = jnp.where((used >= 8) & (used < 8 + count[0]), 1.0, 0.0)
    cond[0:4, :] = cond_left[...]
    for at in range(4):
        cond[4 + at : 5 + at, :] = basis[at, BASIS : BASIS + 1, :]
    cond[8:12, :] = cond_right[...]
    cond[12:16, :] = jnp.zeros((4, WIDE), jnp.float32)
    here = cond[...]
    z_at = lanes_of(here) % 64
    x_next, x_prev = roll(here, -1, 0), roll(here, 1, 0)
    y_next, y_prev = roll(here, -64), roll(here, 64)
    z_next = jnp.where(z_at < 63, roll(here, -1), 0.0)
    z_prev = jnp.where(z_at > 0, roll(here, 1), 0.0)
    tx, ty, tz = joined(here, x_next), joined(here, y_next), joined(here, z_next)
    y_faces = face(ty, here, y_next) + face(roll(ty, 64), here, y_prev)
    diagonal = face(tx, here, x_next) + face(roll(tx, 1, 0), here, x_prev) + y_faces
    diagonal = diagonal + face(tz, here, z_next) + face(roll(tz, 1), here, z_prev)
    for at, value in enumerate((diagonal, tx, ty, tz, relax_weight(diagonal))):
        fine_out[at] = value

    def pairs(value):
        return pair_y(pair_z(value))

    def pair_x(value):
        return value + roll(value, -1, 0)

    lower_y, lower_z = lanes_of(here) % 128 < 64, z_at % 2 == 0
    inner = jnp.where(lower_y, ty, 0.0)
    sum_x = pairs(tx)
    ty1 = pair_x(pairs(ty - inner))
    tz1 = pair_x(pairs(jnp.where(lower_z, 0.0, tz)))
    tx1 = roll(sum_x, -1, 0)
    diagonal1 = pair_x(pairs(diagonal - 2.0 * (inner + jnp.where(lower_z, tz, 0.0))))
    diagonal1 = diagonal1 - 2.0 * sum_x
    for at, value in enumerate((diagonal1, tx1, ty1, tz1, relax_weight(diagonal1))):
        middle_out[at] = value
    fine_copy = pltpu.make_async_copy(fine_out, fine_far, fine_done)
    middle_copy = pltpu.make_async_copy(middle_out, middle_far, middle_done)
    fine_copy.start()
    middle_copy.start()

    def own(value):
        return value[0:8, OWN : OWN + 512]

    def quads(value):
        value = quad_y(quad_z(value))
        return value[4:5] + value[6:7]

    y_faces1 = pair_x(pairs(own(y_faces - 2.0 * inner)))
    tx1, ty1, tz1, diagonal1 = own(tx1), own(ty1), own(tz1), own(diagonal1)
    lane = lanes_of(tx1)
    lower_y = (lax.broadcasted_iota(jnp.int32, tx1.shape, 1) // 128) % 2 == 0
    lower_z = lane % 4 < 2
    inner = jnp.where(lower_y, ty1, 0.0)
    across = quad_y(quad_z(tx1))
    tx2 = across[6:7]
    ty2 = quads(ty1 - inner)
    tz2 = quads(jnp.where(lower_z, 0.0, tz1))
    diagonal2 = quads(diagonal1 - 2.0 * (inner + jnp.where(lower_z, tz1, 0.0)))
    diagonal2 = diagonal2 - 2.0 * across[4:5]
    y_faces2 = quads(y_faces1 - 2.0 * inner)
    line2 = y_faces2 + shift * (diagonal2 - y_faces2)
    coarse = []
    for value in (tx2, ty2, tz2, diagonal2, line2):
        first, second = value[:, 0:128], value[:, 256:384]
        coarse.append(jnp.where(lanes_of(first) < 64, first, second))

    gram = jnp.zeros((80, 128), jnp.float32)
    for at in range(4):
        plane = 4 + at
        row = slice(plane, plane + 1)
        wide = basis[at, 0:8, :]
        after = right[...] if at == 3 else basis[at + 1, 0:8, :]
        before = left[...] if at == 0 else basis[at - 1, 0:8, :]
        dg, sx, sy, sz = (fine_out[kind, row, :] for kind in range(4))
        image = dg * wide - sy * roll(wide, -64) - roll(sy * wide, 64)
        image = image - sz * roll(wide, -1) - roll(sz * wide, 1)
        image = image - sx * after - fine_out[1, plane - 1 : plane, :] * before
        image_out[at] = image
        image = image[:, OWN : OWN + 512]
        wide = basis[at, 8:ROWS, OWN:1024]
        after = locked_right[...] if at == 3 else basis[at + 1, 8:ROWS, OWN : OWN + 512]
        dg, sx, sy, sz = (fine_out[kind, row, OWN:1024] for kind in range(4))
        half = (0.5 * dg) * wide - sy * roll(wide, -64) - sz * roll(wide, -1)
        half = half[:, 0:512] - sx[:, 0:512] * after
        vmat[0:72, :] = basis[at, :, OWN : OWN + 512]
        vmat[68:128, :] = half[0:60]
        umat[0:72, :] = basis[at, :, OWN : OWN + 512]
        umat[72:80, :] = image
        gram = gram + dot_nt(umat[...], vmat[...])
    now = packed_rows(jnp.concatenate([gram[0:4], gram[72:76]], axis=0), [coarse[0], coarse[2]])
    rest = jnp.concatenate([coarse[1], coarse[4], coarse[3]], axis=0)
    for target in range(send_out.shape[0]):
        send_out[target, 0:8, :] = now
        send_out[target, 8:13, :] = gram[5 * target : 5 * target + 5]
        send_out[target, 13:16, :] = rest
    fine_copy.wait()
    middle_copy.wait()


def packed_rows(rows, extra):
    lane = lanes_of(rows)
    row = lax.broadcasted_iota(jnp.int32, rows.shape, 0)
    for at, value in enumerate(extra):
        for part in range(4):
            moved = roll(value, 96 - 32 * part)
            rows = jnp.where((row == 4 * at + part) & (lane >= 96), moved, rows)
    return rows


def unpacked_row(rows, at):
    lane = lanes_of(rows[0:1])
    value = roll(rows[4 * at : 4 * at + 1], -96)
    for part in range(1, 4):
        moved = roll(rows[4 * at + part : 4 * at + part + 1], 32 * part - 96)
        value = jnp.where(lane // 32 == part, moved, value)
    return value


def half_of(value, half, wanted):
    return value if half == wanted else roll(value, 64)


def spot_of(value, place):
    lane = lanes_of(value)
    return (lane // 64 == place // 4) & (lane % 4 == place % 4)


def middle_kernel(lines, got, send_out):
    at_y = lax.axis_index("gy")
    total = got[0]
    for source in range(1, got.shape[0]):
        total = total + got[source]
    packed = jnp.zeros((4, 128), jnp.float32)
    for place in range(8):
        source = at_y + (place - 3) // 2
        valid = (source >= 0) & (source < lines // 2)
        value = got[jnp.clip(source, 0, lines // 2 - 1)]
        tx, tz = unpacked_row(value, 0), unpacked_row(value, 1)
        value = jnp.concatenate([tx, value[13:14], tz, value[15:16]], axis=0)
        value = half_of(value, (place - 3) % 2, place // 4)
        packed = packed + jnp.where(spot_of(value, place) & valid, value, 0.0)
    now = packed_rows(total[0:8], [packed[0:1]])
    for target in range(send_out.shape[0]):
        send_out[target, 0:8, :] = now
        send_out[target, 8:13, :] = total[8:13]
        send_out[target, 13:16, :] = packed[1:4]


def residual_kernel(cells, got, used, image, basis, res_out, sums_out):
    total = got[0]
    for source in range(1, got.shape[0]):
        total = total + got[source]
    sums_out[...] = total[8:16]
    overlap, energy = total[0:4], total[4:8]
    lane = lanes_of(overlap)
    own = lane == lax.broadcasted_iota(jnp.int32, overlap.shape, 0)
    norm = jnp.sum(jnp.where(own, overlap, 0.0), axis=1, keepdims=True)
    top = jnp.sum(jnp.where(own, energy, 0.0), axis=1, keepdims=True)
    quotient = top / cells / (norm / cells + EPSILON)
    coupling = (energy - quotient * overlap) / cells
    weights = jnp.where(used[0:4, :] > 0, coupling, 0.0)
    weights = jnp.concatenate([weights, jnp.zeros((4, 128), jnp.float32)], axis=0)
    for at in range(4):
        field = basis[at]
        value = image[at, 0:4, :] - quotient * field[0:4]
        res_out[at] = value - dot_nn(weights[:, 0:ROWS], field)[0:4]


def padded(value):
    return jnp.concatenate([value, jnp.zeros(value.shape, jnp.float32)], axis=0)


def apply_at(values, coefs, row, row_step, at, y_step, z_step, lanes):
    here = values[at]
    dg, sx, sy, sz = (coefs[kind, row : row + 1, lanes] for kind in range(4))
    before = coefs[1, row - row_step : row - row_step + 1, lanes]
    image = dg * here - sx * values[at + 1] - before * values[at - 1]
    image = image - sy * roll(here, -y_step) - roll(sy * here, y_step)
    return image - sz * roll(here, -z_step) - roll(sz * here, z_step)


def fine_image(values, fine, plane, lanes=slice(0, WIDE)):
    return apply_at(values, fine, plane, 1, plane, 64, 1, lanes)


def middle_image(values, middle, plane):
    return apply_at(values, middle, 2 * plane, 2, plane, 128, 2, slice(0, WIDE))


def planes_of(left, mid, right, first, last):
    parts = [left[at] for at in range(3)] + [mid[at] for at in range(4)]
    parts += [right[at] for at in range(3)]
    return {at: padded(parts[at - 1]) for at in range(first, last)}


def down_kernel(left, mid, right, fine, middle, r1_out, send_out, strip_out):
    source = planes_of(left, mid, right, 1, 11)
    error = {at: fine[4, at : at + 1, :] * source[at] for at in range(1, 11)}
    rest = {at: source[at] - fine_image(error, fine, at) for at in range(2, 10)}
    source1, error1 = {}, {}
    for plane in range(1, 5):
        value = pair_y(pair_z(rest[2 * plane] + rest[2 * plane + 1]))
        source1[plane] = value
        r1_out[plane - 1] = value[0:4]
        error1[plane] = middle[4, 2 * plane : 2 * plane + 1, :] * value
    low = sum(source1[plane] - middle_image(error1, middle, plane) for plane in (2, 3))
    low = quad_y(quad_z(low[:, OWN : OWN + 512]))
    both = jnp.concatenate([low[0:4, 0:128], low[0:4, 256:384]], axis=0)
    for target in range(send_out.shape[0]):
        send_out[target] = both
    for at in range(2):
        tiles = [error1[2 + at][0:4, 128 * t : 128 * t + 128] for t in range(1, 9)]
        lane = lanes_of(tiles[0])
        half, odd = lane // 64, lane % 2
        for group in range(2):
            a, b, c, d = tiles[4 * group : 4 * group + 4]
            value = jnp.where(half == 0, jnp.where(odd == 0, a, b), jnp.where(odd == 0, c, d))
            strip_out[at, 4 * group : 4 * group + 4, :] = value


def line_kernel(lines, got, coefs, strips, send_out, solved):
    at_x, at_y = lax.axis_index("gx"), lax.axis_index("gy")
    factors, previous, previous_factor, previous_link = [], None, None, None
    for source in range(lines // 2):
        rows = coefs[source, 13:15, :]
        turned = roll(rows, 64)
        first = lanes_of(rows) < 64
        for part in range(2):
            line = 2 * source + part
            value = jnp.where(first, rows, turned) if part == 0 else jnp.where(first, turned, rows)
            link, main = value[0:1], value[1:2]
            right = got[source, 4 * part : 4 * part + 4, :]
            solved[line, 4:8, :] = right
            if line == 0:
                scale = pl.reciprocal(main)
                update = scale * right
            else:
                scale = pl.reciprocal(main - previous_link * previous_factor)
                update = scale * (right + previous_link * previous)
            previous, previous_factor, previous_link = update, link * scale, link
            solved[line, 0:4, :] = update
            factors.append(previous_factor)
    for line in range(lines - 2, -1, -1):
        previous = solved[line, 0:4, :] + factors[line] * previous
        solved[line, 0:4, :] = previous
    packed = jnp.zeros((8, 128), jnp.float32)
    for place in range(8):
        line = 2 * at_y - 3 + place
        valid = (line >= 0) & (line < lines)
        value = solved[jnp.clip(line, 0, lines - 1)]
        packed = packed + jnp.where(spot_of(value, place) & valid, value, 0.0)
    for target in range(send_out.shape[0]):
        send_out[target, 0:8, :] = packed
        send_out[target, 8:16, :] = strips[(at_x >= target).astype(jnp.int32)]


def up_kernel(
    got, coefs, r1, left, mid, right, sums, fine_far, middle_far, basis_far,
    pre_out, send_out, fine, middle, vmat, fine_done, middle_done, basis_done,
):
    middle_copy = pltpu.make_async_copy(middle_far, middle, middle_done)
    fine_copy = pltpu.make_async_copy(fine_far, fine, fine_done)
    own = basis_far.at[:, :, OWN : OWN + 512]
    basis_copy = pltpu.make_async_copy(own, vmat, basis_done)
    middle_copy.start()
    fine_copy.start()
    basis_copy.start()
    at_x = lax.axis_index("gx")
    count = got.shape[0]
    error, source, links = {}, {}, {}
    for step in range(-3, 4):
        index = at_x + step
        valid = ((index >= 0) & (index < count)).astype(jnp.float32)
        kept = jnp.clip(index, 0, count - 1)
        rows = got[kept, 0:8, :] * valid
        error[step] = padded(rows[0:4])
        source[step] = padded(rows[4:8])
        near = coefs[kept] * valid
        links[step] = jnp.concatenate([unpacked_row(near, 0), near[13:16]], axis=0)
    lane = lanes_of(error[0])
    spot = lane % 4
    for reach in range(SWEEPS - 2, -1, -1):
        updated = dict(error)
        for step in range(-1 - reach, 2 + reach):
            here = error[step]
            sx, sy, sz, dg = (links[step][kind : kind + 1] for kind in range(4))
            up = jnp.where(spot < 3, roll(here, -1), roll(here, -61))
            flux = sy * here
            down = jnp.where(spot > 0, roll(flux, 1), roll(flux, 61))
            value = dg * here - sx * error[step + 1] - links[step - 1][0:1] * error[step - 1]
            value = value - sy * up - down - sz * roll(here, -4) - roll(sz * here, 4)
            updated[step] = here + relax_weight(dg) * (source[step] - value)
        error = updated
    blank = jnp.zeros((8, 128), jnp.float32)
    coarse = {}
    for step in range(-1, 2):
        tiles = []
        for place in range(2, 6):
            value = jnp.where(spot_of(error[step], place), error[step], 0.0)
            value = quad_z(pair_z(value))
            value = value + roll(value, 64)
            tiles += [value, value]
        coarse[step] = jnp.concatenate([blank] + tiles + [blank], axis=1)

    def strip(step):
        index = at_x + step
        valid = ((index >= 0) & (index < count)).astype(jnp.float32)
        rows = got[jnp.clip(index, 0, count - 1), 8:16, :] * valid
        tiles = []
        for group in range(2):
            part = padded(rows[4 * group : 4 * group + 4])
            for place in range(4):
                at = (lane // 64 == place // 2) & (lane % 2 == place % 2)
                value = pair_z(jnp.where(at, part, 0.0))
                tiles.append(value + roll(value, 64))
        return jnp.concatenate([blank] + tiles + [blank], axis=1)

    middle_copy.wait()
    error1, source1 = {0: strip(-1) + coarse[-1], 5: strip(1) + coarse[1]}, {}
    for plane in range(1, 5):
        source1[plane] = padded(r1[plane - 1])
        weight = middle[4, 2 * plane : 2 * plane + 1, :]
        error1[plane] = weight * source1[plane] + coarse[plane // 2 - 1]
    final1 = {}
    for plane in range(1, 5):
        weight = middle[4, 2 * plane : 2 * plane + 1, :]
        final1[plane] = error1[plane] + weight * (
            source1[plane] - middle_image(error1, middle, plane)
        )
    fine_copy.wait()
    lanes = slice(256, 1024)
    source0 = planes_of(left, mid, right, 2, 10)
    source0 = {at: value[:, lanes] for at, value in source0.items()}
    error0 = {
        at: fine[4, at : at + 1, lanes] * source0[at] + final1[at // 2][:, lanes]
        for at in range(2, 10)
    }
    final0 = {}
    for at in range(3, 9):
        weight = fine[4, at : at + 1, lanes]
        final0[at] = error0[at] + weight * (source0[at] - fine_image(error0, fine, at, lanes))
    basis_copy.wait()
    both = jnp.zeros((8, ROWS), jnp.float32)
    for at in range(4):
        own = slice(128, 640)
        value = final0[4 + at][0:4, own]
        pre_out[at] = value
        vmat[at, BASIS:ROWS, :] = value
        value = jnp.concatenate([value, fine_image(final0, fine, 4 + at, lanes)[0:4, own]], axis=0)
        both = both + dot_nt(value, vmat[at])
    now = jnp.concatenate([both, jnp.zeros((8, 128 - ROWS), jnp.float32)], axis=1)
    for target in range(send_out.shape[0]):
        send_out[target, 0:8, :] = now
        send_out[target, 8:16, :] = sums[...]


def eliminate(matrix, steps):
    row = lax.broadcasted_iota(jnp.int32, matrix.shape, 0)
    for start in range(0, steps, 4):
        columns = [
            jnp.broadcast_to(matrix[:, at : at + 1], matrix.shape) for at in range(start, start + 4)
        ]
        for part in range(4):
            step = start + part
            column = columns[part]
            factor = jnp.where(row > step, column * pl.reciprocal(column[step : step + 1, :]), 0.0)
            matrix = matrix - factor * matrix[step : step + 1, :]
            for other in range(part + 1, 4):
                value = columns[other]
                columns[other] = value - factor * value[step : step + 1, :]
    diagonal = jnp.where(lanes_of(matrix) == row, matrix, 0.0)
    diagonal = jnp.sum(diagonal, axis=1, keepdims=True)
    scale = lax.rsqrt(jnp.where(row[:, 0:1] < steps, diagonal, 1.0))
    return matrix * scale


def small_product(left, right, count):
    terms = [left[:, at : at + 1] * right[at : at + 1, :] for at in range(count)]
    while len(terms) > 1:
        terms = [sum(terms[at : at + 2]) for at in range(0, len(terms), 2)]
    return terms[0]


def ritz_kernel(
    cells, got, gathered, used, pre, basis_far, modes_out, dirs_out, ritz_out, corr_out,
    gram, field, basis_done,
):
    own = basis_far.at[:, :, OWN : OWN + 512]
    basis_copy = pltpu.make_async_copy(own, field, basis_done)
    basis_copy.start()
    total = got[0]
    for source in range(1, got.shape[0]):
        total = total + got[source]
    total = total / cells
    gram[80:128, :] = jnp.zeros((48, 128), jnp.float32)
    for source in range(16):
        gram[5 * source : 5 * source + 5, :] = gathered[source, 0:5, :]
    gram = gram[...] / cells
    shape = (16, 128)
    row = lax.broadcasted_iota(jnp.int32, shape, 0)
    lane = lax.broadcasted_iota(jnp.int32, shape, 1)
    zero4 = jnp.zeros((4, 128), jnp.float32)
    corr = jnp.where(used[0:4, :] > 0, total[0:4], 0.0)
    corr_out[...] = roll(corr, -8)[:, 0:LOCKED]
    locked_part = jnp.concatenate([zero4, -corr, zero4, zero4], axis=0)
    ones = ((row < 4) & (lane == row)) | ((row >= 8) & (row < 12) & (lane == row - 4))
    pre_ones = (row >= 4) & (row < 8) & (lane == row + 64)
    on_basis = jnp.where(ones, 1.0, locked_part)
    weights = jnp.where(pre_ones, 1.0, on_basis)
    pre_lane = (lane >= 68) & (lane < 72)

    def from_pre(part):
        rows4 = jnp.concatenate([zero4, part, zero4, zero4], axis=0)
        rows4 = jnp.where(lane < 72, rows4, 0.0)
        return jnp.where(pre_lane, 0.5 * rows4, rows4)

    products = dot_nn(jnp.concatenate([on_basis, locked_part], axis=0), gram)
    first = jnp.where(lane < 68, products[0:16], 0.0)
    second = roll(jnp.where(lane >= 68, products[16:32], 0.0), -60)
    pair = gram[72:80]
    pair = jnp.concatenate([pair[0:4], zero4, pair[4:8], zero4], axis=0)
    pair = jnp.where(lane < 68, jnp.where(lane < 8, 0.5 * pair, pair), 0.0)
    stacked = [0.5 * first + from_pre(total[0:4]), second + pair + from_pre(total[4:8])]
    stacked = jnp.concatenate(stacked, axis=0)
    straight = dot_nt(stacked, weights)
    turned = dot_nt(weights, stacked)
    mass = straight[0:16] + turned[:, 0:16]
    stiff = straight[16:32] + turned[:, 16:32]
    eye = jnp.where((row < 12) & (lane == row + 64), 1.0, 0.0)
    wide = jnp.zeros((16, 112), jnp.float32)
    mass = jnp.concatenate([mass, wide], axis=1)
    stiff = jnp.concatenate([stiff, wide], axis=1)
    done = eliminate(mass + roll(stiff, 32) + eye, 12)
    inside = (row < 12) & (lane < 12)
    half = jnp.where(inside, roll(done, -32), 0.0)
    inverse = jnp.where(inside, roll(done, -64), 0.0)
    reduced = dot_nt(half, inverse) + dot_nt(inverse, half)
    reduced = 0.5 * jnp.concatenate([reduced, wide], axis=1)
    top = jnp.sum(jnp.where(lane == row, reduced, 0.0), axis=(0, 1), keepdims=True)
    row8 = lax.broadcasted_iota(jnp.int32, (8, 128), 0)
    lane8 = lax.broadcasted_iota(jnp.int32, (8, 128), 1)
    first4 = row8 < 4
    raising = jnp.where(inside & (lane == row), top, 0.0) - reduced
    for step in range(RITZ):
        raised = small_product(basis_q, raising, 12) if step else raising[0:8]
        raised = jnp.where(first4, raised, 0.0)
        joint = roll(raised, 32)
        for part in range(ACTIVE):
            column = jnp.sum(raised * raised[part : part + 1, :], axis=1, keepdims=True)
            joint = joint + jnp.where(lane8 == part, column, 0.0)
        basis_q = jnp.where(first4 & (lane8 < 12), roll(eliminate(joint, 4), -32), 0.0)
    ritz = jnp.sum(basis_q * small_product(basis_q, reduced, 12), axis=1, keepdims=True)
    for part in range(ACTIVE):
        ritz_out[part] = ritz[part, 0]
    coefs = small_product(basis_q, inverse, 12)
    tail = jnp.where(lane8 >= 4, coefs, 0.0)
    both = jnp.concatenate([coefs[0:4], tail[0:4]], axis=0)
    mix = small_product(both, weights, 12)[:, 0:ROWS]
    basis_copy.wait()
    for at in range(4):
        field[at, BASIS:ROWS, :] = pre[at]
        value = dot_nn(mix, field[at])
        for part in range(4):
            modes_out[part, at : at + 1, :] = value[part : part + 1]
            dirs_out[part, at : at + 1, :] = value[4 + part : 5 + part]


def pair_shift(low, high, axis):
    count = lax.axis_size(axis)
    forward = [(at, at + 1) for at in range(count - 1)]
    backward = [(at + 1, at) for at in range(count - 1)]
    above = lax.ppermute(low, axis, backward)
    return lax.ppermute(high, axis, forward), above


def spread(block, axis):
    count = lax.axis_size(axis)
    return lax.all_to_all(jnp.broadcast_to(block, (count,) + block.shape), axis, 0, 0)


def on_device(modes, directions, locked, perm_class, perm_table, locked_count):
    size_x, size_y = lax.axis_size("gx"), lax.axis_size("gy")
    lines = 2 * size_y
    cells = float(4 * 512 * size_x * size_y)
    basis, low, high = kernel_call(
        input_kernel, [(4, ROWS, 512), (4, ROWS, 384), (4, ROWS, 384)],
        perm_table, modes, directions, locked, perm_class, scalars=1, inputs=True,
    )
    low, high = pair_shift(low, high, "gy")
    basis = jnp.concatenate([low, basis, high], axis=2)
    conduct = basis[:, BASIS].reshape(10, 512)
    left, right = pair_shift(
        jnp.concatenate(
            [basis[0, 8:, OWN : OWN + 512], basis[0, :8].reshape(20, 512), conduct], 0
        ),
        jnp.concatenate([basis[3, :8].reshape(20, 512), conduct], 0),
        "gx",
    )
    fine, middle, image, used, send = kernel_call(
        functools.partial(coef_kernel, 4.0 / float(lines * lines)),
        [(5, 16, WIDE), (5, 16, WIDE), (4, 8, WIDE), (8, 128), (size_y, 16, 128)],
        locked_count, left[20:30].reshape(4, WIDE), right[84:94].reshape(4, WIDE), basis,
        left[:20].reshape(8, WIDE), right[64:84].reshape(8, WIDE), right[:64],
        scratch=[(16, WIDE), (128, 512), (80, 512), (5, 16, WIDE), (5, 16, WIDE)],
        scalars=1, far_out=(0, 1),
    )
    got_y = lax.all_to_all(send, "gy", 0, 0)
    (send,) = kernel_call(
        functools.partial(middle_kernel, lines), [(size_x, 16, 128)], got_y
    )
    got_x = lax.all_to_all(send, "gx", 0, 0)
    mid, sums = kernel_call(
        functools.partial(residual_kernel, cells), [(4, 4, WIDE), (8, 128)],
        got_x, used, image, basis,
    )
    left, right = pair_shift(mid[:3], mid[1:], "gx")
    r1, send, strips = kernel_call(
        down_kernel, [(4, 4, WIDE), (size_y, 8, 128), (2, 8, 128)], left, mid, right, fine, middle
    )
    (send,) = kernel_call(
        functools.partial(line_kernel, lines), [(size_x, 16, 128)],
        lax.all_to_all(send, "gy", 0, 0), got_y, strips,
        scratch=[(lines, 8, 128)],
    )
    precond, send = kernel_call(
        up_kernel, [(4, 4, 512), (size_y, 16, 128)],
        lax.all_to_all(send, "gx", 0, 0), got_x, r1, left, mid, right, sums, fine, middle, basis,
        scratch=[(5, 16, WIDE), (5, 16, WIDE), (4, ROWS, 512)], far=(7, 8, 9),
    )
    got_y = lax.all_to_all(send, "gy", 0, 0)
    got_x = spread(jnp.sum(got_y[:, :8], axis=0), "gx")
    new_modes, new_directions, ritz, corr = kernel_call(
        functools.partial(ritz_kernel, cells),
        [(4, 4, 512), (4, 4, 512), (4,), (4, LOCKED)],
        got_x, got_y[:, 8:], used, precond, basis,
        scratch=[(128, 128), (4, ROWS, 512)], far=(4,), results=True,
    )
    return (new_modes, new_directions, ritz, corr.T)


def solution(mesh):
    placed = (
        P(None, "gx", "gy"),
        P(None, "gx", "gy"),
        P(None, "gx", "gy"),
        P("gx", "gy"),
        P(),
        P(),
    )
    return jax.shard_map(
        on_device,
        mesh=mesh,
        in_specs=placed,
        out_specs=(P(None, "gx", "gy"), P(None, "gx", "gy"), P(), P()),
        check_vma=False,
    )
```

```python
import functools

import jax
import jax.numpy as jnp
from jax import lax
from jax.experimental import pallas as pl
from jax.experimental.pallas import tpu as pltpu
from jax.sharding import PartitionSpec as P

NZ = 64
ACTIVE = 4
LOCKED = 60
BASIS = 68
ROWS = 72
SWEEPS = 3
RITZ = 3
OMEGA = 0.6
EPSILON = 1e-06
PRECISE = lax.Precision.HIGHEST
WIDE = 1280
OWN = 384
INTERPRET = False


def kernel_call(
    body, out, *args, scratch=(), scalars=0, far=(), far_out=(), inputs=False, results=False,
    copies=0,
):
    specs, placed = [], []
    for at, value in enumerate(args):
        space = pltpu.SMEM if at < scalars else pl.ANY if at in far else pltpu.VMEM
        specs.append(pl.BlockSpec(memory_space=space))
        if space is pltpu.VMEM and not (inputs or INTERPRET):
            value = pltpu.with_memory_space_constraint(value, pltpu.VMEM)
        placed.append(value)
    shapes, stored = [], []
    for at, shape in enumerate(out):
        space = pltpu.SMEM if len(shape) == 1 else pl.ANY if at in far_out else pltpu.VMEM
        stored.append(pl.BlockSpec(memory_space=space))
        if space is pltpu.VMEM and not (results or INTERPRET):
            shapes.append(pltpu.VMEM(shape, jnp.float32))
        else:
            shapes.append(jax.ShapeDtypeStruct(shape, jnp.float32))
    copies = copies or len(far) + len(far_out)
    held = [pltpu.VMEM(shape, jnp.float32) for shape in scratch]
    held += [pltpu.SemaphoreType.DMA] * copies
    return pl.pallas_call(
        body,
        out_shape=shapes,
        in_specs=specs,
        out_specs=stored,
        scratch_shapes=held,
        interpret=INTERPRET,
    )(*placed)


def roll(value, shift, axis=1):
    return pltpu.roll(value, shift % value.shape[axis], axis)


def lanes_of(value):
    rows, lanes = value.shape
    tile = lax.broadcasted_iota(jnp.int32, (rows, 128), 1)
    return jnp.concatenate([tile] * (lanes // 128), axis=1)


def pair_z(value):
    even = lanes_of(value) % 2 == 0
    return value + jnp.where(even, roll(value, -1), roll(value, 1))


def pair_y(value):
    first = lanes_of(value) % 128 < 64
    return value + jnp.where(first, roll(value, -64), roll(value, 64))


def quad_z(value):
    first = lanes_of(value) % 4 < 2
    return value + jnp.where(first, roll(value, -2), roll(value, 2))


def quad_y(value):
    first = (lax.broadcasted_iota(jnp.int32, value.shape, 1) // 128) % 2 == 0
    return value + jnp.where(first, roll(value, -128), roll(value, 128))


def dot_nt(left, right):
    return lax.dot_general(
        left, right, (((1,), (1,)), ((), ())), precision=PRECISE, preferred_element_type=jnp.float32
    )


def dot_nn(left, right):
    return lax.dot_general(
        left, right, (((1,), (0,)), ((), ())), precision=PRECISE, preferred_element_type=jnp.float32
    )


def relax_weight(diagonal):
    inside = diagonal > 0
    return jnp.where(inside, OMEGA * pl.reciprocal(jnp.where(inside, diagonal, 1.0)), 0.0)


def joined(here, there):
    both = (here > 0) & (there > 0)
    scale = pl.reciprocal(jnp.where(both, here + there, 1.0))
    return jnp.where(both, 2.0 * here * there * scale, 0.0)


def face(coupling, here, there):
    return coupling + jnp.where(there > 0, 0.0, 2.0 * here)


def input_kernel(table, modes, directions, locked, kinds, basis, low_out, high_out):
    value = jnp.zeros((4, 512), jnp.float32)
    kind = kinds[...]
    for at in range(table.shape[0]):
        value = jnp.where(kind == at, table[at], value)
    for at in range(4):
        basis[at, 0:4, :] = modes[:, at, :]
        basis[at, 4:8, :] = directions[:, at, :]
        basis[at, 8:BASIS, :] = locked[:, at, :]
        basis[at, BASIS:ROWS, :] = jnp.zeros((ROWS - BASIS, 512), jnp.float32)
        basis[at, BASIS : BASIS + 1, :] = value[at : at + 1]
        low_out[at] = basis[at, :, 0:384]
        high_out[at] = basis[at, :, 128:512]


def coef_kernel(
    shift, count, cond_left, cond_right, basis, left, right, locked_right,
    fine_far, middle_far, image_out, used_out, send_out, cond, vmat, umat, fine_out, middle_out,
    fine_done, middle_done,
):
    used = lanes_of(used_out)
    used_out[...] = jnp.where((used >= 8) & (used < 8 + count[0]), 1.0, 0.0)
    cond[0:4, :] = cond_left[...]
    for at in range(4):
        cond[4 + at : 5 + at, :] = basis[at, BASIS : BASIS + 1, :]
    cond[8:12, :] = cond_right[...]
    cond[12:16, :] = jnp.zeros((4, WIDE), jnp.float32)
    here = cond[...]
    z_at = lanes_of(here) % 64
    x_next, x_prev = roll(here, -1, 0), roll(here, 1, 0)
    y_next, y_prev = roll(here, -64), roll(here, 64)
    z_next = jnp.where(z_at < 63, roll(here, -1), 0.0)
    z_prev = jnp.where(z_at > 0, roll(here, 1), 0.0)
    tx, ty, tz = joined(here, x_next), joined(here, y_next), joined(here, z_next)
    y_faces = face(ty, here, y_next) + face(roll(ty, 64), here, y_prev)
    diagonal = face(tx, here, x_next) + face(roll(tx, 1, 0), here, x_prev) + y_faces
    diagonal = diagonal + face(tz, here, z_next) + face(roll(tz, 1), here, z_prev)
    for at, value in enumerate((diagonal, tx, ty, tz, relax_weight(diagonal))):
        fine_out[at] = value

    def pairs(value):
        return pair_y(pair_z(value))

    def pair_x(value):
        return value + roll(value, -1, 0)

    lower_y, lower_z = lanes_of(here) % 128 < 64, z_at % 2 == 0
    inner = jnp.where(lower_y, ty, 0.0)
    sum_x = pairs(tx)
    ty1 = pair_x(pairs(ty - inner))
    tz1 = pair_x(pairs(jnp.where(lower_z, 0.0, tz)))
    tx1 = roll(sum_x, -1, 0)
    diagonal1 = pair_x(pairs(diagonal - 2.0 * (inner + jnp.where(lower_z, tz, 0.0))))
    diagonal1 = diagonal1 - 2.0 * sum_x
    for at, value in enumerate((diagonal1, tx1, ty1, tz1, relax_weight(diagonal1))):
        middle_out[at] = value
    fine_copy = pltpu.make_async_copy(fine_out, fine_far, fine_done)
    middle_copy = pltpu.make_async_copy(middle_out, middle_far, middle_done)
    fine_copy.start()
    middle_copy.start()

    def own(value):
        return value[0:8, OWN : OWN + 512]

    def quads(value):
        value = quad_y(quad_z(value))
        return value[4:5] + value[6:7]

    y_faces1 = pair_x(pairs(own(y_faces - 2.0 * inner)))
    tx1, ty1, tz1, diagonal1 = own(tx1), own(ty1), own(tz1), own(diagonal1)
    lane = lanes_of(tx1)
    lower_y = (lax.broadcasted_iota(jnp.int32, tx1.shape, 1) // 128) % 2 == 0
    lower_z = lane % 4 < 2
    inner = jnp.where(lower_y, ty1, 0.0)
    across = quad_y(quad_z(tx1))
    tx2 = across[6:7]
    ty2 = quads(ty1 - inner)
    tz2 = quads(jnp.where(lower_z, 0.0, tz1))
    diagonal2 = quads(diagonal1 - 2.0 * (inner + jnp.where(lower_z, tz1, 0.0)))
    diagonal2 = diagonal2 - 2.0 * across[4:5]
    y_faces2 = quads(y_faces1 - 2.0 * inner)
    line2 = y_faces2 + shift * (diagonal2 - y_faces2)
    coarse = []
    for value in (tx2, ty2, tz2, diagonal2, line2):
        first, second = value[:, 0:128], value[:, 256:384]
        coarse.append(jnp.where(lanes_of(first) < 64, first, second))

    gram = jnp.zeros((80, 128), jnp.float32)
    for at in range(4):
        plane = 4 + at
        row = slice(plane, plane + 1)
        wide = basis[at, 0:8, :]
        after = right[...] if at == 3 else basis[at + 1, 0:8, :]
        before = left[...] if at == 0 else basis[at - 1, 0:8, :]
        dg, sx, sy, sz = (fine_out[kind, row, :] for kind in range(4))
        image = dg * wide - sy * roll(wide, -64) - roll(sy * wide, 64)
        image = image - sz * roll(wide, -1) - roll(sz * wide, 1)
        image = image - sx * after - fine_out[1, plane - 1 : plane, :] * before
        image_out[at] = image[0:4]
        image = image[:, OWN : OWN + 512]
        wide = basis[at, 8:ROWS, OWN:1024]
        after = locked_right[...] if at == 3 else basis[at + 1, 8:ROWS, OWN : OWN + 512]
        dg, sx, sy, sz = (fine_out[kind, row, OWN:1024] for kind in range(4))
        half = (0.5 * dg) * wide - sy * roll(wide, -64) - sz * roll(wide, -1)
        half = half[:, 0:512] - sx[:, 0:512] * after
        vmat[0:72, :] = basis[at, :, OWN : OWN + 512]
        vmat[68:128, :] = half[0:60]
        umat[0:72, :] = basis[at, :, OWN : OWN + 512]
        umat[72:80, :] = image
        gram = gram + dot_nt(umat[...], vmat[...])
    now = packed_rows(jnp.concatenate([gram[0:4], gram[72:76]], axis=0), [coarse[0], coarse[2]])
    rest = jnp.concatenate([coarse[1], coarse[4], coarse[3]], axis=0)
    for target in range(send_out.shape[0]):
        send_out[target, 0:8, :] = now
        send_out[target, 8:13, :] = gram[5 * target : 5 * target + 5]
        send_out[target, 13:16, :] = rest
    fine_copy.wait()
    middle_copy.wait()


def packed_rows(rows, extra):
    lane = lanes_of(rows)
    row = lax.broadcasted_iota(jnp.int32, rows.shape, 0)
    for at, value in enumerate(extra):
        for part in range(4):
            moved = roll(value, 96 - 32 * part)
            rows = jnp.where((row == 4 * at + part) & (lane >= 96), moved, rows)
    return rows


def unpacked_row(rows, at):
    lane = lanes_of(rows[0:1])
    value = roll(rows[4 * at : 4 * at + 1], -96)
    for part in range(1, 4):
        moved = roll(rows[4 * at + part : 4 * at + part + 1], 32 * part - 96)
        value = jnp.where(lane // 32 == part, moved, value)
    return value


def half_of(value, half, wanted):
    return value if half == wanted else roll(value, 64)


def spot_of(value, place):
    lane = lanes_of(value)
    return (lane // 64 == place // 4) & (lane % 4 == place % 4)


def middle_kernel(lines, got, send_out):
    at_y = lax.axis_index("gy")
    total = got[0]
    for source in range(1, got.shape[0]):
        total = total + got[source]
    packed = jnp.zeros((4, 128), jnp.float32)
    for place in range(8):
        source = at_y + (place - 3) // 2
        valid = (source >= 0) & (source < lines // 2)
        value = got[jnp.clip(source, 0, lines // 2 - 1)]
        tx, tz = unpacked_row(value, 0), unpacked_row(value, 1)
        value = jnp.concatenate([tx, value[13:14], tz, value[15:16]], axis=0)
        value = half_of(value, (place - 3) % 2, place // 4)
        packed = packed + jnp.where(spot_of(value, place) & valid, value, 0.0)
    now = packed_rows(total[0:8], [packed[0:1]])
    for target in range(send_out.shape[0]):
        send_out[target, 0:8, :] = now
        send_out[target, 8:13, :] = total[8:13]
        send_out[target, 13:16, :] = packed[1:4]


def residual_kernel(cells, got, used, image, basis, res_out, sums_out):
    total = got[0]
    for source in range(1, got.shape[0]):
        total = total + got[source]
    sums_out[...] = total[8:16]
    overlap, energy = total[0:4], total[4:8]
    lane = lanes_of(overlap)
    own = lane == lax.broadcasted_iota(jnp.int32, overlap.shape, 0)
    norm = jnp.sum(jnp.where(own, overlap, 0.0), axis=1, keepdims=True)
    top = jnp.sum(jnp.where(own, energy, 0.0), axis=1, keepdims=True)
    quotient = top / cells / (norm / cells + EPSILON)
    coupling = (energy - quotient * overlap) / cells
    weights = jnp.where(used[0:4, :] > 0, coupling, 0.0)
    weights = jnp.concatenate([weights, jnp.zeros((4, 128), jnp.float32)], axis=0)
    for at in range(4):
        field = basis[at]
        value = image[at] - quotient * field[0:4]
        res_out[at] = value - dot_nn(weights[:, 0:ROWS], field)[0:4]


def padded(value):
    return jnp.concatenate([value, jnp.zeros(value.shape, jnp.float32)], axis=0)


def apply_at(values, coefs, row, row_step, at, y_step, z_step, lanes):
    here = values[at]
    dg, sx, sy, sz = (coefs[kind, row : row + 1, lanes] for kind in range(4))
    before = coefs[1, row - row_step : row - row_step + 1, lanes]
    image = dg * here - sx * values[at + 1] - before * values[at - 1]
    image = image - sy * roll(here, -y_step) - roll(sy * here, y_step)
    return image - sz * roll(here, -z_step) - roll(sz * here, z_step)


def fine_image(values, fine, plane, lanes=slice(0, WIDE)):
    return apply_at(values, fine, plane, 1, plane, 64, 1, lanes)


def middle_image(values, middle, plane):
    return apply_at(values, middle, 2 * plane, 2, plane, 128, 2, slice(0, WIDE))


def planes_of(left, mid, right, first, last):
    parts = [left[at] for at in range(3)] + [mid[at] for at in range(4)]
    parts += [right[at] for at in range(3)]
    return {at: padded(parts[at - 1]) for at in range(first, last)}


def down_kernel(left, mid, right, fine, middle, r1_out, send_out, strip_out):
    source = planes_of(left, mid, right, 1, 11)
    error = {at: fine[4, at : at + 1, :] * source[at] for at in range(1, 11)}
    rest = {at: source[at] - fine_image(error, fine, at) for at in range(2, 10)}
    source1, error1 = {}, {}
    for plane in range(1, 5):
        value = pair_y(pair_z(rest[2 * plane] + rest[2 * plane + 1]))
        source1[plane] = value
        r1_out[plane - 1] = value[0:4]
        error1[plane] = middle[4, 2 * plane : 2 * plane + 1, :] * value
    low = sum(source1[plane] - middle_image(error1, middle, plane) for plane in (2, 3))
    low = quad_y(quad_z(low[:, OWN : OWN + 512]))
    both = jnp.concatenate([low[0:4, 0:128], low[0:4, 256:384]], axis=0)
    for target in range(send_out.shape[0]):
        send_out[target] = both
    for at in range(2):
        tiles = [error1[2 + at][0:4, 128 * t : 128 * t + 128] for t in range(1, 9)]
        lane = lanes_of(tiles[0])
        half, odd = lane // 64, lane % 2
        for group in range(2):
            a, b, c, d = tiles[4 * group : 4 * group + 4]
            value = jnp.where(half == 0, jnp.where(odd == 0, a, b), jnp.where(odd == 0, c, d))
            strip_out[at, 4 * group : 4 * group + 4, :] = value


def line_kernel(lines, got, coefs, strips, send_out, solved):
    at_x, at_y = lax.axis_index("gx"), lax.axis_index("gy")
    factors, previous, previous_factor, previous_link = [], None, None, None
    for source in range(lines // 2):
        rows = coefs[source, 13:15, :]
        turned = roll(rows, 64)
        first = lanes_of(rows) < 64
        for part in range(2):
            line = 2 * source + part
            value = jnp.where(first, rows, turned) if part == 0 else jnp.where(first, turned, rows)
            link, main = value[0:1], value[1:2]
            right = got[source, 4 * part : 4 * part + 4, :]
            solved[line, 4:8, :] = right
            if line == 0:
                scale = pl.reciprocal(main)
                update = scale * right
            else:
                scale = pl.reciprocal(main - previous_link * previous_factor)
                update = scale * (right + previous_link * previous)
            previous, previous_factor, previous_link = update, link * scale, link
            solved[line, 0:4, :] = update
            factors.append(previous_factor)
    for line in range(lines - 2, -1, -1):
        previous = solved[line, 0:4, :] + factors[line] * previous
        solved[line, 0:4, :] = previous
    packed = jnp.zeros((8, 128), jnp.float32)
    for place in range(8):
        line = 2 * at_y - 3 + place
        valid = (line >= 0) & (line < lines)
        value = solved[jnp.clip(line, 0, lines - 1)]
        packed = packed + jnp.where(spot_of(value, place) & valid, value, 0.0)
    for target in range(send_out.shape[0]):
        send_out[target, 0:8, :] = packed
        send_out[target, 8:16, :] = strips[(at_x >= target).astype(jnp.int32)]


def up_kernel(
    got, coefs, r1, left, mid, right, sums, fine_far, middle_far, basis_far,
    pre_out, send_out, fine, middle, vmat, fine_done, middle_done, basis_done,
):
    middle_copy = pltpu.make_async_copy(middle_far, middle, middle_done)
    fine_copy = pltpu.make_async_copy(fine_far, fine, fine_done)
    own = basis_far.at[:, :, OWN : OWN + 512]
    basis_copy = pltpu.make_async_copy(own, vmat, basis_done)
    middle_copy.start()
    fine_copy.start()
    basis_copy.start()
    at_x = lax.axis_index("gx")
    count = got.shape[0]
    error, source, links = {}, {}, {}
    for step in range(-3, 4):
        index = at_x + step
        valid = ((index >= 0) & (index < count)).astype(jnp.float32)
        kept = jnp.clip(index, 0, count - 1)
        rows = got[kept, 0:8, :] * valid
        error[step] = padded(rows[0:4])
        source[step] = padded(rows[4:8])
        near = coefs[kept] * valid
        links[step] = jnp.concatenate([unpacked_row(near, 0), near[13:16]], axis=0)
    lane = lanes_of(error[0])
    spot = lane % 4
    for reach in range(SWEEPS - 2, -1, -1):
        updated = dict(error)
        for step in range(-1 - reach, 2 + reach):
            here = error[step]
            sx, sy, sz, dg = (links[step][kind : kind + 1] for kind in range(4))
            up = jnp.where(spot < 3, roll(here, -1), roll(here, -61))
            flux = sy * here
            down = jnp.where(spot > 0, roll(flux, 1), roll(flux, 61))
            value = dg * here - sx * error[step + 1] - links[step - 1][0:1] * error[step - 1]
            value = value - sy * up - down - sz * roll(here, -4) - roll(sz * here, 4)
            updated[step] = here + relax_weight(dg) * (source[step] - value)
        error = updated
    blank = jnp.zeros((8, 128), jnp.float32)
    coarse = {}
    for step in range(-1, 2):
        tiles = []
        for place in range(2, 6):
            value = jnp.where(spot_of(error[step], place), error[step], 0.0)
            value = quad_z(pair_z(value))
            value = value + roll(value, 64)
            tiles += [value, value]
        coarse[step] = jnp.concatenate([blank] + tiles + [blank], axis=1)

    def strip(step):
        index = at_x + step
        valid = ((index >= 0) & (index < count)).astype(jnp.float32)
        rows = got[jnp.clip(index, 0, count - 1), 8:16, :] * valid
        tiles = []
        for group in range(2):
            part = padded(rows[4 * group : 4 * group + 4])
            for place in range(4):
                at = (lane // 64 == place // 2) & (lane % 2 == place % 2)
                value = pair_z(jnp.where(at, part, 0.0))
                tiles.append(value + roll(value, 64))
        return jnp.concatenate([blank] + tiles + [blank], axis=1)

    middle_copy.wait()
    error1, source1 = {0: strip(-1) + coarse[-1], 5: strip(1) + coarse[1]}, {}
    for plane in range(1, 5):
        source1[plane] = padded(r1[plane - 1])
        weight = middle[4, 2 * plane : 2 * plane + 1, :]
        error1[plane] = weight * source1[plane] + coarse[plane // 2 - 1]
    final1 = {}
    for plane in range(1, 5):
        weight = middle[4, 2 * plane : 2 * plane + 1, :]
        final1[plane] = error1[plane] + weight * (
            source1[plane] - middle_image(error1, middle, plane)
        )
    fine_copy.wait()
    lanes = slice(256, 1024)
    source0 = planes_of(left, mid, right, 2, 10)
    source0 = {at: value[:, lanes] for at, value in source0.items()}
    error0 = {
        at: fine[4, at : at + 1, lanes] * source0[at] + final1[at // 2][:, lanes]
        for at in range(2, 10)
    }
    final0 = {}
    for at in range(3, 9):
        weight = fine[4, at : at + 1, lanes]
        final0[at] = error0[at] + weight * (source0[at] - fine_image(error0, fine, at, lanes))
    basis_copy.wait()
    both = jnp.zeros((8, ROWS), jnp.float32)
    for at in range(4):
        own = slice(128, 640)
        value = final0[4 + at][0:4, own]
        pre_out[at] = value
        vmat[at, BASIS:ROWS, :] = value
        value = jnp.concatenate([value, fine_image(final0, fine, 4 + at, lanes)[0:4, own]], axis=0)
        both = both + dot_nt(value, vmat[at])
    now = jnp.concatenate([both, jnp.zeros((8, 128 - ROWS), jnp.float32)], axis=1)
    for target in range(send_out.shape[0]):
        send_out[target, 0:8, :] = now
        send_out[target, 8:16, :] = sums[...]


def eliminate(matrix, steps):
    row = lax.broadcasted_iota(jnp.int32, matrix.shape, 0)
    for start in range(0, steps, 4):
        columns = [
            jnp.broadcast_to(matrix[:, at : at + 1], matrix.shape) for at in range(start, start + 4)
        ]
        for part in range(4):
            step = start + part
            column = columns[part]
            factor = jnp.where(row > step, column * pl.reciprocal(column[step : step + 1, :]), 0.0)
            matrix = matrix - factor * matrix[step : step + 1, :]
            for other in range(part + 1, 4):
                value = columns[other]
                columns[other] = value - factor * value[step : step + 1, :]
    diagonal = jnp.where(lanes_of(matrix) == row, matrix, 0.0)
    diagonal = jnp.sum(diagonal, axis=1, keepdims=True)
    scale = lax.rsqrt(jnp.where(row[:, 0:1] < steps, diagonal, 1.0))
    return matrix * scale


def small_product(left, right, count):
    terms = [left[:, at : at + 1] * right[at : at + 1, :] for at in range(count)]
    while len(terms) > 1:
        terms = [sum(terms[at : at + 2]) for at in range(0, len(terms), 2)]
    return terms[0]


def ritz_kernel(
    cells, got, gathered, used, pre, basis_far, modes_out, dirs_out, ritz_out, corr_out,
    gram, field, basis_done,
):
    own = basis_far.at[:, :, OWN : OWN + 512]
    basis_copy = pltpu.make_async_copy(own, field, basis_done)
    basis_copy.start()
    total = got[0]
    for source in range(1, got.shape[0]):
        total = total + got[source]
    total = total / cells
    gram[80:128, :] = jnp.zeros((48, 128), jnp.float32)
    for source in range(16):
        gram[5 * source : 5 * source + 5, :] = gathered[source, 0:5, :]
    gram = gram[...] / cells
    shape = (16, 128)
    row = lax.broadcasted_iota(jnp.int32, shape, 0)
    lane = lax.broadcasted_iota(jnp.int32, shape, 1)
    zero4 = jnp.zeros((4, 128), jnp.float32)
    corr = jnp.where(used[0:4, :] > 0, total[0:4], 0.0)
    corr_out[...] = roll(corr, -8)[:, 0:LOCKED]
    locked_part = jnp.concatenate([zero4, -corr, zero4, zero4], axis=0)
    ones = ((row < 4) & (lane == row)) | ((row >= 8) & (row < 12) & (lane == row - 4))
    pre_ones = (row >= 4) & (row < 8) & (lane == row + 64)
    on_basis = jnp.where(ones, 1.0, locked_part)
    weights = jnp.where(pre_ones, 1.0, on_basis)
    pre_lane = (lane >= 68) & (lane < 72)

    def from_pre(part):
        rows4 = jnp.concatenate([zero4, part, zero4, zero4], axis=0)
        rows4 = jnp.where(lane < 72, rows4, 0.0)
        return jnp.where(pre_lane, 0.5 * rows4, rows4)

    products = dot_nn(jnp.concatenate([on_basis, locked_part], axis=0), gram)
    first = jnp.where(lane < 68, products[0:16], 0.0)
    second = roll(jnp.where(lane >= 68, products[16:32], 0.0), -60)
    pair = gram[72:80]
    pair = jnp.concatenate([pair[0:4], zero4, pair[4:8], zero4], axis=0)
    pair = jnp.where(lane < 68, jnp.where(lane < 8, 0.5 * pair, pair), 0.0)
    stacked = [0.5 * first + from_pre(total[0:4]), second + pair + from_pre(total[4:8])]
    stacked = jnp.concatenate(stacked, axis=0)
    straight = dot_nt(stacked, weights)
    turned = dot_nt(weights, stacked)
    mass = straight[0:16] + turned[:, 0:16]
    stiff = straight[16:32] + turned[:, 16:32]
    eye = jnp.where((row < 12) & (lane == row + 64), 1.0, 0.0)
    wide = jnp.zeros((16, 112), jnp.float32)
    mass = jnp.concatenate([mass, wide], axis=1)
    stiff = jnp.concatenate([stiff, wide], axis=1)
    done = eliminate(mass + roll(stiff, 32) + eye, 12)
    inside = (row < 12) & (lane < 12)
    half = jnp.where(inside, roll(done, -32), 0.0)
    inverse = jnp.where(inside, roll(done, -64), 0.0)
    reduced = dot_nt(half, inverse) + dot_nt(inverse, half)
    reduced = 0.5 * jnp.concatenate([reduced, wide], axis=1)
    top = jnp.sum(jnp.where(lane == row, reduced, 0.0), axis=(0, 1), keepdims=True)
    row8 = lax.broadcasted_iota(jnp.int32, (8, 128), 0)
    lane8 = lax.broadcasted_iota(jnp.int32, (8, 128), 1)
    first4 = row8 < 4
    basis_q = jnp.where(first4 & (lane8 == row8), 1.0, 0.0)
    for step in range(RITZ):
        raised = top * basis_q - small_product(basis_q, reduced, 12)
        joint = roll(raised, 32)
        for part in range(ACTIVE):
            column = jnp.sum(raised * raised[part : part + 1, :], axis=1, keepdims=True)
            joint = joint + jnp.where(lane8 == part, column, 0.0)
        basis_q = jnp.where(first4 & (lane8 < 12), roll(eliminate(joint, 4), -32), 0.0)
    ritz = jnp.sum(basis_q * small_product(basis_q, reduced, 12), axis=1, keepdims=True)
    for part in range(ACTIVE):
        ritz_out[part] = ritz[part, 0]
    coefs = small_product(basis_q, inverse, 12)
    tail = jnp.where(lane8 >= 4, coefs, 0.0)
    both = jnp.concatenate([coefs[0:4], tail[0:4]], axis=0)
    mix = small_product(both, weights, 12)[:, 0:ROWS]
    basis_copy.wait()
    for at in range(4):
        field[at, BASIS:ROWS, :] = pre[at]
        value = dot_nn(mix, field[at])
        for part in range(4):
            modes_out[part, at : at + 1, :] = value[part : part + 1]
            dirs_out[part, at : at + 1, :] = value[4 + part : 5 + part]


def pair_shift(low, high, axis):
    count = lax.axis_size(axis)
    forward = [(at, at + 1) for at in range(count - 1)]
    backward = [(at + 1, at) for at in range(count - 1)]
    above = lax.ppermute(low, axis, backward)
    return lax.ppermute(high, axis, forward), above


def spread(block, axis):
    count = lax.axis_size(axis)
    return lax.all_to_all(jnp.broadcast_to(block, (count,) + block.shape), axis, 0, 0)


def on_device(modes, directions, locked, perm_class, perm_table, locked_count):
    size_x, size_y = lax.axis_size("gx"), lax.axis_size("gy")
    lines = 2 * size_y
    cells = float(4 * 512 * size_x * size_y)
    basis, low, high = kernel_call(
        input_kernel, [(4, ROWS, 512), (4, ROWS, 384), (4, ROWS, 384)],
        perm_table, modes, directions, locked, perm_class, scalars=1, inputs=True,
    )
    low, high = pair_shift(low, high, "gy")
    basis = jnp.concatenate([low, basis, high], axis=2)
    conduct = basis[:, BASIS].reshape(10, 512)
    left, right = pair_shift(
        jnp.concatenate(
            [basis[0, 8:, OWN : OWN + 512], basis[0, :8].reshape(20, 512), conduct], 0
        ),
        jnp.concatenate([basis[3, :8].reshape(20, 512), conduct], 0),
        "gx",
    )
    fine, middle, image, used, send = kernel_call(
        functools.partial(coef_kernel, 4.0 / float(lines * lines)),
        [(5, 16, WIDE), (5, 16, WIDE), (4, 4, WIDE), (8, 128), (size_y, 16, 128)],
        locked_count, left[20:30].reshape(4, WIDE), right[84:94].reshape(4, WIDE), basis,
        left[:20].reshape(8, WIDE), right[64:84].reshape(8, WIDE), right[:64],
        scratch=[(16, WIDE), (128, 512), (80, 512), (5, 16, WIDE), (5, 16, WIDE)],
        scalars=1, far_out=(0, 1),
    )
    got_y = lax.all_to_all(send, "gy", 0, 0)
    (send,) = kernel_call(
        functools.partial(middle_kernel, lines), [(size_x, 16, 128)], got_y
    )
    got_x = lax.all_to_all(send, "gx", 0, 0)
    mid, sums = kernel_call(
        functools.partial(residual_kernel, cells), [(4, 4, WIDE), (8, 128)],
        got_x, used, image, basis,
    )
    left, right = pair_shift(mid[:3], mid[1:], "gx")
    r1, send, strips = kernel_call(
        down_kernel, [(4, 4, WIDE), (size_y, 8, 128), (2, 8, 128)], left, mid, right, fine, middle
    )
    (send,) = kernel_call(
        functools.partial(line_kernel, lines), [(size_x, 16, 128)],
        lax.all_to_all(send, "gy", 0, 0), got_y, strips,
        scratch=[(lines, 8, 128)],
    )
    precond, send = kernel_call(
        up_kernel, [(4, 4, 512), (size_y, 16, 128)],
        lax.all_to_all(send, "gx", 0, 0), got_x, r1, left, mid, right, sums, fine, middle, basis,
        scratch=[(5, 16, WIDE), (5, 16, WIDE), (4, ROWS, 512)], far=(7, 8, 9),
    )
    got_y = lax.all_to_all(send, "gy", 0, 0)
    got_x = spread(jnp.sum(got_y[:, :8], axis=0), "gx")
    new_modes, new_directions, ritz, corr = kernel_call(
        functools.partial(ritz_kernel, cells),
        [(4, 4, 512), (4, 4, 512), (4,), (4, LOCKED)],
        got_x, got_y[:, 8:], used, precond, basis,
        scratch=[(128, 128), (4, ROWS, 512)], far=(4,), results=True,
    )
    return (new_modes, new_directions, ritz, corr.T)


def solution(mesh):
    placed = (
        P(None, "gx", "gy"),
        P(None, "gx", "gy"),
        P(None, "gx", "gy"),
        P("gx", "gy"),
        P(),
        P(),
    )
    return jax.shard_map(
        on_device,
        mesh=mesh,
        in_specs=placed,
        out_specs=(P(None, "gx", "gy"), P(None, "gx", "gy"), P(), P()),
        check_vma=False,
    )
```
